512 devices in a mesh: lon: 32 (over x_lo, z), lat: 16 (over x_hi, y, core).
Axes of the slice: x: 4 (x_hi: 2, x_lo: 2; x = x_hi * 2 + x_lo), y: 4, z: 16, core: 2. Of those that a mesh axis runs over, the one named last changes fastest.
Arguments:
- fields: float32 [6, 4, 2048, 4096], P(None, None, 'lat', 'lon'), may hold values from -6 to 6
- face_weights: float32 [2, 2048, 4096], P(None, 'lat', 'lon'), may hold values from 0.5 to 1.5
- inv_area: float32 [2048, 4096], P('lat', 'lon'), may hold values from 0.5 to 1.5
- cell_mask: int32 [2048, 4096], P('lat', 'lon'), may hold values 0 or 1
- land_blocks: int32 [16, 32], P('lat', 'lon'), may hold values 0 or 1
Outputs:
- new_fields: float32 [6, 4, 2048, 4096], P(None, None, 'lat', 'lon')
The draws below stay inside these ranges and needn't reach their ends.
All inputs are finite; a program needn't handle non-finite values. No bound on the sum of `cell_mask` or of `land_blocks` on one device may be relied on, other than what follows from the above.
Results may differ from the reference program's by a relative error of at most 0.00002.
Values sent between devices are 32-bit elements; how exact they have to be, the bound alone decides.
No kernel may reach another device: no remote copies, remote signals or barrier semaphores. Data moves between devices by JAX's collectives and lax.ppermute only.
A program may use at most 64 MiB of HBM per device.

```python
import jax
import jax.numpy as jnp

CI = 128
CJ = 128
NF = 6
NK = 4
SUBSTEPS = 2
NI = 4096
NJ = 2048
BLOCKS_LAT = 16
BLOCKS_LON = 32


def touch_ends(entries, key, smallest, high):
    extent = entries.shape
    spot = [jax.random.randint(jax.random.fold_in(key, axis), (), 0, extent[axis]) for axis in range(len(extent))]
    entries = entries.at[tuple(spot)].set(smallest)
    longest = extent.index(max(extent))
    spot[longest] = (spot[longest] + 1) % extent[longest]
    return entries.at[tuple(spot)].set(high)


def block_levels(stream_key, dims, pieces, least, largest):
    level = 1.0
    for dim, shards_of in pieces:
        heights = jax.random.uniform(jax.random.fold_in(jax.random.fold_in(stream_key, 6), dim), (shards_of,), jnp.float32, least / len(pieces), largest / len(pieces))
        level = level * jnp.repeat(jnp.exp(heights), dims[dim] // shards_of).reshape((-1,) + (1,) * (len(dims) - 1 - dim))
    return level


def gaussian(own_key, dims, width, most, split=(), dtype=jnp.bfloat16):
    drawn = width * jax.random.normal(own_key, dims, jnp.float32)
    if split:
        drawn = drawn * block_levels(own_key, dims, split, -0.22, 0.18)
    return jnp.clip(drawn, -most, most).astype(dtype)


def setup_inputs(seed: int = 0) -> dict:
    arg_keys = jax.random.split(jax.random.key(seed), 6)
    return {
        "fields": gaussian(arg_keys[0], (NF, NK, NJ, NI), 1.0, 6.0, ((2, 16), (3, 32)), jnp.float32),
        "face_weights": jnp.clip(0.5 + 1.0 * jax.random.uniform(arg_keys[1], (2, NJ, NI), jnp.float32) ** block_levels(arg_keys[1], (2, NJ, NI), ((1, 16), (2, 32)), -0.2, 0.2), 0.5, 1.5),
        "inv_area": jnp.clip(0.5 + 1.0 * jax.random.uniform(arg_keys[2], (NJ, NI), jnp.float32) ** block_levels(arg_keys[2], (NJ, NI), ((0, 16), (1, 32)), -0.2, 0.2), 0.5, 1.5),
        "cell_mask": touch_ends((jax.random.randint(arg_keys[3], (NJ, NI), 0, 5) < 4).astype(jnp.int32), jax.random.fold_in(arg_keys[3], 1), 0, 1),
        "land_blocks": touch_ends((jax.random.randint(arg_keys[4], (BLOCKS_LAT, BLOCKS_LON), 0, 4) < 1).astype(jnp.int32), jax.random.fold_in(arg_keys[4], 1), 0, 1),
    }


TIME_STEP = 0.1
ADVECTION = 0.5


def face_flux(near_side, far_side, face_speed, face_weight):
    return face_weight * (ADVECTION * face_speed * (near_side + far_side) * 0.5 - (far_side - near_side))


def tendency(lon_fields, lat_fields, east_ext, north_ext, inv_area):
    u_speed = lon_fields[4]
    east_speed = 0.5 * (u_speed[..., :-1] + u_speed[..., 1:])
    flux_east = face_flux(lon_fields[..., :-1], lon_fields[..., 1:], east_speed, east_ext)
    v_speed = lat_fields[5]
    north_speed = 0.5 * (v_speed[:, :-1, :] + v_speed[:, 1:, :])
    flux_north = face_flux(lat_fields[:, :, :-1, :], lat_fields[:, :, 1:, :], north_speed, north_ext)
    return inv_area * ((flux_east[..., :-1] - flux_east[..., 1:]) + (flux_north[:, :, :-1, :] - flux_north[:, :, 1:, :]))


def reference(fields, face_weights, inv_area, cell_mask, land_blocks):
    land_cells = jnp.repeat(jnp.repeat(land_blocks, CJ, axis=0), CI, axis=1)
    ocean_mask = cell_mask.astype(jnp.float32) * (1 - land_cells).astype(jnp.float32)
    flip_sign = jnp.where(jnp.arange(NF) >= 4, -1.0, 1.0).astype(jnp.float32)[:, None, None]
    east_weight = face_weights[0]
    north_weight = face_weights[1]
    east_ext = jnp.concatenate([east_weight[:, -1:], east_weight], axis=1)
    north_ext = jnp.concatenate([jnp.zeros_like(north_weight[:1]), north_weight], axis=0)
    current = fields
    for substep in range(SUBSTEPS):
        lon_fields = jnp.concatenate([current[..., -1:], current, current[..., :1]], axis=-1)
        fold_row = current[:, :, -1, ::-1] * flip_sign
        south_zero = jnp.zeros_like(current[:, :, :1, :])
        lat_fields = jnp.concatenate([south_zero, current, fold_row[:, :, None, :]], axis=2)
        change = tendency(lon_fields, lat_fields, east_ext, north_ext, inv_area)
        current = current + TIME_STEP * ocean_mask * change
    return current
```

```python
import functools

import jax
import jax.numpy as jnp
from jax import lax
from jax.experimental import pallas as pl
from jax.experimental.pallas import tpu as pltpu
from jax.sharding import PartitionSpec as P

F32 = jnp.float32
TIME_STEP = 0.1
NP = 24
GE, GN, GM, GS = 24, 25, 26, 27
ROWS2, ROWS4 = 56, 112
PAD = 8
CHUNK = 32
HIGH = lax.Precision.HIGHEST


def lon_pairs(nlon, nlat, odd):
    def other(i):
        if not odd:
            return i ^ 1
        return (i + 1) % nlon if i % 2 else (i - 1) % nlon

    return [(i * nlat + l, other(i) * nlat + l) for i in range(nlon) for l in range(nlat)]


def lat_pairs(nlon, nlat, odd):
    pairs = []
    for i in range(nlon):
        for l in range(nlat):
            if not odd:
                pairs.append((i * nlat + l, i * nlat + (l ^ 1)))
            elif l == nlat - 1:
                pairs.append((i * nlat + l, (nlon - 1 - i) * nlat + l))
            elif l > 0:
                pairs.append((i * nlat + l, i * nlat + (l + 1 if l % 2 else l - 1)))
    return pairs


def lanes(shape):
    return lax.broadcasted_iota(jnp.int32, shape, 1)


def rows_of(shape):
    return lax.broadcasted_iota(jnp.int32, shape, 0)


def roll(x, shift, axis):
    n = x.shape[axis]
    shift %= n
    return x if shift == 0 else pltpu.roll(x, shift, axis)


def step_factor(area, mask, land):
    sea = mask.astype(F32) * (1 - land).astype(F32)
    return TIME_STEP * sea * area


def coefs(u, ue, uw, v, vn, vs, me, mw, mn, ms, base):
    te = me * (0.125 * (u + ue))
    tw = mw * (0.125 * (u + uw))
    tn = mn * (0.125 * (v + vn))
    ts = ms * (0.125 * (v + vs))
    return me - te, mw + tw, mn - tn, ms + ts, base + ((tw - te) + (ts - tn))


def apply(c, x, xe, xw, xn, xs):
    ce, cw, cn, cs, cc = c
    return cc * x + ((ce * xe + cw * xw) + (cn * xn + cs * xs))


def rows_kernel(f_lo, f_hi, w_lo, w_hi, a_lo, a_hi, k_lo, k_hi, land, to_odd, to_even):
    odd = lax.axis_index("lat") % 2 == 1
    m_lo = step_factor(a_lo[0:2], k_lo[0:2], land[0, 0])
    m_hi = step_factor(a_hi[6:8], k_hi[6:8], land[0, 0])
    zero = jnp.zeros((2, 128), F32)
    for g in range(28):
        if g < NP:
            south, north = f_lo[g, 0:2], f_hi[g, 6:8]
        elif g < GM:
            south, north = w_lo[g - NP, 0:2], w_hi[g - NP, 6:8]
        elif g == GM:
            south, north = m_lo, m_hi
        else:
            south, north = zero, zero
        to_odd[2 * g : 2 * g + 2] = jnp.where(odd, north, south)
        to_even[2 * g : 2 * g + 2] = jnp.where(odd, south, north)


def columns_kernel(f, w, area, mask, land, out):
    for r in range(0, 128, CHUNK):
        rr = slice(r, r + CHUNK)
        group = lanes((CHUNK, 128)) // 4
        acc = jnp.zeros((CHUNK, 128), F32)
        for g in range(GM + 1):
            if g < NP:
                x = f[g, rr]
            elif g < GM:
                x = w[g - NP, rr]
            else:
                x = step_factor(area[rr], mask[rr], land[0, 0])
            acc = jnp.where(group == g, roll(x, 4 * g + 2, 1), acc)
        out[rr] = acc


def strips_kernel(to_odd, to_even, got_odd, got_even, pack, out, north, south, recv):
    odd = lax.axis_index("lat") % 2 == 1
    top = lax.axis_index("lat") == lax.axis_size("lat") - 1
    raw = jnp.where(odd, got_odd[...], got_even[...])
    row = rows_of((ROWS2, 128))
    flip = (rows_of((128, 128)) + lanes((128, 128)) == 127).astype(F32)
    mirrored = jnp.dot(raw, flip, precision=HIGH, preferred_element_type=F32)
    mirrored = jnp.where((row >= 32) & (row < 48), -mirrored, mirrored)
    mirrored = jnp.where(row % 2 == 0, roll(mirrored, -1, 0), roll(mirrored, 1, 0))
    recv[0] = jnp.where(top, mirrored, raw)
    recv[1] = jnp.where(odd, got_even[...], got_odd[...])
    recv[2] = jnp.where(odd, to_odd[...], to_even[...])
    recv[3] = jnp.where(odd, to_even[...], to_odd[...])
    for g in range(28):
        two = slice(2 * g, 2 * g + 2)
        north[4 * g : 4 * g + 2] = recv[2, two]
        north[4 * g + 2 : 4 * g + 4] = recv[0, two]
        south[4 * g : 4 * g + 2] = recv[1, two]
        south[4 * g + 2 : 4 * g + 4] = recv[3, two]
    a, b = recv[0, 2 * GN : 2 * GN + 1], recv[0, 2 * GN + 1 : 2 * GN + 2]
    north[4 * GN + 2 : 4 * GN + 3] = jnp.where(top, b, a)
    north[4 * GS + 2 : 4 * GS + 3] = jnp.where(top, a, recv[2, 2 * GN + 1 : 2 * GN + 2])
    south[4 * GS + 1 : 4 * GS + 2] = recv[1, 2 * GN : 2 * GN + 1]
    lane = lanes((ROWS4, 128))
    acc = jnp.where(lane // 4 == 28, roll(north[...], 114, 1), pack[0:ROWS4])
    out[0:ROWS4] = jnp.where(lane // 4 == 29, roll(south[...], 118, 1), acc)
    out[ROWS4:128] = pack[ROWS4:128]


def repeat_group(x, g):
    y = roll(x, -4 * g, 1)
    y = jnp.where(lanes(y.shape) < 4, y, 0.0)
    for s in (4, 8, 16, 32, 64):
        y = y + roll(y, s, 1)
    return y


def repeat_field(x, f):
    y = jnp.where(lanes(x.shape) // 16 == f, x, 0.0)
    for s in (16, 32, 64):
        y = y + roll(y, s, 1)
    return y


def repeat_half(v, half):
    low = rows_of(v.shape) < 4
    other = roll(v, 4, 0)
    return jnp.where(low, v, other) if half == 0 else jnp.where(low, other, v)


def lat_strip(strip, from_west, from_east, shift_w, shift_e, top):
    lane = lanes((8, 128))
    def tile(t):
        x = strip[8 * t : 8 * t + 8]
        w = roll(from_west[8 * t : 8 * t + 8], shift_w, 1)
        e = roll(from_east[8 * t : 8 * t + 8], shift_e, 1)
        return x, jnp.where(lane == 127, e, roll(x, -1, 1)), jnp.where(lane == 0, w, roll(x, 1, 1))

    x12, e12, w12 = tile(12)
    x13, _, _ = tile(13)
    here, right, left = (repeat_half(a, 0) for a in (x12, e12, w12))
    we = here if top is None else jnp.where(top, right, here)
    ww = left if top is None else jnp.where(top, here, left)
    m = repeat_half(x13, 0)
    me, mw = m * we, m * ww
    mn, ms = m * repeat_half(x12, 1), m * repeat_half(x13, 1)
    base = 1.0 - ((me + mw) + (mn + ms))
    c = []
    for t in range(2):
        u, ue, uw = tile(8 + t)
        v = tile(10 + t)[0]
        c.append(coefs(u, ue, uw, v, roll(v, -1, 0), roll(v, 1, 0), me, mw, mn, ms, base))
    out = []
    for t in range(12):
        x, xe, xw = tile(t)
        out.append(apply(c[t % 2], x, xe, xw, roll(x, -1, 0), roll(x, 1, 0)))
    return out


def step_kernel(f_hbm, w, area, mask, land, pack, got_even, got_odd, north, south, out_hbm,
                buf, mid, res, side, side_v, side_w, edge, edge1, halo1, mw5, sem_in, sem_out):
    odd = lax.axis_index("lon") % 2 == 1
    top = lax.axis_index("lat") == lax.axis_size("lat") - 1
    copies = [
        pltpu.make_async_copy(f_hbm.at[:, k], buf.at[:, k, pl.ds(PAD, 128)], sem_in.at[k])
        for k in range(4)
    ]
    for c in copies:
        c.start()

    west = jnp.where(odd, got_even[...], got_odd[...])
    east = jnp.where(odd, got_odd[...], got_even[...])
    own = pack[...]
    lane = lanes((128, 128))
    j = lane % 4

    both = jnp.where(lane < 120, west, roll(east, 8, 1))
    turned = both.T
    nw, ne = roll(turned[113:114], -1, 1), turned[122:123]
    sw, se = turned[117:118], roll(turned[126:127], 1, 1)

    for s, (strip, above, below) in enumerate(
        (
            (jnp.where(j < 2, west, own), nw, sw),
            (jnp.where(j < 2, own, east), ne, se),
        )
    ):
        side[s, PAD : PAD + 128] = strip
        side[s, PAD - 1 : PAD] = below
        side[s, PAD + 128 : PAD + 129] = above
        for r in range(0, 128 + 2 * PAD, 16):
            x = side[s, r : r + 16]
            side_v[s, r : r + 16] = repeat_field(x, 5)
            side_w[s, r : r + 16] = repeat_group(x, GN)
    edge[...] = jnp.where(j == 1, side[0, PAD : PAD + 128], roll(side[1, PAD : PAD + 128], -2, 1))
    for r in range(0, 128, CHUNK):
        new = []
        for s in range(2):
            at = lambda ref, d: ref[s, PAD + r + d : PAD + r + d + CHUNK]
            x = at(side, 0)
            we, m, u = repeat_group(x, GE), repeat_group(x, GM), repeat_field(x, 4)
            me, mw = m * we, m * roll(we, 1, 1)
            mn, ms = m * at(side_w, 0), m * at(side_w, -1)
            base = 1.0 - ((me + mw) + (mn + ms))
            c = coefs(u, roll(u, -1, 1), roll(u, 1, 1), at(side_v, 0), at(side_v, 1), at(side_v, -1),
                      me, mw, mn, ms, base)
            new.append(apply(c, x, roll(x, -1, 1), roll(x, 1, 1), at(side, 1), at(side, -1)))
        jj = lanes((CHUNK, 128)) % 4
        edge1[r : r + CHUNK] = jnp.where(jj == 1, new[0], roll(new[1], -2, 1))

    for s, tiles in enumerate(
        (
            lat_strip(south, west, east, 11, 9, None),
            lat_strip(north, west, east, 15, 13, top),
        )
    ):
        for t in range(12):
            halo1[s, 8 * t : 8 * t + 8] = tiles[t]

    m = step_factor(area[...], mask[...], land[0, 0])
    we, wn = w[0], w[1]
    ww = jnp.where(lane == 0, roll(edge[...], -(4 * GE + 1), 1), roll(we, 1, 1))
    first = rows_of((128, 128)) == 0
    ws = jnp.where(first, south[4 * GN + 1 : 4 * GN + 2], roll(wn, 1, 0))
    me, mw, mn, ms = m * we, m * ww, m * wn, m * ws
    for n, x in enumerate((me, mw, mn, ms, 1.0 - ((me + mw) + (mn + ms)))):
        mw5[n] = x

    def substep(get, ring, put, k):
        lane = lanes((CHUNK, 128))
        for r in range(0, 128, CHUNK):
            rr = slice(r, r + CHUNK)

            def around(f):
                x = get(f, r)
                col = roll(ring[rr], -(4 * (4 * f + k) + 1), 1)
                xe = jnp.where(lane == 127, col, roll(x, -1, 1))
                xw = jnp.where(lane == 0, col, roll(x, 1, 1))
                return x, xe, xw, get(f, r + 1), get(f, r - 1)

            u, ue, uw, _, _ = around(4)
            v, vn, vs = get(5, r), get(5, r + 1), get(5, r - 1)
            c = coefs(u, ue, uw, v, vn, vs, mw5[0, rr], mw5[1, rr], mw5[2, rr], mw5[3, rr], mw5[4, rr])
            for f in range(6):
                put(f, r, apply(c, *around(f)))

    outs = []
    for k in range(4):
        for f in range(6):
            g = 4 * f + k
            mid[f, PAD - 1 : PAD] = halo1[0, 4 * g + 1 : 4 * g + 2]
            mid[f, PAD + 128 : PAD + 129] = halo1[1, 4 * g + 2 : 4 * g + 3]
        copies[k].wait()
        for f in range(6):
            g = 4 * f + k
            buf[f, k, PAD - 1 : PAD] = south[4 * g + 1 : 4 * g + 2]
            buf[f, k, PAD + 128 : PAD + 129] = north[4 * g + 2 : 4 * g + 3]

        def put_mid(f, r, x):
            mid[f, PAD + r : PAD + r + CHUNK] = x

        def put_res(f, r, x):
            res[f, k, r : r + CHUNK] = x

        substep(lambda f, r: buf[f, k, PAD + r : PAD + r + CHUNK], edge, put_mid, k)
        substep(lambda f, r: mid[f, PAD + r : PAD + r + CHUNK], edge1, put_res, k)
        c = pltpu.make_async_copy(res.at[:, k], out_hbm.at[:, k], sem_out.at[k])
        c.start()
        outs.append(c)
    for c in outs:
        c.wait()


def cost(nbytes, flops):
    return pl.CostEstimate(flops=flops, bytes_accessed=nbytes, transcendentals=0)


def vmem():
    return pl.BlockSpec(memory_space=pltpu.VMEM)


def smem():
    return pl.BlockSpec(memory_space=pltpu.SMEM)


def local(nlon, nlat, fields, weights, area, mask, land):
    shape = jax.ShapeDtypeStruct
    planes = fields.reshape(NP, 128, 128)
    params = pltpu.CompilerParams(vmem_limit_bytes=24 << 20)

    def lo3(n):
        return pl.BlockSpec((n, 8, 128), lambda i: (0, 0, 0))

    def hi3(n):
        return pl.BlockSpec((n, 8, 128), lambda i: (0, 15, 0))

    lo2 = pl.BlockSpec((8, 128), lambda i: (0, 0))
    hi2 = pl.BlockSpec((8, 128), lambda i: (15, 0))
    whole = pl.BlockSpec((ROWS2, 128), lambda i: (0, 0))
    rows = shape((ROWS2, 128), F32)
    to_odd, to_even = pl.pallas_call(
        rows_kernel,
        grid=(1,),
        out_shape=(rows, rows),
        in_specs=[lo3(NP), hi3(NP), lo3(2), hi3(2), lo2, hi2, lo2, hi2, smem()],
        out_specs=(whole, whole),
        compiler_params=params,
        cost_estimate=cost(1 << 18, 1 << 16),
        name="rows",
    )(planes, planes, weights, weights, area, area, mask, mask, land)

    axes = ("lon", "lat")
    with jax.named_scope("lat_odd"):
        got_odd = lax.ppermute(to_odd, axes, lat_pairs(nlon, nlat, True))
    with jax.named_scope("lat_even"):
        got_even = lax.ppermute(to_even, axes, lat_pairs(nlon, nlat, False))

    tile = shape((128, 128), F32)
    pack = pl.pallas_call(
        columns_kernel,
        out_shape=tile,
        in_specs=[vmem()] * 4 + [smem()],
        out_specs=vmem(),
        compiler_params=params,
        cost_estimate=cost(2 << 20, 1 << 20),
        name="columns",
    )(planes, weights, area, mask, land)

    pack, north, south = pl.pallas_call(
        strips_kernel,
        out_shape=(tile, shape((ROWS4, 128), F32), shape((ROWS4, 128), F32)),
        in_specs=[vmem()] * 5,
        out_specs=(vmem(),) * 3,
        scratch_shapes=[pltpu.VMEM((4, ROWS2, 128), F32)],
        compiler_params=params,
        cost_estimate=cost(1 << 18, 1 << 18),
        name="strips",
    )(to_odd, to_even, got_odd, got_even, pack)

    with jax.named_scope("lon_even"):
        col_even = lax.ppermute(pack, axes, lon_pairs(nlon, nlat, False))
    with jax.named_scope("lon_odd"):
        col_odd = lax.ppermute(pack, axes, lon_pairs(nlon, nlat, True))

    padded = 128 + 2 * PAD
    return pl.pallas_call(
        step_kernel,
        out_shape=shape((6, 4, 128, 128), F32),
        in_specs=[pl.BlockSpec(memory_space=pl.ANY)] + [vmem()] * 3 + [smem()] + [vmem()] * 5,
        out_specs=pl.BlockSpec(memory_space=pl.ANY),
        scratch_shapes=[
            pltpu.VMEM((6, 4, padded, 128), F32),
            pltpu.VMEM((6, padded, 128), F32),
            pltpu.VMEM((6, 4, 128, 128), F32),
            pltpu.VMEM((2, padded, 128), F32),
            pltpu.VMEM((2, padded, 128), F32),
            pltpu.VMEM((2, padded, 128), F32),
            pltpu.VMEM((128, 128), F32),
            pltpu.VMEM((128, 128), F32),
            pltpu.VMEM((2, 96, 128), F32),
            pltpu.VMEM((5, 128, 128), F32),
            pltpu.SemaphoreType.DMA((4,)),
            pltpu.SemaphoreType.DMA((4,)),
        ],
        compiler_params=params,
        cost_estimate=cost(4 << 20, 20 << 20),
        name="step",
    )(fields, weights, area, mask, land, pack, col_even, col_odd, north, south)


def solution(mesh):
    in_specs = (
        P(None, None, "lat", "lon"),
        P(None, "lat", "lon"),
        P("lat", "lon"),
        P("lat", "lon"),
        P("lat", "lon"),
    )
    body = functools.partial(local, mesh.shape["lon"], mesh.shape["lat"])
    return jax.shard_map(
        body, mesh=mesh, in_specs=in_specs, out_specs=P(None, None, "lat", "lon"), check_vma=False
    )
```

```python
import functools

import jax
import jax.numpy as jnp
import numpy as np
from jax import lax
from jax.experimental import pallas as pl
from jax.experimental.pallas import tpu as pltpu
from jax.sharding import PartitionSpec as P

F32 = jnp.float32
TIME_STEP = 0.1
NP = 24
GE, GN, GM, GS = 24, 25, 26, 27
ROWS2, ROWS4 = 56, 112
PAD = 8
CHUNK = 32
HIGH = lax.Precision.HIGHEST


def lon_pairs(nlon, nlat, odd):
    def other(i):
        if not odd:
            return i ^ 1
        return (i + 1) % nlon if i % 2 else (i - 1) % nlon

    return [(i * nlat + l, other(i) * nlat + l) for i in range(nlon) for l in range(nlat)]


def lat_pairs(nlon, nlat, odd):
    pairs = []
    for i in range(nlon):
        for l in range(nlat):
            if not odd:
                pairs.append((i * nlat + l, i * nlat + (l ^ 1)))
            elif l == nlat - 1:
                pairs.append((i * nlat + l, (nlon - 1 - i) * nlat + l))
            elif l > 0:
                pairs.append((i * nlat + l, i * nlat + (l + 1 if l % 2 else l - 1)))
    return pairs


def lanes(shape):
    return lax.broadcasted_iota(jnp.int32, shape, 1)


def rows_of(shape):
    return lax.broadcasted_iota(jnp.int32, shape, 0)


def roll(x, shift, axis):
    n = x.shape[axis]
    shift %= n
    return x if shift == 0 else pltpu.roll(x, shift, axis)


def step_factor(area, mask, land):
    sea = mask.astype(F32) * (1 - land).astype(F32)
    return TIME_STEP * sea * area


def coefs(se, sw, sn, ss, me, mw, mn, ms, base):
    te, tw, tn, ts = me * (0.125 * se), mw * (0.125 * sw), mn * (0.125 * sn), ms * (0.125 * ss)
    return me - te, mw + tw, mn - tn, ms + ts, base + ((tw - te) + (ts - tn))


def apply(c, x, xe, xw, xn, xs):
    ce, cw, cn, cs, cc = c
    return cc * x + ((ce * xe + cw * xw) + (cn * xn + cs * xs))


def rows_kernel(f, w, area, mask, land, to_odd, to_even, fb, wb, ab, kb, sem):
    copies = []
    for n, (src, dst) in enumerate(((f, fb), (w, wb), (area, ab), (mask, kb))):
        for h in range(2):
            rows = pl.ds(120 * h, 8)
            part = src.at[:, rows] if len(src.shape) == 3 else src.at[rows]
            copies.append(pltpu.make_async_copy(part, dst.at[h], sem.at[2 * n + h]))
    for c in copies:
        c.start()
    odd = lax.axis_index("lat") % 2 == 1
    for c in copies:
        c.wait()
    m_lo = step_factor(ab[0, 0:2], kb[0, 0:2], land[0, 0])
    m_hi = step_factor(ab[1, 6:8], kb[1, 6:8], land[0, 0])
    zero = jnp.zeros((2, 128), F32)
    for g in range(28):
        if g < NP:
            south, north = fb[0, g, 0:2], fb[1, g, 6:8]
        elif g < GM:
            south, north = wb[0, g - NP, 0:2], wb[1, g - NP, 6:8]
        elif g == GM:
            south, north = m_lo, m_hi
        else:
            south, north = zero, zero
        to_odd[2 * g : 2 * g + 2] = jnp.where(odd, north, south)
        to_even[2 * g : 2 * g + 2] = jnp.where(odd, south, north)


def columns_kernel(f, w, area, mask, land, out):
    for r in range(0, 128, CHUNK):
        rr = slice(r, r + CHUNK)
        group = lanes((CHUNK, 128)) // 4
        acc = jnp.zeros((CHUNK, 128), F32)
        for g in range(28):
            if g < NP:
                x = f[g, rr]
            elif g < GM:
                x = w[g - NP, rr]
            elif g == GM:
                x = step_factor(area[rr], mask[rr], land[0, 0])
            else:
                x = w[0, rr]
            acc = jnp.where(group == g, roll(x, 4 * g + 2 + (g == GS), 1), acc)
        out[rr] = acc


def strips_kernel(to_odd, to_even, got_odd, got_even, pack, out, north, south, recv):
    odd = lax.axis_index("lat") % 2 == 1
    top = lax.axis_index("lat") == lax.axis_size("lat") - 1
    raw = jnp.where(odd, got_odd[...], got_even[...])
    row = rows_of((ROWS2, 128))
    flip = (rows_of((128, 128)) + lanes((128, 128)) == 127).astype(F32)
    mirrored = jnp.dot(raw, flip, precision=HIGH, preferred_element_type=F32)
    mirrored = jnp.where((row >= 32) & (row < 48), -mirrored, mirrored)
    mirrored = jnp.where(row % 2 == 0, roll(mirrored, -1, 0), roll(mirrored, 1, 0))
    recv[0] = jnp.where(top, mirrored, raw)
    recv[1] = jnp.where(odd, got_even[...], got_odd[...])
    recv[2] = jnp.where(odd, to_odd[...], to_even[...])
    recv[3] = jnp.where(odd, to_even[...], to_odd[...])
    for g in range(28):
        two = slice(2 * g, 2 * g + 2)
        north[4 * g : 4 * g + 2] = recv[2, two]
        north[4 * g + 2 : 4 * g + 4] = recv[0, two]
        south[4 * g : 4 * g + 2] = recv[1, two]
        south[4 * g + 2 : 4 * g + 4] = recv[3, two]
    a, b = recv[0, 2 * GN : 2 * GN + 1], recv[0, 2 * GN + 1 : 2 * GN + 2]
    north[4 * GN + 2 : 4 * GN + 3] = jnp.where(top, b, a)
    north[4 * GS + 2 : 4 * GS + 3] = jnp.where(top, a, recv[2, 2 * GN + 1 : 2 * GN + 2])
    south[4 * GS + 1 : 4 * GS + 2] = recv[1, 2 * GN : 2 * GN + 1]
    lane = lanes((ROWS4, 128))
    acc = jnp.where(lane // 4 == 28, roll(north[...], 114, 1), pack[0:ROWS4])
    out[0:ROWS4] = jnp.where(lane // 4 == 29, roll(south[...], 118, 1), acc)
    out[ROWS4:128] = pack[ROWS4:128]


def repeat_half(v, half):
    low = rows_of(v.shape) < 4
    other = roll(v, 4, 0)
    return jnp.where(low, v, other) if half == 0 else jnp.where(low, other, v)


def lat_strip(strip, ends, shift_w, shift_e, top):
    lane = lanes((8, 128))

    def tile(t):
        x = strip[8 * t : 8 * t + 8]
        xe, xw = roll(x, -1, 1), roll(x, 1, 1)
        if ends is not None:
            w = roll(ends[0][8 * t : 8 * t + 8], shift_w, 1)
            e = roll(ends[1][8 * t : 8 * t + 8], shift_e, 1)
            xe, xw = jnp.where(lane == 127, e, xe), jnp.where(lane == 0, w, xw)
        return x, xe, xw

    x12, e12, w12 = tile(12)
    x13 = strip[104:112]
    here, right, left = (repeat_half(a, 0) for a in (x12, e12, w12))
    we = here if top is None else jnp.where(top, right, here)
    ww = left if top is None else jnp.where(top, here, left)
    m = repeat_half(x13, 0)
    me, mw = m * we, m * ww
    mn, ms = m * repeat_half(x12, 1), m * repeat_half(x13, 1)
    base = 1.0 - ((me + mw) + (mn + ms))
    c = []
    for t in range(2):
        u, ue, uw = tile(8 + t)
        v = strip[8 * (10 + t) : 8 * (10 + t) + 8]
        c.append(coefs(u + ue, u + uw, v + roll(v, -1, 0), v + roll(v, 1, 0), me, mw, mn, ms, base))
    out = []
    for t in range(12):
        x, xe, xw = tile(t)
        out.append(apply(c[t % 2], x, xe, xw, roll(x, -1, 0), roll(x, 1, 0)))
    return out


def inner_kernel(fields, w, area, mask, land, north, south, res, ends, mid, halo, mw5):
    top = lax.axis_index("lat") == lax.axis_size("lat") - 1
    for s, tiles in enumerate(
        (lat_strip(south, None, 0, 0, None), lat_strip(north, None, 0, 0, top))
    ):
        for t in range(12):
            halo[s, 8 * t : 8 * t + 8] = tiles[t]

    m = step_factor(area[...], mask[...], land[0, 0])
    we, wn = w[0], w[1]
    first = rows_of((128, 128)) == 0
    ws = jnp.where(first, south[4 * GN + 1 : 4 * GN + 2], roll(wn, 1, 0))
    me, mw, mn, ms = m * we, m * roll(we, 1, 1), m * wn, m * ws
    for n, x in enumerate((me, mw, mn, ms, 1.0 - ((me + mw) + (mn + ms)))):
        mw5[n] = x
    ends[...] = jnp.zeros((128, 128), F32)

    lane = lanes((CHUNK, 128))
    row = rows_of((CHUNK, 128))
    for k in range(4):

        def first_get(f, r):
            g = 4 * f + k
            x = fields[f, k, r : r + CHUNK]
            if r == 0:
                s = jnp.where(row == 0, south[4 * g + 1 : 4 * g + 2], roll(x, 1, 0))
            else:
                s = fields[f, k, r - 1 : r - 1 + CHUNK]
            if r == 128 - CHUNK:
                n = jnp.where(row == CHUNK - 1, north[4 * g + 2 : 4 * g + 3], roll(x, -1, 0))
            else:
                n = fields[f, k, r + 1 : r + 1 + CHUNK]
            return x, n, s

        def second_get(f, r):
            return tuple(mid[f, PAD + r + d : PAD + r + d + CHUNK] for d in (0, 1, -1))

        for f in range(6):
            g = 4 * f + k
            mid[f, PAD - 1 : PAD] = halo[0, 4 * g + 1 : 4 * g + 2]
            mid[f, PAD + 128 : PAD + 129] = halo[1, 4 * g + 2 : 4 * g + 3]
        for substep, get in enumerate((first_get, second_get)):
            for r in range(0, 128, CHUNK):
                rr = slice(r, r + CHUNK)
                u = get(4, r)[0]
                v, vn, vs = get(5, r)
                c = coefs(u + roll(u, -1, 1), u + roll(u, 1, 1), v + vn, v + vs,
                          *(mw5[n, rr] for n in range(5)))
                acc = ends[rr]
                for f in range(6):
                    g = 4 * f + k
                    x, xn, xs = get(f, r)
                    xe, xw = roll(x, -1, 1), roll(x, 1, 1)
                    y = apply(c, x, xe, xw, xn, xs)
                    if substep == 0:
                        mid[f, PAD + r : PAD + r + CHUNK] = y
                    else:
                        res[f, k, rr] = y
                        beside = jnp.where(lane < 64, xe, xw)
                        acc = jnp.where(lane // 4 == g, roll(beside, 4 * g + 2, 1), acc)
                if substep == 1:
                    ends[rr] = acc


def spread_matrix():
    out = np.zeros((7, 128, 128), np.float32)
    for l in range(128):
        k, j = l // 4 % 4, l % 4
        u, v = 64 + 4 * k + j, 80 + 4 * k + j
        for n, src in enumerate((
            (u, u + 1), (u, u - 1), (v,), (4 * GE + j,),
            (4 * GS if j == 0 else 4 * GE + j - 1,), (4 * GN + j,), (4 * GM + j,),
        )):
            for i in src:
                out[n, i, l] = 1.0
    return np.concatenate(list(out), axis=1)


def spread(x, matrix):
    hi = x.astype(jnp.bfloat16)
    rest = x - hi.astype(F32)
    mid = rest.astype(jnp.bfloat16)
    lo = (rest - mid.astype(F32)).astype(jnp.bfloat16)
    dot = functools.partial(jnp.dot, preferred_element_type=F32)
    return dot(lo, matrix) + dot(mid, matrix) + dot(hi, matrix)


def outer_kernel(pack, got_even, got_odd, north, south, inner, ends, matrix, out_hbm,
                 side, wide, halo, z, res, sem):
    odd = lax.axis_index("lon") % 2 == 1
    top = lax.axis_index("lat") == lax.axis_size("lat") - 1
    west = jnp.where(odd, got_even[...], got_odd[...])
    east = jnp.where(odd, got_odd[...], got_even[...])
    own = pack[...]
    lane = lanes((128, 128))
    j = lane % 4
    span = 128 + 2 * PAD

    def fill(s, strip, above, below):
        side[s, PAD : PAD + 128] = strip
        side[s, 0:PAD] = jnp.broadcast_to(below, (PAD, 128))
        side[s, PAD + 128 : span] = jnp.broadcast_to(above, (PAD, 128))

    def widen(n):
        for s in range(2):
            wide[s, :, 0 : 128 * n] = spread(side[s], matrix[:, 0 : 128 * n])

    def update(s, r):
        def rep(n, d=0):
            return wide[s, PAD + r + d : PAD + r + d + CHUNK, 128 * n : 128 * n + 128]

        def at(d):
            return side[s, PAD + r + d : PAD + r + d + CHUNK]

        m, v, x = rep(6), rep(2), at(0)
        me, mw, mn, ms = m * rep(3), m * rep(4), m * rep(5), m * rep(5, -1)
        base = 1.0 - ((me + mw) + (mn + ms))
        c = coefs(rep(0), rep(1), v + rep(2, 1), v + rep(2, -1), me, mw, mn, ms, base)
        return apply(c, x, roll(x, -1, 1), roll(x, 1, 1), at(1), at(-1))

    j1 = lanes((1, 128)) % 4

    def as_row(turned, columns, shift):
        parts = [roll(turned[c : c + 1], shift + d, 1) for c, d in zip(columns, (-2, -1, 0, 1))]
        low = jnp.where(j1 == 0, parts[0], parts[1])
        return jnp.where(j1 < 2, low, jnp.where(j1 == 2, parts[2], parts[3]))

    three = jnp.where(lane < 112, roll(own, -8, 1), jnp.where(lane < 120, west, roll(east, 8, 1)))
    turned = three.T
    above, below = as_row(turned, range(104, 108), 0), as_row(turned, range(108, 112), 1)
    fill(0, jnp.where(j < 2, west, own),
         jnp.where(j1 == 1, roll(turned[113:114], -1, 1), above),
         jnp.where(j1 == 1, turned[117:118], below))
    fill(1, jnp.where(j < 2, own, east),
         jnp.where(j1 == 2, turned[122:123], above),
         jnp.where(j1 == 2, roll(turned[126:127], 1, 1), below))
    widen(7)

    packs = (west, east)
    low = lat_strip(south, packs, 11, 9, None)
    high = lat_strip(north, packs, 15, 13, top)
    ring = rows_of((8, 128)) % 4 == 2
    for t in range(12):
        halo[8 * t : 8 * t + 8] = jnp.where(ring, high[t], low[t])
    halo[96:128] = jnp.zeros((32, 128), F32)
    turned = halo[...].T
    outer = (126, 127, 0, 1)
    above, below = as_row(turned, outer, 0), as_row(turned, outer, 1)

    new = [[update(s, r) for r in range(0, 128, CHUNK)] for s in range(2)]
    edge = (j == 0) | (j == 3)
    for s in range(2):
        strip = jnp.where(edge, roll(ends[...], 1 - 2 * s, 1), jnp.concatenate(new[s], axis=0))
        fill(s, strip, above, below)
    widen(3)
    jj = lanes((CHUNK, 128)) % 4
    for r in range(0, 128, CHUNK):
        z[r : r + CHUNK] = jnp.where(jj < 2, update(1, r), update(0, r))

    outs = []
    outer = (lanes((CHUNK, 128)) < 2) | (lanes((CHUNK, 128)) >= 126)
    for k in range(4):
        for r in range(0, 128, CHUNK):
            rr = slice(r, r + CHUNK)
            zr = z[rr]
            for f in range(6):
                res[f, k, rr] = jnp.where(outer, roll(zr, -(4 * (4 * f + k) + 2), 1), inner[f, k, rr])
        c = pltpu.make_async_copy(res.at[:, k], out_hbm.at[:, k], sem.at[k])
        c.start()
        outs.append(c)
    for c in outs:
        c.wait()


def cost(nbytes, flops):
    return pl.CostEstimate(flops=flops, bytes_accessed=nbytes, transcendentals=0)


def vmem():
    return pl.BlockSpec(memory_space=pltpu.VMEM)


def smem():
    return pl.BlockSpec(memory_space=pltpu.SMEM)


def local(nlon, nlat, fields, weights, area, mask, land):
    shape = jax.ShapeDtypeStruct
    planes = fields.reshape(NP, 128, 128)
    params = pltpu.CompilerParams(vmem_limit_bytes=24 << 20)

    rows = shape((ROWS2, 128), F32)
    to_odd, to_even = pl.pallas_call(
        rows_kernel,
        out_shape=(rows, rows),
        in_specs=[pl.BlockSpec(memory_space=pltpu.HBM)] * 4 + [smem()],
        out_specs=(vmem(), vmem()),
        scratch_shapes=[
            pltpu.VMEM((2, NP, 8, 128), F32),
            pltpu.VMEM((2, 2, 8, 128), F32),
            pltpu.VMEM((2, 8, 128), F32),
            pltpu.VMEM((2, 8, 128), jnp.int32),
            pltpu.SemaphoreType.DMA((8,)),
        ],
        cost_estimate=cost(1 << 18, 1 << 16),
        name="rows",
    )(planes, weights, area, mask, land)

    axes = ("lon", "lat")
    with jax.named_scope("lat_odd"):
        got_odd = lax.ppermute(to_odd, axes, lat_pairs(nlon, nlat, True))
    with jax.named_scope("lat_even"):
        got_even = lax.ppermute(to_even, axes, lat_pairs(nlon, nlat, False))

    tile = shape((128, 128), F32)
    pack = pl.pallas_call(
        columns_kernel,
        out_shape=tile,
        in_specs=[vmem()] * 4 + [smem()],
        out_specs=vmem(),
        compiler_params=params,
        cost_estimate=cost(2 << 20, 1 << 20),
        name="columns",
    )(planes, weights, area, mask, land)

    pack, north, south = pl.pallas_call(
        strips_kernel,
        out_shape=(tile, shape((ROWS4, 128), F32), shape((ROWS4, 128), F32)),
        in_specs=[vmem()] * 5,
        out_specs=(vmem(),) * 3,
        scratch_shapes=[pltpu.VMEM((4, ROWS2, 128), F32)],
        compiler_params=params,
        cost_estimate=cost(1 << 18, 1 << 18),
        name="strips",
    )(to_odd, to_even, got_odd, got_even, pack)

    with jax.named_scope("lon_even"):
        col_even = lax.ppermute(pack, axes, lon_pairs(nlon, nlat, False))
    with jax.named_scope("lon_odd"):
        col_odd = lax.ppermute(pack, axes, lon_pairs(nlon, nlat, True))

    padded = 128 + 2 * PAD
    state = shape((6, 4, 128, 128), F32)
    inner, ends = pl.pallas_call(
        inner_kernel,
        out_shape=(state, tile),
        in_specs=[vmem()] * 4 + [smem()] + [vmem()] * 2,
        out_specs=(vmem(), vmem()),
        scratch_shapes=[
            pltpu.VMEM((6, padded, 128), F32),
            pltpu.VMEM((2, 96, 128), F32),
            pltpu.VMEM((5, 128, 128), F32),
        ],
        compiler_params=params,
        cost_estimate=cost(4 << 20, 20 << 20),
        name="inner",
    )(fields, weights, area, mask, land, north, south)

    return pl.pallas_call(
        outer_kernel,
        out_shape=state,
        in_specs=[vmem()] * 8,
        out_specs=pl.BlockSpec(memory_space=pltpu.HBM),
        scratch_shapes=[
            pltpu.VMEM((2, padded, 128), F32),
            pltpu.VMEM((2, padded, 7 * 128), F32),
            pltpu.VMEM((128, 128), F32),
            pltpu.VMEM((128, 128), F32),
            pltpu.VMEM((6, 4, 128, 128), F32),
            pltpu.SemaphoreType.DMA((4,)),
        ],
        compiler_params=params,
        cost_estimate=cost(4 << 20, 1 << 20),
        name="outer",
    )(pack, col_even, col_odd, north, south, inner, ends, jnp.asarray(spread_matrix(), jnp.bfloat16))


def solution(mesh):
    in_specs = (
        P(None, None, "lat", "lon"),
        P(None, "lat", "lon"),
        P("lat", "lon"),
        P("lat", "lon"),
        P("lat", "lon"),
    )
    body = functools.partial(local, mesh.shape["lon"], mesh.shape["lat"])
    return jax.shard_map(
        body, mesh=mesh, in_specs=in_specs, out_specs=P(None, None, "lat", "lon"), check_vma=False
    )
```

```python
import functools

import jax
import jax.numpy as jnp
import numpy as np
from jax import lax
from jax.experimental import pallas as pl
from jax.experimental.pallas import tpu as pltpu
from jax.sharding import PartitionSpec as P

F32 = jnp.float32
TIME_STEP = 0.1
NP = 24
GE, GN, GM, GS = 24, 25, 26, 27
ROWS2, ROWS4 = 56, 112
PAD = 8
CHUNK = 32
HIGH = lax.Precision.HIGHEST


def lon_pairs(nlon, nlat, odd):
    def other(i):
        if not odd:
            return i ^ 1
        return (i + 1) % nlon if i % 2 else (i - 1) % nlon

    return [(i * nlat + l, other(i) * nlat + l) for i in range(nlon) for l in range(nlat)]


def lat_pairs(nlon, nlat, odd):
    pairs = []
    for i in range(nlon):
        for l in range(nlat):
            if not odd:
                pairs.append((i * nlat + l, i * nlat + (l ^ 1)))
            elif l == nlat - 1:
                pairs.append((i * nlat + l, (nlon - 1 - i) * nlat + l))
            elif l > 0:
                pairs.append((i * nlat + l, i * nlat + (l + 1 if l % 2 else l - 1)))
    return pairs


def lanes(shape):
    return lax.broadcasted_iota(jnp.int32, shape, 1)


def rows_of(shape):
    return lax.broadcasted_iota(jnp.int32, shape, 0)


def roll(x, shift, axis):
    n = x.shape[axis]
    shift %= n
    return x if shift == 0 else pltpu.roll(x, shift, axis)


def step_factor(area, mask, sea):
    return TIME_STEP * (mask.astype(F32) * sea) * area


def coefs(se, sw, sn, ss, me, mw, mn, ms, base):
    te, tw, tn, ts = me * (0.125 * se), mw * (0.125 * sw), mn * (0.125 * sn), ms * (0.125 * ss)
    return me - te, mw + tw, mn - tn, ms + ts, base + ((tw - te) + (ts - tn))


def apply(c, x, xe, xw, xn, xs):
    ce, cw, cn, cs, cc = c
    return cc * x + ((ce * xe + cw * xw) + (cn * xn + cs * xs))


def rows_kernel(f, w, area, mask, land, to_odd, to_even, sea, fb, wb, ab, kb, sem):
    copies = []
    for n, (src, dst) in enumerate(((f, fb), (w, wb), (area, ab), (mask, kb))):
        for h in range(2):
            rows = pl.ds(120 * h, 8)
            part = src.at[:, rows] if len(src.shape) == 3 else src.at[rows]
            copies.append(pltpu.make_async_copy(part, dst.at[h], sem.at[2 * n + h]))
    for c in copies:
        c.start()
    odd = lax.axis_index("lat") % 2 == 1
    for c in copies:
        c.wait()
    is_sea = (1 - land[0, 0]).astype(F32)
    sea[...] = jnp.full((8, 128), is_sea, F32)
    m_lo = step_factor(ab[0, 0:2], kb[0, 0:2], is_sea)
    m_hi = step_factor(ab[1, 6:8], kb[1, 6:8], is_sea)
    zero = jnp.zeros((2, 128), F32)
    for g in range(28):
        if g < NP:
            south, north = fb[0, g, 0:2], fb[1, g, 6:8]
        elif g < GM:
            south, north = wb[0, g - NP, 0:2], wb[1, g - NP, 6:8]
        elif g == GM:
            south, north = m_lo, m_hi
        else:
            south, north = zero, zero
        to_odd[2 * g : 2 * g + 2] = jnp.where(odd, north, south)
        to_even[2 * g : 2 * g + 2] = jnp.where(odd, south, north)


def columns_kernel(f, w, area, mask, sea, out):
    for r in range(0, 128, CHUNK):
        rr = slice(r, r + CHUNK)
        group = lanes((CHUNK, 128)) // 4
        acc = jnp.zeros((CHUNK, 128), F32)
        for g in range(28):
            if g < NP:
                x = f[g, rr]
            elif g < GM:
                x = w[g - NP, rr]
            elif g == GM:
                x = step_factor(area[rr], mask[rr], sea[0:1])
            else:
                x = w[0, rr]
            acc = jnp.where(group == g, roll(x, 4 * g + 2 + (g == GS), 1), acc)
        out[rr] = acc


def strips_kernel(to_odd, to_even, got_odd, got_even, pack, out, lon_odd, lon_even, north, south, recv):
    odd = lax.axis_index("lat") % 2 == 1
    top = lax.axis_index("lat") == lax.axis_size("lat") - 1
    raw = jnp.where(odd, got_odd[...], got_even[...])
    row = rows_of((ROWS2, 128))
    flip = (rows_of((128, 128)) + lanes((128, 128)) == 127).astype(F32)
    mirrored = jnp.dot(raw, flip, precision=HIGH, preferred_element_type=F32)
    mirrored = jnp.where((row >= 32) & (row < 48), -mirrored, mirrored)
    mirrored = jnp.where(row % 2 == 0, roll(mirrored, -1, 0), roll(mirrored, 1, 0))
    recv[0] = jnp.where(top, mirrored, raw)
    recv[1] = jnp.where(odd, got_even[...], got_odd[...])
    recv[2] = jnp.where(odd, to_odd[...], to_even[...])
    recv[3] = jnp.where(odd, to_even[...], to_odd[...])
    for g in range(28):
        two = slice(2 * g, 2 * g + 2)
        north[4 * g : 4 * g + 2] = recv[2, two]
        north[4 * g + 2 : 4 * g + 4] = recv[0, two]
        south[4 * g : 4 * g + 2] = recv[1, two]
        south[4 * g + 2 : 4 * g + 4] = recv[3, two]
    a, b = recv[0, 2 * GN : 2 * GN + 1], recv[0, 2 * GN + 1 : 2 * GN + 2]
    north[4 * GN + 2 : 4 * GN + 3] = jnp.where(top, b, a)
    north[4 * GS + 2 : 4 * GS + 3] = jnp.where(top, a, recv[2, 2 * GN + 1 : 2 * GN + 2])
    south[4 * GS + 1 : 4 * GS + 2] = recv[1, 2 * GN : 2 * GN + 1]
    lane = lanes((ROWS4, 128))
    acc = jnp.where(lane // 4 == 28, roll(north[...], 114, 1), pack[0:ROWS4])
    out[0:ROWS4] = jnp.where(lane // 4 == 29, roll(south[...], 118, 1), acc)
    out[ROWS4:128] = pack[ROWS4:128]
    j = lanes((64, 128)) % 4
    a, b = out[0:64], out[64:128]
    to_east = jnp.where(j < 2, a, roll(b, 2, 1))
    to_west = jnp.where(j < 2, roll(b, -2, 1), a)
    lon_is_odd = lax.axis_index("lon") % 2 == 1
    lon_odd[...] = jnp.where(lon_is_odd, to_east, to_west)
    lon_even[...] = jnp.where(lon_is_odd, to_west, to_east)


def repeat_half(v, half):
    low = rows_of(v.shape) < 4
    other = roll(v, 4, 0)
    return jnp.where(low, v, other) if half == 0 else jnp.where(low, other, v)


def lat_strip(strip, ends, shift_w, shift_e, top):
    lane = lanes((8, 128))
    if ends is not None:
        west = roll(ends[0][0:ROWS4], shift_w, 1)
        east = roll(ends[1][0:ROWS4], shift_e, 1)

    def tile(t):
        x = strip[8 * t : 8 * t + 8]
        xe, xw = roll(x, -1, 1), roll(x, 1, 1)
        if ends is not None:
            xe = jnp.where(lane == 127, east[8 * t : 8 * t + 8], xe)
            xw = jnp.where(lane == 0, west[8 * t : 8 * t + 8], xw)
        return x, xe, xw

    x12, e12, w12 = tile(12)
    x13 = strip[104:112]
    here, right, left = (repeat_half(a, 0) for a in (x12, e12, w12))
    we = here if top is None else jnp.where(top, right, here)
    ww = left if top is None else jnp.where(top, here, left)
    m = repeat_half(x13, 0)
    me, mw = m * we, m * ww
    mn, ms = m * repeat_half(x12, 1), m * repeat_half(x13, 1)
    base = 1.0 - ((me + mw) + (mn + ms))
    c = []
    for t in range(2):
        u, ue, uw = tile(8 + t)
        v = strip[8 * (10 + t) : 8 * (10 + t) + 8]
        c.append(coefs(u + ue, u + uw, v + roll(v, -1, 0), v + roll(v, 1, 0), me, mw, mn, ms, base))
    out = []
    for t in range(12):
        x, xe, xw = tile(t)
        out.append(apply(c[t % 2], x, xe, xw, roll(x, -1, 0), roll(x, 1, 0)))
    return out


def inner_kernel(fields, w, area, mask, sea, north, south, res, ends, mid, halo, mw5, beside):
    top = lax.axis_index("lat") == lax.axis_size("lat") - 1
    for s, tiles in enumerate(
        (lat_strip(south, None, 0, 0, None), lat_strip(north, None, 0, 0, top))
    ):
        for t in range(12):
            halo[s, 8 * t : 8 * t + 8] = tiles[t]

    m = step_factor(area[...], mask[...], sea[0:1])
    we, wn = w[0], w[1]
    first = rows_of((128, 128)) == 0
    ws = jnp.where(first, south[4 * GN + 1 : 4 * GN + 2], roll(wn, 1, 0))
    me, mw, mn, ms = m * we, m * roll(we, 1, 1), m * wn, m * ws
    for n, x in enumerate((me, mw, mn, ms, 1.0 - ((me + mw) + (mn + ms)))):
        mw5[n] = x
    lane = lanes((CHUNK, 128))
    row = rows_of((CHUNK, 128))

    def level(k, _):
        def first_get(f, r):
            g = 4 * (4 * f + k)
            x = fields[f, k, r : r + CHUNK]
            if r == 0:
                s = jnp.where(row == 0, south[pl.ds(g + 1, 1)], roll(x, 1, 0))
            else:
                s = fields[f, k, r - 1 : r - 1 + CHUNK]
            if r == 128 - CHUNK:
                n = jnp.where(row == CHUNK - 1, north[pl.ds(g + 2, 1)], roll(x, -1, 0))
            else:
                n = fields[f, k, r + 1 : r + 1 + CHUNK]
            return x, n, s

        def second_get(f, r):
            return tuple(mid[f, PAD + r + d : PAD + r + d + CHUNK] for d in (0, 1, -1))

        for f in range(6):
            g = 4 * (4 * f + k)
            mid[f, PAD - 1 : PAD] = halo[0, pl.ds(g + 1, 1)]
            mid[f, PAD + 128 : PAD + 129] = halo[1, pl.ds(g + 2, 1)]
        for substep, get in enumerate((first_get, second_get)):
            for r in range(0, 128, CHUNK):
                rr = slice(r, r + CHUNK)
                u = get(4, r)[0]
                v, vn, vs = get(5, r)
                c = coefs(u + roll(u, -1, 1), u + roll(u, 1, 1), v + vn, v + vs,
                          *(mw5[n, rr] for n in range(5)))
                for f in range(6):
                    x, xn, xs = get(f, r)
                    xe, xw = roll(x, -1, 1), roll(x, 1, 1)
                    y = apply(c, x, xe, xw, xn, xs)
                    if substep == 0:
                        mid[f, PAD + r : PAD + r + CHUNK] = y
                    else:
                        res[f, k, rr] = y
                        beside[f, k, rr] = jnp.where(lane < 64, xe, xw)
        return 0

    lax.fori_loop(0, 4, level, 0)
    for r in range(0, 128, CHUNK):
        acc = jnp.zeros((CHUNK, 128), F32)
        for g in range(NP):
            x = roll(beside[g // 4, g % 4, r : r + CHUNK], 4 * g + 2, 1)
            acc = jnp.where(lane // 4 == g, x, acc)
        ends[r : r + CHUNK] = acc


def spread_matrix():
    out = np.zeros((7, 128, 128), np.float32)
    for l in range(128):
        k, j = l // 4 % 4, l % 4
        u, v = 64 + 4 * k + j, 80 + 4 * k + j
        for n, src in enumerate((
            (u, u + 1), (u, u - 1), (v,), (4 * GE + j,),
            (4 * GS if j == 0 else 4 * GE + j - 1,), (4 * GN + j,), (4 * GM + j,),
        )):
            for i in src:
                out[n, i, l] = 1.0
    return np.concatenate(list(out), axis=1)


def spread(x, matrix):
    hi = x.astype(jnp.bfloat16)
    rest = x - hi.astype(F32)
    mid = rest.astype(jnp.bfloat16)
    lo = (rest - mid.astype(F32)).astype(jnp.bfloat16)
    dot = functools.partial(jnp.dot, preferred_element_type=F32)
    return dot(lo, matrix) + dot(mid, matrix) + dot(hi, matrix)


def outer_kernel(pack, got_even, got_odd, north, south, inner, ends, matrix, out_hbm,
                 side, wide, halo, z, res, sem):
    odd = lax.axis_index("lon") % 2 == 1
    top = lax.axis_index("lat") == lax.axis_size("lat") - 1
    west = jnp.where(odd, got_even[...], got_odd[...])
    east = jnp.where(odd, got_odd[...], got_even[...])
    west = jnp.concatenate([west, roll(west, -2, 1)], axis=0)
    east = jnp.concatenate([east, roll(east, 2, 1)], axis=0)
    own = pack[...]
    lane = lanes((128, 128))
    j = lane % 4
    span = 128 + 2 * PAD

    def fill(s, strip, above, below):
        side[s, PAD : PAD + 128] = strip
        side[s, 0:PAD] = jnp.broadcast_to(below, (PAD, 128))
        side[s, PAD + 128 : span] = jnp.broadcast_to(above, (PAD, 128))

    def widen(n):
        for s in range(2):
            wide[s, :, 0 : 128 * n] = spread(side[s], matrix[:, 0 : 128 * n])

    def update(s, r):
        def rep(n, d=0):
            return wide[s, PAD + r + d : PAD + r + d + CHUNK, 128 * n : 128 * n + 128]

        def at(d):
            return side[s, PAD + r + d : PAD + r + d + CHUNK]

        m, v, x = rep(6), rep(2), at(0)
        me, mw, mn, ms = m * rep(3), m * rep(4), m * rep(5), m * rep(5, -1)
        base = 1.0 - ((me + mw) + (mn + ms))
        c = coefs(rep(0), rep(1), v + rep(2, 1), v + rep(2, -1), me, mw, mn, ms, base)
        return apply(c, x, roll(x, -1, 1), roll(x, 1, 1), at(1), at(-1))

    j1 = lanes((1, 128)) % 4

    def as_row(turned, columns, shift):
        parts = [roll(turned[c : c + 1], shift + d, 1) for c, d in zip(columns, (-2, -1, 0, 1))]
        low = jnp.where(j1 == 0, parts[0], parts[1])
        return jnp.where(j1 < 2, low, jnp.where(j1 == 2, parts[2], parts[3]))

    three = jnp.where(lane < 112, roll(own, -8, 1), jnp.where(lane < 120, west, roll(east, 8, 1)))
    turned = three.T
    above, below = as_row(turned, range(104, 108), 0), as_row(turned, range(108, 112), 1)
    fill(0, jnp.where(j < 2, west, own),
         jnp.where(j1 == 1, roll(turned[113:114], -1, 1), above),
         jnp.where(j1 == 1, turned[117:118], below))
    fill(1, jnp.where(j < 2, own, east),
         jnp.where(j1 == 2, turned[122:123], above),
         jnp.where(j1 == 2, roll(turned[126:127], 1, 1), below))
    widen(7)

    packs = (west, east)
    low = lat_strip(south, packs, 11, 9, None)
    high = lat_strip(north, packs, 15, 13, top)
    ring = rows_of((8, 128)) % 4 == 2
    for t in range(12):
        halo[8 * t : 8 * t + 8] = jnp.where(ring, high[t], low[t])
    halo[96:128] = jnp.zeros((32, 128), F32)
    turned = halo[...].T
    outer = (126, 127, 0, 1)
    above, below = as_row(turned, outer, 0), as_row(turned, outer, 1)

    new = [[update(s, r) for r in range(0, 128, CHUNK)] for s in range(2)]
    edge = (j == 0) | (j == 3)
    for s in range(2):
        strip = jnp.where(edge, roll(ends[...], 1 - 2 * s, 1), jnp.concatenate(new[s], axis=0))
        fill(s, strip, above, below)
    widen(3)
    jj = lanes((CHUNK, 128)) % 4
    for r in range(0, 128, CHUNK):
        z[r : r + CHUNK] = jnp.where(jj < 2, update(1, r), update(0, r))

    outs = []
    outer = (lanes((CHUNK, 128)) < 2) | (lanes((CHUNK, 128)) >= 126)
    for k in range(4):
        for r in range(0, 128, CHUNK):
            rr = slice(r, r + CHUNK)
            zr = z[rr]
            for f in range(6):
                res[f, k, rr] = jnp.where(outer, roll(zr, -(4 * (4 * f + k) + 2), 1), inner[f, k, rr])
        c = pltpu.make_async_copy(res.at[:, k], out_hbm.at[:, k], sem.at[k])
        c.start()
        outs.append(c)
    for c in outs:
        c.wait()


def cost(nbytes, flops):
    return pl.CostEstimate(flops=flops, bytes_accessed=nbytes, transcendentals=0)


def vmem():
    return pl.BlockSpec(memory_space=pltpu.VMEM)


def local(nlon, nlat, fields, weights, area, mask, land):
    shape = jax.ShapeDtypeStruct
    planes = fields.reshape(NP, 128, 128)
    params = pltpu.CompilerParams(vmem_limit_bytes=24 << 20)

    rows = shape((ROWS2, 128), F32)
    to_odd, to_even, sea = pl.pallas_call(
        rows_kernel,
        out_shape=(rows, rows, shape((8, 128), F32)),
        in_specs=[pl.BlockSpec(memory_space=pltpu.HBM)] * 4 + [pl.BlockSpec(memory_space=pltpu.SMEM)],
        out_specs=(vmem(),) * 3,
        scratch_shapes=[
            pltpu.VMEM((2, NP, 8, 128), F32),
            pltpu.VMEM((2, 2, 8, 128), F32),
            pltpu.VMEM((2, 8, 128), F32),
            pltpu.VMEM((2, 8, 128), jnp.int32),
            pltpu.SemaphoreType.DMA((8,)),
        ],
        cost_estimate=cost(1 << 18, 1 << 16),
        name="rows",
    )(planes, weights, area, mask, land)

    axes = ("lon", "lat")
    with jax.named_scope("lat_odd"):
        got_odd = lax.ppermute(to_odd, axes, lat_pairs(nlon, nlat, True))
    with jax.named_scope("lat_even"):
        got_even = lax.ppermute(to_even, axes, lat_pairs(nlon, nlat, False))

    tile, half = shape((128, 128), F32), shape((64, 128), F32)
    pack = pl.pallas_call(
        columns_kernel,
        out_shape=tile,
        in_specs=[vmem()] * 5,
        out_specs=vmem(),
        compiler_params=params,
        cost_estimate=cost(2 << 20, 1 << 20),
        name="columns",
    )(planes, weights, area, mask, sea)

    pack, lon_odd, lon_even, north, south = pl.pallas_call(
        strips_kernel,
        out_shape=(tile, half, half, shape((ROWS4, 128), F32), shape((ROWS4, 128), F32)),
        in_specs=[vmem()] * 5,
        out_specs=(vmem(),) * 5,
        scratch_shapes=[pltpu.VMEM((4, ROWS2, 128), F32)],
        compiler_params=params,
        cost_estimate=cost(1 << 18, 1 << 18),
        name="strips",
    )(to_odd, to_even, got_odd, got_even, pack)

    with jax.named_scope("lon_even"):
        col_even = lax.ppermute(lon_even, axes, lon_pairs(nlon, nlat, False))
    with jax.named_scope("lon_odd"):
        col_odd = lax.ppermute(lon_odd, axes, lon_pairs(nlon, nlat, True))

    padded = 128 + 2 * PAD
    state = shape((6, 4, 128, 128), F32)
    inner, ends = pl.pallas_call(
        inner_kernel,
        out_shape=(state, tile),
        in_specs=[vmem()] * 7,
        out_specs=(vmem(), vmem()),
        scratch_shapes=[
            pltpu.VMEM((6, padded, 128), F32),
            pltpu.VMEM((2, 96, 128), F32),
            pltpu.VMEM((5, 128, 128), F32),
            pltpu.VMEM((6, 4, 128, 128), F32),
        ],
        compiler_params=params,
        cost_estimate=cost(4 << 20, 20 << 20),
        name="inner",
    )(fields, weights, area, mask, sea, north, south)

    return pl.pallas_call(
        outer_kernel,
        out_shape=state,
        in_specs=[vmem()] * 8,
        out_specs=pl.BlockSpec(memory_space=pltpu.HBM),
        scratch_shapes=[
            pltpu.VMEM((2, padded, 128), F32),
            pltpu.VMEM((2, padded, 7 * 128), F32),
            pltpu.VMEM((128, 128), F32),
            pltpu.VMEM((128, 128), F32),
            pltpu.VMEM((6, 4, 128, 128), F32),
            pltpu.SemaphoreType.DMA((4,)),
        ],
        compiler_params=params,
        cost_estimate=cost(4 << 20, 1 << 20),
        name="outer",
    )(pack, col_even, col_odd, north, south, inner, ends, jnp.asarray(spread_matrix(), jnp.bfloat16))


def solution(mesh):
    in_specs = (
        P(None, None, "lat", "lon"),
        P(None, "lat", "lon"),
        P("lat", "lon"),
        P("lat", "lon"),
        P("lat", "lon"),
    )
    body = functools.partial(local, mesh.shape["lon"], mesh.shape["lat"])
    return jax.shard_map(
        body, mesh=mesh, in_specs=in_specs, out_specs=P(None, None, "lat", "lon"), check_vma=False
    )
```

```python
import functools

import jax
import jax.numpy as jnp
import numpy as np
from jax import lax
from jax.experimental import pallas as pl
from jax.experimental.pallas import tpu as pltpu
from jax.sharding import PartitionSpec as P

F32 = jnp.float32
TIME_STEP = 0.1
NP = 24
GE, GN, GM, GS = 24, 25, 26, 27
ROWS2, ROWS4 = 56, 112
PAD = 8
CHUNK = 32
HIGH = lax.Precision.HIGHEST


def lon_pairs(nlon, nlat, step):
    return [(i * nlat + l, (i + step) % nlon * nlat + l) for i in range(nlon) for l in range(nlat)]


def lat_pairs(nlon, nlat, odd):
    pairs = []
    for i in range(nlon):
        for l in range(nlat):
            if not odd:
                pairs.append((i * nlat + l, i * nlat + (l ^ 1)))
            elif l == nlat - 1:
                pairs.append((i * nlat + l, (nlon - 1 - i) * nlat + l))
            elif l > 0:
                pairs.append((i * nlat + l, i * nlat + (l + 1 if l % 2 else l - 1)))
    return pairs


def lanes(shape):
    return lax.broadcasted_iota(jnp.int32, shape, 1)


def rows_of(shape):
    return lax.broadcasted_iota(jnp.int32, shape, 0)


def roll(x, shift, axis):
    n = x.shape[axis]
    shift %= n
    return x if shift == 0 else pltpu.roll(x, shift, axis)


def step_factor(area, mask, sea):
    return TIME_STEP * (mask.astype(F32) * sea) * area


def coefs(se, sw, sn, ss, me, mw, mn, ms, base):
    te, tw, tn, ts = me * (0.125 * se), mw * (0.125 * sw), mn * (0.125 * sn), ms * (0.125 * ss)
    return me - te, mw + tw, mn - tn, ms + ts, base + ((tw - te) + (ts - tn))


def apply(c, x, xe, xw, xn, xs):
    ce, cw, cn, cs, cc = c
    return cc * x + ((ce * xe + cw * xw) + (cn * xn + cs * xs))


def rows_kernel(f, w, area, mask, land, to_odd, to_even, fb, wb, ab, kb, sem):
    copies = []
    for n, (src, dst) in enumerate(((f, fb), (w, wb), (area, ab), (mask, kb))):
        for h in range(2):
            rows = pl.ds(120 * h, 8)
            part = src.at[:, rows] if len(src.shape) == 3 else src.at[rows]
            copies.append(pltpu.make_async_copy(part, dst.at[h], sem.at[2 * n + h]))
    for c in copies:
        c.start()
    odd = lax.axis_index("lat") % 2 == 1
    for c in copies:
        c.wait()
    is_sea = (1 - land[0, 0]).astype(F32)
    m_lo = step_factor(ab[0, 0:2], kb[0, 0:2], is_sea)
    m_hi = step_factor(ab[1, 6:8], kb[1, 6:8], is_sea)
    zero = jnp.zeros((2, 128), F32)
    for g in range(28):
        if g < NP:
            south, north = fb[0, g, 0:2], fb[1, g, 6:8]
        elif g < GM:
            south, north = wb[0, g - NP, 0:2], wb[1, g - NP, 6:8]
        elif g == GM:
            south, north = m_lo, m_hi
        else:
            south, north = zero, zero
        to_odd[2 * g : 2 * g + 2] = jnp.where(odd, north, south)
        to_even[2 * g : 2 * g + 2] = jnp.where(odd, south, north)


def columns_kernel(f, w, area, mask, land, out):
    sea = (1 - land[0, 0]).astype(F32)
    for r in range(0, 128, CHUNK):
        rr = slice(r, r + CHUNK)
        group = lanes((CHUNK, 128)) // 4
        acc = jnp.zeros((CHUNK, 128), F32)
        for g in range(28):
            if g < NP:
                x = f[g, rr]
            elif g < GM:
                x = w[g - NP, rr]
            elif g == GM:
                x = step_factor(area[rr], mask[rr], sea)
            else:
                x = w[0, rr]
            acc = jnp.where(group == g, roll(x, 4 * g + 2 + (g == GS), 1), acc)
        out[rr] = acc


def strips_kernel(to_odd, to_even, got_odd, got_even, pack, out, to_east, to_west, north, south, recv):
    odd = lax.axis_index("lat") % 2 == 1
    top = lax.axis_index("lat") == lax.axis_size("lat") - 1
    raw = jnp.where(odd, got_odd[...], got_even[...])
    row = rows_of((ROWS2, 128))
    flip = (rows_of((128, 128)) + lanes((128, 128)) == 127).astype(F32)
    mirrored = jnp.dot(raw, flip, precision=HIGH, preferred_element_type=F32)
    mirrored = jnp.where((row >= 32) & (row < 48), -mirrored, mirrored)
    mirrored = jnp.where(row % 2 == 0, roll(mirrored, -1, 0), roll(mirrored, 1, 0))
    recv[0] = jnp.where(top, mirrored, raw)
    recv[1] = jnp.where(odd, got_even[...], got_odd[...])
    recv[2] = jnp.where(odd, to_odd[...], to_even[...])
    recv[3] = jnp.where(odd, to_even[...], to_odd[...])
    for g in range(28):
        two = slice(2 * g, 2 * g + 2)
        north[4 * g : 4 * g + 2] = recv[2, two]
        north[4 * g + 2 : 4 * g + 4] = recv[0, two]
        south[4 * g : 4 * g + 2] = recv[1, two]
        south[4 * g + 2 : 4 * g + 4] = recv[3, two]
    a, b = recv[0, 2 * GN : 2 * GN + 1], recv[0, 2 * GN + 1 : 2 * GN + 2]
    north[4 * GN + 2 : 4 * GN + 3] = jnp.where(top, b, a)
    north[4 * GS + 2 : 4 * GS + 3] = jnp.where(top, a, recv[2, 2 * GN + 1 : 2 * GN + 2])
    south[4 * GS + 1 : 4 * GS + 2] = recv[1, 2 * GN : 2 * GN + 1]
    lane = lanes((ROWS4, 128))
    acc = jnp.where(lane // 4 == 28, roll(north[...], 114, 1), pack[0:ROWS4])
    out[0:ROWS4] = jnp.where(lane // 4 == 29, roll(south[...], 118, 1), acc)
    out[ROWS4:128] = pack[ROWS4:128]
    j = lanes((64, 128)) % 4
    a, b = out[0:64], out[64:128]
    to_east[...] = jnp.where(j < 2, a, roll(b, 2, 1))
    to_west[...] = jnp.where(j < 2, roll(b, -2, 1), a)


def repeat_half(v, half):
    low = rows_of(v.shape) < 4
    other = roll(v, 4, 0)
    return jnp.where(low, v, other) if half == 0 else jnp.where(low, other, v)


def lat_strip(strip, ends, shift_w, shift_e, top):
    lane = lanes((8, 128))
    if ends is not None:
        west = roll(ends[0][0:ROWS4], shift_w, 1)
        east = roll(ends[1][0:ROWS4], shift_e, 1)

    def tile(t):
        x = strip[8 * t : 8 * t + 8]
        xe, xw = roll(x, -1, 1), roll(x, 1, 1)
        if ends is not None:
            xe = jnp.where(lane == 127, east[8 * t : 8 * t + 8], xe)
            xw = jnp.where(lane == 0, west[8 * t : 8 * t + 8], xw)
        return x, xe, xw

    x12, e12, w12 = tile(12)
    x13 = strip[104:112]
    here, right, left = (repeat_half(a, 0) for a in (x12, e12, w12))
    we = here if top is None else jnp.where(top, right, here)
    ww = left if top is None else jnp.where(top, here, left)
    m = repeat_half(x13, 0)
    me, mw = m * we, m * ww
    mn, ms = m * repeat_half(x12, 1), m * repeat_half(x13, 1)
    base = 1.0 - ((me + mw) + (mn + ms))
    c = []
    for t in range(2):
        u, ue, uw = tile(8 + t)
        v = strip[8 * (10 + t) : 8 * (10 + t) + 8]
        c.append(coefs(u + ue, u + uw, v + roll(v, -1, 0), v + roll(v, 1, 0), me, mw, mn, ms, base))
    out = []
    for t in range(12):
        x, xe, xw = tile(t)
        out.append(apply(c[t % 2], x, xe, xw, roll(x, -1, 0), roll(x, 1, 0)))
    return out


def inner_kernel(early, fields, w, area, mask, land, north, south, *refs):
    blocks = lax.axis_size("lon") // 2
    soon = lax.axis_index("lon") % blocks < max(1, blocks // 4)

    @pl.when(soon if early else jnp.logical_not(soon))
    def _():
        inner_steps(fields, w, area, mask, land, north, south, *refs[-6:])


def inner_steps(fields, w, area, mask, land, north, south, res, ends, mid, halo, mw5, beside):
    top = lax.axis_index("lat") == lax.axis_size("lat") - 1
    for s, tiles in enumerate(
        (lat_strip(south, None, 0, 0, None), lat_strip(north, None, 0, 0, top))
    ):
        for t in range(12):
            halo[s, 8 * t : 8 * t + 8] = tiles[t]

    m = step_factor(area[...], mask[...], (1 - land[0, 0]).astype(F32))
    we, wn = w[0], w[1]
    first = rows_of((128, 128)) == 0
    ws = jnp.where(first, south[4 * GN + 1 : 4 * GN + 2], roll(wn, 1, 0))
    me, mw, mn, ms = m * we, m * roll(we, 1, 1), m * wn, m * ws
    for n, x in enumerate((me, mw, mn, ms, 1.0 - ((me + mw) + (mn + ms)))):
        mw5[n] = x
    lane = lanes((CHUNK, 128))
    row = rows_of((CHUNK, 128))

    def level(k, _):
        def first_get(f, r):
            g = 4 * (4 * f + k)
            x = fields[f, k, r : r + CHUNK]
            if r == 0:
                s = jnp.where(row == 0, south[pl.ds(g + 1, 1)], roll(x, 1, 0))
            else:
                s = fields[f, k, r - 1 : r - 1 + CHUNK]
            if r == 128 - CHUNK:
                n = jnp.where(row == CHUNK - 1, north[pl.ds(g + 2, 1)], roll(x, -1, 0))
            else:
                n = fields[f, k, r + 1 : r + 1 + CHUNK]
            return x, n, s

        def second_get(f, r):
            return tuple(mid[f, PAD + r + d : PAD + r + d + CHUNK] for d in (0, 1, -1))

        for f in range(6):
            g = 4 * (4 * f + k)
            mid[f, PAD - 1 : PAD] = halo[0, pl.ds(g + 1, 1)]
            mid[f, PAD + 128 : PAD + 129] = halo[1, pl.ds(g + 2, 1)]
        for substep, get in enumerate((first_get, second_get)):
            for r in range(0, 128, CHUNK):
                rr = slice(r, r + CHUNK)
                u = get(4, r)[0]
                v, vn, vs = get(5, r)
                c = coefs(u + roll(u, -1, 1), u + roll(u, 1, 1), v + vn, v + vs,
                          *(mw5[n, rr] for n in range(5)))
                for f in range(6):
                    x, xn, xs = get(f, r)
                    xe, xw = roll(x, -1, 1), roll(x, 1, 1)
                    y = apply(c, x, xe, xw, xn, xs)
                    if substep == 0:
                        mid[f, PAD + r : PAD + r + CHUNK] = y
                    else:
                        res[f, k, rr] = y
                        beside[f, k, rr] = jnp.where(lane < 64, xe, xw)
        return 0

    lax.fori_loop(0, 4, level, 0)
    for r in range(0, 128, CHUNK):
        acc = jnp.zeros((CHUNK, 128), F32)
        for g in range(NP):
            x = roll(beside[g // 4, g % 4, r : r + CHUNK], 4 * g + 2, 1)
            acc = jnp.where(lane // 4 == g, x, acc)
        ends[r : r + CHUNK] = acc


def spread_matrix():
    out = np.zeros((7, 128, 128), np.float32)
    for l in range(128):
        k, j = l // 4 % 4, l % 4
        u, v = 64 + 4 * k + j, 80 + 4 * k + j
        for n, src in enumerate((
            (u, u + 1), (u, u - 1), (v,), (4 * GE + j,),
            (4 * GS if j == 0 else 4 * GE + j - 1,), (4 * GN + j,), (4 * GM + j,),
        )):
            for i in src:
                out[n, i, l] = 1.0
    return np.concatenate(list(out), axis=1)


def spread(x, matrix):
    hi = x.astype(jnp.bfloat16)
    rest = x - hi.astype(F32)
    mid = rest.astype(jnp.bfloat16)
    lo = (rest - mid.astype(F32)).astype(jnp.bfloat16)
    dot = functools.partial(jnp.dot, preferred_element_type=F32)
    return dot(lo, matrix) + dot(mid, matrix) + dot(hi, matrix)


def outer_kernel(pack, got_west, got_east, north, south, inner, ends, matrix, out_hbm,
                 side, wide, halo, z, res, sem):
    top = lax.axis_index("lat") == lax.axis_size("lat") - 1
    west, east = got_west[...], got_east[...]
    west = jnp.concatenate([west, roll(west, -2, 1)], axis=0)
    east = jnp.concatenate([east, roll(east, 2, 1)], axis=0)
    own = pack[...]
    lane = lanes((128, 128))
    j = lane % 4
    span = 128 + 2 * PAD

    def fill(s, strip, above, below):
        side[s, PAD : PAD + 128] = strip
        side[s, 0:PAD] = jnp.broadcast_to(below, (PAD, 128))
        side[s, PAD + 128 : span] = jnp.broadcast_to(above, (PAD, 128))

    def widen(n):
        for s in range(2):
            wide[s, :, 0 : 128 * n] = spread(side[s], matrix[:, 0 : 128 * n])

    def update(s, r):
        def rep(n, d=0):
            return wide[s, PAD + r + d : PAD + r + d + CHUNK, 128 * n : 128 * n + 128]

        def at(d):
            return side[s, PAD + r + d : PAD + r + d + CHUNK]

        m, v, x = rep(6), rep(2), at(0)
        me, mw, mn, ms = m * rep(3), m * rep(4), m * rep(5), m * rep(5, -1)
        base = 1.0 - ((me + mw) + (mn + ms))
        c = coefs(rep(0), rep(1), v + rep(2, 1), v + rep(2, -1), me, mw, mn, ms, base)
        return apply(c, x, roll(x, -1, 1), roll(x, 1, 1), at(1), at(-1))

    j1 = lanes((1, 128)) % 4

    def as_row(turned, columns, shift):
        parts = [roll(turned[c : c + 1], shift + d, 1) for c, d in zip(columns, (-2, -1, 0, 1))]
        low = jnp.where(j1 == 0, parts[0], parts[1])
        return jnp.where(j1 < 2, low, jnp.where(j1 == 2, parts[2], parts[3]))

    three = jnp.where(lane < 112, roll(own, -8, 1), jnp.where(lane < 120, west, roll(east, 8, 1)))
    turned = three.T
    above, below = as_row(turned, range(104, 108), 0), as_row(turned, range(108, 112), 1)
    fill(0, jnp.where(j < 2, west, own),
         jnp.where(j1 == 1, roll(turned[113:114], -1, 1), above),
         jnp.where(j1 == 1, turned[117:118], below))
    fill(1, jnp.where(j < 2, own, east),
         jnp.where(j1 == 2, turned[122:123], above),
         jnp.where(j1 == 2, roll(turned[126:127], 1, 1), below))
    widen(7)

    packs = (west, east)
    low = lat_strip(south, packs, 11, 9, None)
    high = lat_strip(north, packs, 15, 13, top)
    ring = rows_of((8, 128)) % 4 == 2
    for t in range(12):
        halo[8 * t : 8 * t + 8] = jnp.where(ring, high[t], low[t])
    halo[96:128] = jnp.zeros((32, 128), F32)
    turned = halo[...].T
    outer = (126, 127, 0, 1)
    above, below = as_row(turned, outer, 0), as_row(turned, outer, 1)

    new = [[update(s, r) for r in range(0, 128, CHUNK)] for s in range(2)]
    edge = (j == 0) | (j == 3)
    for s in range(2):
        strip = jnp.where(edge, roll(ends[...], 1 - 2 * s, 1), jnp.concatenate(new[s], axis=0))
        fill(s, strip, above, below)
    widen(3)
    jj = lanes((CHUNK, 128)) % 4
    for r in range(0, 128, CHUNK):
        z[r : r + CHUNK] = jnp.where(jj < 2, update(1, r), update(0, r))

    outs = []
    outer = (lanes((CHUNK, 128)) < 2) | (lanes((CHUNK, 128)) >= 126)
    for k in range(4):
        for r in range(0, 128, CHUNK):
            rr = slice(r, r + CHUNK)
            zr = z[rr]
            for f in range(6):
                res[f, k, rr] = jnp.where(outer, roll(zr, -(4 * (4 * f + k) + 2), 1), inner[f, k, rr])
        c = pltpu.make_async_copy(res.at[:, k], out_hbm.at[:, k], sem.at[k])
        c.start()
        outs.append(c)
    for c in outs:
        c.wait()


def cost(nbytes, flops):
    return pl.CostEstimate(flops=flops, bytes_accessed=nbytes, transcendentals=0)


def smem():
    return pl.BlockSpec(memory_space=pltpu.SMEM)


def vmem():
    return pl.BlockSpec(memory_space=pltpu.VMEM)


def local(nlon, nlat, fields, weights, area, mask, land):
    shape = jax.ShapeDtypeStruct
    planes = fields.reshape(NP, 128, 128)
    params = pltpu.CompilerParams(vmem_limit_bytes=24 << 20)

    rows = shape((ROWS2, 128), F32)
    to_odd, to_even = pl.pallas_call(
        rows_kernel,
        out_shape=(rows, rows),
        in_specs=[pl.BlockSpec(memory_space=pltpu.HBM)] * 4 + [smem()],
        out_specs=(vmem(),) * 2,
        scratch_shapes=[
            pltpu.VMEM((2, NP, 8, 128), F32),
            pltpu.VMEM((2, 2, 8, 128), F32),
            pltpu.VMEM((2, 8, 128), F32),
            pltpu.VMEM((2, 8, 128), jnp.int32),
            pltpu.SemaphoreType.DMA((8,)),
        ],
        cost_estimate=cost(1 << 18, 1 << 16),
        name="rows",
    )(planes, weights, area, mask, land)

    axes = ("lon", "lat")
    with jax.named_scope("lat_odd"):
        got_odd = lax.ppermute(to_odd, axes, lat_pairs(nlon, nlat, True))
    with jax.named_scope("lat_even"):
        got_even = lax.ppermute(to_even, axes, lat_pairs(nlon, nlat, False))

    tile, half = shape((128, 128), F32), shape((64, 128), F32)
    pack = pl.pallas_call(
        columns_kernel,
        out_shape=tile,
        in_specs=[vmem()] * 4 + [smem()],
        out_specs=vmem(),
        compiler_params=params,
        cost_estimate=cost(2 << 20, 1 << 20),
        name="columns",
    )(planes, weights, area, mask, land)

    pack, to_east, to_west, north, south = pl.pallas_call(
        strips_kernel,
        out_shape=(tile, half, half, shape((ROWS4, 128), F32), shape((ROWS4, 128), F32)),
        in_specs=[vmem()] * 5,
        out_specs=(vmem(),) * 5,
        scratch_shapes=[pltpu.VMEM((4, ROWS2, 128), F32)],
        compiler_params=params,
        cost_estimate=cost(1 << 18, 1 << 18),
        name="strips",
    )(to_odd, to_even, got_odd, got_even, pack)

    with jax.named_scope("lon_east"):
        got_west = lax.ppermute(to_east, axes, lon_pairs(nlon, nlat, 1))

    padded = 128 + 2 * PAD
    state = shape((6, 4, 128, 128), F32)
    inputs = (fields, weights, area, mask, land, north, south)

    def inner_call(early, before):
        return pl.pallas_call(
            functools.partial(inner_kernel, early),
            out_shape=(state, tile),
            in_specs=[vmem()] * 4 + [smem()] + [vmem()] * (2 + len(before)),
            out_specs=(vmem(), vmem()),
            scratch_shapes=[
                pltpu.VMEM((6, padded, 128), F32),
                pltpu.VMEM((2, 96, 128), F32),
                pltpu.VMEM((5, 128, 128), F32),
                pltpu.VMEM((6, 4, 128, 128), F32),
            ],
            input_output_aliases={7: 0, 8: 1} if before else {},
            compiler_params=params,
            cost_estimate=cost(4 << 20, 20 << 20),
            name="inner_early" if early else "inner_late",
        )(*inputs, *before)

    inner, ends = inner_call(True, ())
    to_west, inner, ends = lax.optimization_barrier((to_west, inner, ends))
    with jax.named_scope("lon_west"):
        got_east = lax.ppermute(to_west, axes, lon_pairs(nlon, nlat, -1))
    inner, ends = inner_call(False, (inner, ends))

    return pl.pallas_call(
        outer_kernel,
        out_shape=state,
        in_specs=[vmem()] * 8,
        out_specs=pl.BlockSpec(memory_space=pltpu.HBM),
        scratch_shapes=[
            pltpu.VMEM((2, padded, 128), F32),
            pltpu.VMEM((2, padded, 7 * 128), F32),
            pltpu.VMEM((128, 128), F32),
            pltpu.VMEM((128, 128), F32),
            pltpu.VMEM((6, 4, 128, 128), F32),
            pltpu.SemaphoreType.DMA((4,)),
        ],
        compiler_params=params,
        cost_estimate=cost(4 << 20, 1 << 20),
        name="outer",
    )(pack, got_west, got_east, north, south, inner, ends, jnp.asarray(spread_matrix(), jnp.bfloat16))


def solution(mesh):
    in_specs = (
        P(None, None, "lat", "lon"),
        P(None, "lat", "lon"),
        P("lat", "lon"),
        P("lat", "lon"),
        P("lat", "lon"),
    )
    body = functools.partial(local, mesh.shape["lon"], mesh.shape["lat"])
    return jax.shard_map(
        body, mesh=mesh, in_specs=in_specs, out_specs=P(None, None, "lat", "lon"), check_vma=False
    )
```

```python
import functools

import jax
import jax.numpy as jnp
import numpy as np
from jax import lax
from jax.experimental import pallas as pl
from jax.experimental.pallas import tpu as pltpu
from jax.sharding import PartitionSpec as P

F32 = jnp.float32
TIME_STEP = 0.1
NP = 24
GE, GN, GM, GS = 24, 25, 26, 27
ROWS2, ROWS4 = 56, 112
PAD = 8
CHUNK = 32
HIGH = lax.Precision.HIGHEST


def lon_pairs(nlon, nlat, step):
    return [(i * nlat + l, (i + step) % nlon * nlat + l) for i in range(nlon) for l in range(nlat)]


def lat_pairs(nlon, nlat, odd):
    pairs = []
    for i in range(nlon):
        for l in range(nlat):
            if not odd:
                pairs.append((i * nlat + l, i * nlat + (l ^ 1)))
            elif l == nlat - 1:
                pairs.append((i * nlat + l, (nlon - 1 - i) * nlat + l))
            elif l > 0:
                pairs.append((i * nlat + l, i * nlat + (l + 1 if l % 2 else l - 1)))
    return pairs


def lanes(shape):
    return lax.broadcasted_iota(jnp.int32, shape, 1)


def rows_of(shape):
    return lax.broadcasted_iota(jnp.int32, shape, 0)


def roll(x, shift, axis):
    n = x.shape[axis]
    shift %= n
    return x if shift == 0 else pltpu.roll(x, shift, axis)


def step_factor(area, mask, sea):
    return TIME_STEP * (mask.astype(F32) * sea) * area


def coefs(se, sw, sn, ss, me, mw, mn, ms, base):
    te, tw, tn, ts = me * (0.125 * se), mw * (0.125 * sw), mn * (0.125 * sn), ms * (0.125 * ss)
    return me - te, mw + tw, mn - tn, ms + ts, base + ((tw - te) + (ts - tn))


def apply(c, x, xe, xw, xn, xs):
    ce, cw, cn, cs, cc = c
    return cc * x + ((ce * xe + cw * xw) + (cn * xn + cs * xs))


def rows_kernel(f, w, area, mask, land, to_odd, to_even, fb, wb, ab, kb, sem):
    copies = []
    for n, (src, dst) in enumerate(((f, fb), (w, wb), (area, ab), (mask, kb))):
        for h in range(2):
            rows = pl.ds(120 * h, 8)
            part = src.at[:, rows] if len(src.shape) == 3 else src.at[rows]
            copies.append(pltpu.make_async_copy(part, dst.at[h], sem.at[2 * n + h]))
    for c in copies:
        c.start()
    odd = lax.axis_index("lat") % 2 == 1
    for c in copies:
        c.wait()
    is_sea = (1 - land[0, 0]).astype(F32)
    m_lo = step_factor(ab[0, 0:2], kb[0, 0:2], is_sea)
    m_hi = step_factor(ab[1, 6:8], kb[1, 6:8], is_sea)
    zero = jnp.zeros((2, 128), F32)
    for g in range(28):
        if g < NP:
            south, north = fb[0, g, 0:2], fb[1, g, 6:8]
        elif g < GM:
            south, north = wb[0, g - NP, 0:2], wb[1, g - NP, 6:8]
        elif g == GM:
            south, north = m_lo, m_hi
        else:
            south, north = zero, zero
        to_odd[2 * g : 2 * g + 2] = jnp.where(odd, north, south)
        to_even[2 * g : 2 * g + 2] = jnp.where(odd, south, north)


def columns_kernel(f, w, area, mask, land, out):
    sea = (1 - land[0, 0]).astype(F32)
    for r in range(0, 128, CHUNK):
        rr = slice(r, r + CHUNK)
        group = lanes((CHUNK, 128)) // 4
        acc = jnp.zeros((CHUNK, 128), F32)
        for g in range(28):
            if g < NP:
                x = f[g, rr]
            elif g < GM:
                x = w[g - NP, rr]
            elif g == GM:
                x = step_factor(area[rr], mask[rr], sea)
            else:
                x = w[0, rr]
            acc = jnp.where(group == g, roll(x, 4 * g + 2 + (g == GS), 1), acc)
        out[rr] = acc


def strips_kernel(to_odd, to_even, got_odd, got_even, pack, out, to_east, to_west, north, south, recv):
    odd = lax.axis_index("lat") % 2 == 1
    top = lax.axis_index("lat") == lax.axis_size("lat") - 1
    raw = jnp.where(odd, got_odd[...], got_even[...])
    row = rows_of((ROWS2, 128))
    flip = (rows_of((128, 128)) + lanes((128, 128)) == 127).astype(F32)
    mirrored = jnp.dot(raw, flip, precision=HIGH, preferred_element_type=F32)
    mirrored = jnp.where((row >= 32) & (row < 48), -mirrored, mirrored)
    mirrored = jnp.where(row % 2 == 0, roll(mirrored, -1, 0), roll(mirrored, 1, 0))
    recv[0] = jnp.where(top, mirrored, raw)
    recv[1] = jnp.where(odd, got_even[...], got_odd[...])
    recv[2] = jnp.where(odd, to_odd[...], to_even[...])
    recv[3] = jnp.where(odd, to_even[...], to_odd[...])
    for g in range(28):
        two = slice(2 * g, 2 * g + 2)
        north[4 * g : 4 * g + 2] = recv[2, two]
        north[4 * g + 2 : 4 * g + 4] = recv[0, two]
        south[4 * g : 4 * g + 2] = recv[1, two]
        south[4 * g + 2 : 4 * g + 4] = recv[3, two]
    a, b = recv[0, 2 * GN : 2 * GN + 1], recv[0, 2 * GN + 1 : 2 * GN + 2]
    north[4 * GN + 2 : 4 * GN + 3] = jnp.where(top, b, a)
    north[4 * GS + 2 : 4 * GS + 3] = jnp.where(top, a, recv[2, 2 * GN + 1 : 2 * GN + 2])
    south[4 * GS + 1 : 4 * GS + 2] = recv[1, 2 * GN : 2 * GN + 1]
    lane = lanes((ROWS4, 128))
    acc = jnp.where(lane // 4 == 28, roll(north[...], 114, 1), pack[0:ROWS4])
    out[0:ROWS4] = jnp.where(lane // 4 == 29, roll(south[...], 118, 1), acc)
    out[ROWS4:128] = pack[ROWS4:128]
    j = lanes((64, 128)) % 4
    a, b = out[0:64], out[64:128]
    to_east[...] = jnp.where(j < 2, a, roll(b, 2, 1))
    to_west[...] = jnp.where(j < 2, roll(b, -2, 1), a)


def repeat_half(v, half):
    low = rows_of(v.shape) < 4
    other = roll(v, 4, 0)
    return jnp.where(low, v, other) if half == 0 else jnp.where(low, other, v)


def lat_strip(strip, ends, shift_w, shift_e, top):
    lane = lanes((8, 128))
    if ends is not None:
        west = roll(ends[0][0:ROWS4], shift_w, 1)
        east = roll(ends[1][0:ROWS4], shift_e, 1)

    def tile(t):
        x = strip[8 * t : 8 * t + 8]
        xe, xw = roll(x, -1, 1), roll(x, 1, 1)
        if ends is not None:
            xe = jnp.where(lane == 127, east[8 * t : 8 * t + 8], xe)
            xw = jnp.where(lane == 0, west[8 * t : 8 * t + 8], xw)
        return x, xe, xw

    x12, e12, w12 = tile(12)
    x13 = strip[104:112]
    here, right, left = (repeat_half(a, 0) for a in (x12, e12, w12))
    we = here if top is None else jnp.where(top, right, here)
    ww = left if top is None else jnp.where(top, here, left)
    m = repeat_half(x13, 0)
    me, mw = m * we, m * ww
    mn, ms = m * repeat_half(x12, 1), m * repeat_half(x13, 1)
    base = 1.0 - ((me + mw) + (mn + ms))
    c = []
    for t in range(2):
        u, ue, uw = tile(8 + t)
        v = strip[8 * (10 + t) : 8 * (10 + t) + 8]
        c.append(coefs(u + ue, u + uw, v + roll(v, -1, 0), v + roll(v, 1, 0), me, mw, mn, ms, base))
    out = []
    for t in range(12):
        x, xe, xw = tile(t)
        out.append(apply(c[t % 2], x, xe, xw, roll(x, -1, 0), roll(x, 1, 0)))
    return out


def runs_early():
    first = lax.axis_index("lon") % (lax.axis_size("lon") // 2) == 0
    return first & (lax.axis_index("lat") < lax.axis_size("lat") - 2)


def inner_kernel(early, fields, w, area, mask, land, north, south, *refs):
    @pl.when(runs_early() if early else jnp.logical_not(runs_early()))
    def _():
        inner_steps(fields, w, area, mask, land, north, south, *refs)


def inner_steps(fields, w, area, mask, land, north, south, res, ends, mid, halo, mw5, beside):
    top = lax.axis_index("lat") == lax.axis_size("lat") - 1
    for s, tiles in enumerate(
        (lat_strip(south, None, 0, 0, None), lat_strip(north, None, 0, 0, top))
    ):
        for t in range(12):
            halo[s, 8 * t : 8 * t + 8] = tiles[t]

    m = step_factor(area[...], mask[...], (1 - land[0, 0]).astype(F32))
    we, wn = w[0], w[1]
    first = rows_of((128, 128)) == 0
    ws = jnp.where(first, south[4 * GN + 1 : 4 * GN + 2], roll(wn, 1, 0))
    me, mw, mn, ms = m * we, m * roll(we, 1, 1), m * wn, m * ws
    for n, x in enumerate((me, mw, mn, ms, 1.0 - ((me + mw) + (mn + ms)))):
        mw5[n] = x
    lane = lanes((CHUNK, 128))
    row = rows_of((CHUNK, 128))

    def level(k, _):
        def first_get(f, r):
            g = 4 * (4 * f + k)
            x = fields[f, k, r : r + CHUNK]
            if r == 0:
                s = jnp.where(row == 0, south[pl.ds(g + 1, 1)], roll(x, 1, 0))
            else:
                s = fields[f, k, r - 1 : r - 1 + CHUNK]
            if r == 128 - CHUNK:
                n = jnp.where(row == CHUNK - 1, north[pl.ds(g + 2, 1)], roll(x, -1, 0))
            else:
                n = fields[f, k, r + 1 : r + 1 + CHUNK]
            return x, n, s

        def second_get(f, r):
            return tuple(mid[f, PAD + r + d : PAD + r + d + CHUNK] for d in (0, 1, -1))

        for f in range(6):
            g = 4 * (4 * f + k)
            mid[f, PAD - 1 : PAD] = halo[0, pl.ds(g + 1, 1)]
            mid[f, PAD + 128 : PAD + 129] = halo[1, pl.ds(g + 2, 1)]
        for substep, get in enumerate((first_get, second_get)):
            for r in range(0, 128, CHUNK):
                rr = slice(r, r + CHUNK)
                u = get(4, r)[0]
                v, vn, vs = get(5, r)
                c = coefs(u + roll(u, -1, 1), u + roll(u, 1, 1), v + vn, v + vs,
                          *(mw5[n, rr] for n in range(5)))
                for f in range(6):
                    x, xn, xs = get(f, r)
                    xe, xw = roll(x, -1, 1), roll(x, 1, 1)
                    y = apply(c, x, xe, xw, xn, xs)
                    if substep == 0:
                        mid[f, PAD + r : PAD + r + CHUNK] = y
                    else:
                        res[f, k, rr] = y
                        beside[f, k, rr] = jnp.where(lane < 64, xe, xw)
        return 0

    lax.fori_loop(0, 4, level, 0)
    for r in range(0, 128, CHUNK):
        acc = jnp.zeros((CHUNK, 128), F32)
        for g in range(NP):
            x = roll(beside[g // 4, g % 4, r : r + CHUNK], 4 * g + 2, 1)
            acc = jnp.where(lane // 4 == g, x, acc)
        ends[r : r + CHUNK] = acc


def spread_matrix():
    out = np.zeros((7, 128, 128), np.float32)
    for l in range(128):
        k, j = l // 4 % 4, l % 4
        u, v = 64 + 4 * k + j, 80 + 4 * k + j
        for n, src in enumerate((
            (u, u + 1), (u, u - 1), (v,), (4 * GE + j,),
            (4 * GS if j == 0 else 4 * GE + j - 1,), (4 * GN + j,), (4 * GM + j,),
        )):
            for i in src:
                out[n, i, l] = 1.0
    return np.concatenate(list(out), axis=1)


def spread(x, matrix):
    hi = x.astype(jnp.bfloat16)
    rest = x - hi.astype(F32)
    mid = rest.astype(jnp.bfloat16)
    lo = (rest - mid.astype(F32)).astype(jnp.bfloat16)
    dot = functools.partial(jnp.dot, preferred_element_type=F32)
    return dot(lo, matrix) + dot(mid, matrix) + dot(hi, matrix)


def outer_kernel(pack, got_west, got_east, north, south, inner_a, inner_b, ends_a, ends_b, matrix, out_hbm,
                 side, wide, halo, z, res, sem):
    top = lax.axis_index("lat") == lax.axis_size("lat") - 1
    west, east = got_west[...], got_east[...]
    west = jnp.concatenate([west, roll(west, -2, 1)], axis=0)
    east = jnp.concatenate([east, roll(east, 2, 1)], axis=0)
    own = pack[...]
    early = runs_early()
    ends = jnp.where(early, ends_a[...], ends_b[...])
    lane = lanes((128, 128))
    j = lane % 4
    span = 128 + 2 * PAD

    def fill(s, strip, above, below):
        side[s, PAD : PAD + 128] = strip
        side[s, 0:PAD] = jnp.broadcast_to(below, (PAD, 128))
        side[s, PAD + 128 : span] = jnp.broadcast_to(above, (PAD, 128))

    def widen(n):
        for s in range(2):
            wide[s, :, 0 : 128 * n] = spread(side[s], matrix[:, 0 : 128 * n])

    def update(s, r):
        def rep(n, d=0):
            return wide[s, PAD + r + d : PAD + r + d + CHUNK, 128 * n : 128 * n + 128]

        def at(d):
            return side[s, PAD + r + d : PAD + r + d + CHUNK]

        m, v, x = rep(6), rep(2), at(0)
        me, mw, mn, ms = m * rep(3), m * rep(4), m * rep(5), m * rep(5, -1)
        base = 1.0 - ((me + mw) + (mn + ms))
        c = coefs(rep(0), rep(1), v + rep(2, 1), v + rep(2, -1), me, mw, mn, ms, base)
        return apply(c, x, roll(x, -1, 1), roll(x, 1, 1), at(1), at(-1))

    j1 = lanes((1, 128)) % 4

    def as_row(turned, columns, shift):
        parts = [roll(turned[c : c + 1], shift + d, 1) for c, d in zip(columns, (-2, -1, 0, 1))]
        low = jnp.where(j1 == 0, parts[0], parts[1])
        return jnp.where(j1 < 2, low, jnp.where(j1 == 2, parts[2], parts[3]))

    three = jnp.where(lane < 112, roll(own, -8, 1), jnp.where(lane < 120, west, roll(east, 8, 1)))
    turned = three.T
    above, below = as_row(turned, range(104, 108), 0), as_row(turned, range(108, 112), 1)
    fill(0, jnp.where(j < 2, west, own),
         jnp.where(j1 == 1, roll(turned[113:114], -1, 1), above),
         jnp.where(j1 == 1, turned[117:118], below))
    fill(1, jnp.where(j < 2, own, east),
         jnp.where(j1 == 2, turned[122:123], above),
         jnp.where(j1 == 2, roll(turned[126:127], 1, 1), below))
    widen(7)

    packs = (west, east)
    low = lat_strip(south, packs, 11, 9, None)
    high = lat_strip(north, packs, 15, 13, top)
    ring = rows_of((8, 128)) % 4 == 2
    for t in range(12):
        halo[8 * t : 8 * t + 8] = jnp.where(ring, high[t], low[t])
    halo[96:128] = jnp.zeros((32, 128), F32)
    turned = halo[...].T
    outer = (126, 127, 0, 1)
    above, below = as_row(turned, outer, 0), as_row(turned, outer, 1)

    new = [[update(s, r) for r in range(0, 128, CHUNK)] for s in range(2)]
    edge = (j == 0) | (j == 3)
    for s in range(2):
        strip = jnp.where(edge, roll(ends, 1 - 2 * s, 1), jnp.concatenate(new[s], axis=0))
        fill(s, strip, above, below)
    widen(3)
    jj = lanes((CHUNK, 128)) % 4
    for r in range(0, 128, CHUNK):
        z[r : r + CHUNK] = jnp.where(jj < 2, update(1, r), update(0, r))

    outs = []
    outer = (lanes((CHUNK, 128)) < 2) | (lanes((CHUNK, 128)) >= 126)
    for k in range(4):
        for r in range(0, 128, CHUNK):
            rr = slice(r, r + CHUNK)
            zr = z[rr]
            for f in range(6):
                x = jnp.where(early, inner_a[f, k, rr], inner_b[f, k, rr])
                res[f, k, rr] = jnp.where(outer, roll(zr, -(4 * (4 * f + k) + 2), 1), x)
        c = pltpu.make_async_copy(res.at[:, k], out_hbm.at[:, k], sem.at[k])
        c.start()
        outs.append(c)
    for c in outs:
        c.wait()


def cost(nbytes, flops):
    return pl.CostEstimate(flops=flops, bytes_accessed=nbytes, transcendentals=0)


def smem():
    return pl.BlockSpec(memory_space=pltpu.SMEM)


def vmem():
    return pl.BlockSpec(memory_space=pltpu.VMEM)


def local(nlon, nlat, fields, weights, area, mask, land):
    shape = jax.ShapeDtypeStruct
    planes = fields.reshape(NP, 128, 128)
    params = pltpu.CompilerParams(vmem_limit_bytes=24 << 20)

    rows = shape((ROWS2, 128), F32)
    to_odd, to_even = pl.pallas_call(
        rows_kernel,
        out_shape=(rows, rows),
        in_specs=[pl.BlockSpec(memory_space=pltpu.HBM)] * 4 + [smem()],
        out_specs=(vmem(),) * 2,
        scratch_shapes=[
            pltpu.VMEM((2, NP, 8, 128), F32),
            pltpu.VMEM((2, 2, 8, 128), F32),
            pltpu.VMEM((2, 8, 128), F32),
            pltpu.VMEM((2, 8, 128), jnp.int32),
            pltpu.SemaphoreType.DMA((8,)),
        ],
        cost_estimate=cost(1 << 18, 1 << 16),
        name="rows",
    )(planes, weights, area, mask, land)

    axes = ("lon", "lat")
    with jax.named_scope("lat_odd"):
        got_odd = lax.ppermute(to_odd, axes, lat_pairs(nlon, nlat, True))
    with jax.named_scope("lat_even"):
        got_even = lax.ppermute(to_even, axes, lat_pairs(nlon, nlat, False))

    tile, half = shape((128, 128), F32), shape((64, 128), F32)
    pack = pl.pallas_call(
        columns_kernel,
        out_shape=tile,
        in_specs=[vmem()] * 4 + [smem()],
        out_specs=vmem(),
        compiler_params=params,
        cost_estimate=cost(2 << 20, 1 << 20),
        name="columns",
    )(planes, weights, area, mask, land)

    pack, to_east, to_west, north, south = pl.pallas_call(
        strips_kernel,
        out_shape=(tile, half, half, shape((ROWS4, 128), F32), shape((ROWS4, 128), F32)),
        in_specs=[vmem()] * 5,
        out_specs=(vmem(),) * 5,
        scratch_shapes=[pltpu.VMEM((4, ROWS2, 128), F32)],
        compiler_params=params,
        cost_estimate=cost(1 << 18, 1 << 18),
        name="strips",
    )(to_odd, to_even, got_odd, got_even, pack)

    with jax.named_scope("lon_east"):
        got_west = lax.ppermute(to_east, axes, lon_pairs(nlon, nlat, 1))

    padded = 128 + 2 * PAD
    state = shape((6, 4, 128, 128), F32)
    inputs = (fields, weights, area, mask, land, north, south)

    def inner_call(early):
        return pl.pallas_call(
            functools.partial(inner_kernel, early),
            out_shape=(state, tile),
            in_specs=[vmem()] * 4 + [smem()] + [vmem()] * 2,
            out_specs=(vmem(), vmem()),
            scratch_shapes=[
                pltpu.VMEM((6, padded, 128), F32),
                pltpu.VMEM((2, 96, 128), F32),
                pltpu.VMEM((5, 128, 128), F32),
                pltpu.VMEM((6, 4, 128, 128), F32),
            ],
            compiler_params=params,
            cost_estimate=cost(4 << 20, 20 << 20),
            name="inner_early" if early else "inner_late",
        )(*inputs)

    inner_a, ends_a = inner_call(True)
    to_west, inner_a, ends_a = lax.optimization_barrier((to_west, inner_a, ends_a))
    with jax.named_scope("lon_west"):
        got_east = lax.ppermute(to_west, axes, lon_pairs(nlon, nlat, -1))
    inner_b, ends_b = inner_call(False)

    return pl.pallas_call(
        outer_kernel,
        out_shape=state,
        in_specs=[vmem()] * 10,
        out_specs=pl.BlockSpec(memory_space=pltpu.HBM),
        scratch_shapes=[
            pltpu.VMEM((2, padded, 128), F32),
            pltpu.VMEM((2, padded, 7 * 128), F32),
            pltpu.VMEM((128, 128), F32),
            pltpu.VMEM((128, 128), F32),
            pltpu.VMEM((6, 4, 128, 128), F32),
            pltpu.SemaphoreType.DMA((4,)),
        ],
        compiler_params=params,
        cost_estimate=cost(4 << 20, 1 << 20),
        name="outer",
    )(pack, got_west, got_east, north, south, inner_a, inner_b, ends_a, ends_b, jnp.asarray(spread_matrix(), jnp.bfloat16))


def solution(mesh):
    in_specs = (
        P(None, None, "lat", "lon"),
        P(None, "lat", "lon"),
        P("lat", "lon"),
        P("lat", "lon"),
        P("lat", "lon"),
    )
    body = functools.partial(local, mesh.shape["lon"], mesh.shape["lat"])
    return jax.shard_map(
        body, mesh=mesh, in_specs=in_specs, out_specs=P(None, None, "lat", "lon"), check_vma=False
    )
```

```python
import functools

import jax
import jax.numpy as jnp
import numpy as np
from jax import lax
from jax.experimental import pallas as pl
from jax.experimental.pallas import tpu as pltpu
from jax.sharding import PartitionSpec as P

F32 = jnp.float32
TIME_STEP = 0.1
NP = 24
GE, GN, GM, GS = 24, 25, 26, 27
ROWS2, ROWS4 = 56, 112
PAD = 8
CHUNK = 32
HIGH = lax.Precision.HIGHEST


def lon_pairs(nlon, nlat, step):
    return [(i * nlat + l, (i + step) % nlon * nlat + l) for i in range(nlon) for l in range(nlat)]


def lat_pairs(nlon, nlat, odd):
    pairs = []
    for i in range(nlon):
        for l in range(nlat):
            if not odd:
                pairs.append((i * nlat + l, i * nlat + (l ^ 1)))
            elif l == nlat - 1:
                pairs.append((i * nlat + l, (nlon - 1 - i) * nlat + l))
            elif l > 0:
                pairs.append((i * nlat + l, i * nlat + (l + 1 if l % 2 else l - 1)))
    return pairs


def lanes(shape):
    return lax.broadcasted_iota(jnp.int32, shape, 1)


def rows_of(shape):
    return lax.broadcasted_iota(jnp.int32, shape, 0)


def roll(x, shift, axis):
    n = x.shape[axis]
    shift %= n
    return x if shift == 0 else pltpu.roll(x, shift, axis)


def step_factor(area, mask, sea):
    return TIME_STEP * (mask.astype(F32) * sea) * area


def coefs(se, sw, sn, ss, me, mw, mn, ms, base):
    te, tw, tn, ts = me * (0.125 * se), mw * (0.125 * sw), mn * (0.125 * sn), ms * (0.125 * ss)
    return me - te, mw + tw, mn - tn, ms + ts, base + ((tw - te) + (ts - tn))


def apply(c, x, xe, xw, xn, xs):
    ce, cw, cn, cs, cc = c
    return cc * x + ((ce * xe + cw * xw) + (cn * xn + cs * xs))


def rows_kernel(f, w, area, mask, land, to_odd, to_even, fb, wb, ab, kb, sem):
    copies = []
    for n, (src, dst) in enumerate(((f, fb), (w, wb), (area, ab), (mask, kb))):
        for h in range(2):
            rows = pl.ds(120 * h, 8)
            part = src.at[:, rows] if len(src.shape) == 3 else src.at[rows]
            copies.append(pltpu.make_async_copy(part, dst.at[h], sem.at[2 * n + h]))
    for c in copies:
        c.start()
    odd = lax.axis_index("lat") % 2 == 1
    for c in copies:
        c.wait()
    is_sea = (1 - land[0, 0]).astype(F32)
    m_lo = step_factor(ab[0, 0:2], kb[0, 0:2], is_sea)
    m_hi = step_factor(ab[1, 6:8], kb[1, 6:8], is_sea)
    zero = jnp.zeros((2, 128), F32)
    for g in range(28):
        if g < NP:
            south, north = fb[0, g, 0:2], fb[1, g, 6:8]
        elif g < GM:
            south, north = wb[0, g - NP, 0:2], wb[1, g - NP, 6:8]
        elif g == GM:
            south, north = m_lo, m_hi
        else:
            south, north = zero, zero
        to_odd[2 * g : 2 * g + 2] = jnp.where(odd, north, south)
        to_even[2 * g : 2 * g + 2] = jnp.where(odd, south, north)


def columns_kernel(f, w, area, mask, land, out):
    sea = (1 - land[0, 0]).astype(F32)
    for r in range(0, 128, CHUNK):
        rr = slice(r, r + CHUNK)
        group = lanes((CHUNK, 128)) // 4
        acc = jnp.zeros((CHUNK, 128), F32)
        for g in range(28):
            if g < NP:
                x = f[g, rr]
            elif g < GM:
                x = w[g - NP, rr]
            elif g == GM:
                x = step_factor(area[rr], mask[rr], sea)
            else:
                x = w[0, rr]
            acc = jnp.where(group == g, roll(x, 4 * g + 2 + (g == GS), 1), acc)
        out[rr] = acc


def strips_kernel(to_odd, to_even, got_odd, got_even, pack, out, to_east, to_west, north, south, recv):
    odd = lax.axis_index("lat") % 2 == 1
    top = lax.axis_index("lat") == lax.axis_size("lat") - 1
    raw = jnp.where(odd, got_odd[...], got_even[...])
    row = rows_of((ROWS2, 128))
    flip = (rows_of((128, 128)) + lanes((128, 128)) == 127).astype(F32)
    mirrored = jnp.dot(raw, flip, precision=HIGH, preferred_element_type=F32)
    mirrored = jnp.where((row >= 32) & (row < 48), -mirrored, mirrored)
    mirrored = jnp.where(row % 2 == 0, roll(mirrored, -1, 0), roll(mirrored, 1, 0))
    recv[0] = jnp.where(top, mirrored, raw)
    recv[1] = jnp.where(odd, got_even[...], got_odd[...])
    recv[2] = jnp.where(odd, to_odd[...], to_even[...])
    recv[3] = jnp.where(odd, to_even[...], to_odd[...])
    for g in range(28):
        two = slice(2 * g, 2 * g + 2)
        north[4 * g : 4 * g + 2] = recv[2, two]
        north[4 * g + 2 : 4 * g + 4] = recv[0, two]
        south[4 * g : 4 * g + 2] = recv[1, two]
        south[4 * g + 2 : 4 * g + 4] = recv[3, two]
    a, b = recv[0, 2 * GN : 2 * GN + 1], recv[0, 2 * GN + 1 : 2 * GN + 2]
    north[4 * GN + 2 : 4 * GN + 3] = jnp.where(top, b, a)
    north[4 * GS + 2 : 4 * GS + 3] = jnp.where(top, a, recv[2, 2 * GN + 1 : 2 * GN + 2])
    south[4 * GS + 1 : 4 * GS + 2] = recv[1, 2 * GN : 2 * GN + 1]
    lane = lanes((ROWS4, 128))
    acc = jnp.where(lane // 4 == 28, roll(north[...], 114, 1), pack[0:ROWS4])
    out[0:ROWS4] = jnp.where(lane // 4 == 29, roll(south[...], 118, 1), acc)
    out[ROWS4:128] = pack[ROWS4:128]
    j = lanes((64, 128)) % 4
    a, b = out[0:64], out[64:128]
    to_east[...] = jnp.where(j < 2, a, roll(b, 2, 1))
    to_west[...] = jnp.where(j < 2, roll(b, -2, 1), a)


def repeat_half(v, half):
    low = rows_of(v.shape) < 4
    other = roll(v, 4, 0)
    return jnp.where(low, v, other) if half == 0 else jnp.where(low, other, v)


def lat_strip(strip, ends, shift_w, shift_e, top):
    lane = lanes((8, 128))
    if ends is not None:
        west = roll(ends[0][0:ROWS4], shift_w, 1)
        east = roll(ends[1][0:ROWS4], shift_e, 1)

    def tile(t):
        x = strip[8 * t : 8 * t + 8]
        xe, xw = roll(x, -1, 1), roll(x, 1, 1)
        if ends is not None:
            xe = jnp.where(lane == 127, east[8 * t : 8 * t + 8], xe)
            xw = jnp.where(lane == 0, west[8 * t : 8 * t + 8], xw)
        return x, xe, xw

    x12, e12, w12 = tile(12)
    x13 = strip[104:112]
    here, right, left = (repeat_half(a, 0) for a in (x12, e12, w12))
    we = here if top is None else jnp.where(top, right, here)
    ww = left if top is None else jnp.where(top, here, left)
    m = repeat_half(x13, 0)
    me, mw = m * we, m * ww
    mn, ms = m * repeat_half(x12, 1), m * repeat_half(x13, 1)
    base = 1.0 - ((me + mw) + (mn + ms))
    c = []
    for t in range(2):
        u, ue, uw = tile(8 + t)
        v = strip[8 * (10 + t) : 8 * (10 + t) + 8]
        c.append(coefs(u + ue, u + uw, v + roll(v, -1, 0), v + roll(v, 1, 0), me, mw, mn, ms, base))
    out = []
    for t in range(12):
        x, xe, xw = tile(t)
        out.append(apply(c[t % 2], x, xe, xw, roll(x, -1, 0), roll(x, 1, 0)))
    return out


def runs_early():
    return lax.axis_index("lon") % (lax.axis_size("lon") // 2) == 0


def inner_kernel(early, fields, w, area, mask, land, north, south, *refs):
    @pl.when(runs_early() if early else jnp.logical_not(runs_early()))
    def _():
        inner_steps(fields, w, area, mask, land, north, south, *refs)


def inner_steps(fields, w, area, mask, land, north, south, res, ends, mid, halo, mw5, beside):
    top = lax.axis_index("lat") == lax.axis_size("lat") - 1
    for s, tiles in enumerate(
        (lat_strip(south, None, 0, 0, None), lat_strip(north, None, 0, 0, top))
    ):
        for t in range(12):
            halo[s, 8 * t : 8 * t + 8] = tiles[t]

    m = step_factor(area[...], mask[...], (1 - land[0, 0]).astype(F32))
    we, wn = w[0], w[1]
    first = rows_of((128, 128)) == 0
    ws = jnp.where(first, south[4 * GN + 1 : 4 * GN + 2], roll(wn, 1, 0))
    me, mw, mn, ms = m * we, m * roll(we, 1, 1), m * wn, m * ws
    for n, x in enumerate((me, mw, mn, ms, 1.0 - ((me + mw) + (mn + ms)))):
        mw5[n] = x
    lane = lanes((CHUNK, 128))
    row = rows_of((CHUNK, 128))

    def level(k, _):
        def first_get(f, r):
            g = 4 * (4 * f + k)
            x = fields[f, k, r : r + CHUNK]
            if r == 0:
                s = jnp.where(row == 0, south[pl.ds(g + 1, 1)], roll(x, 1, 0))
            else:
                s = fields[f, k, r - 1 : r - 1 + CHUNK]
            if r == 128 - CHUNK:
                n = jnp.where(row == CHUNK - 1, north[pl.ds(g + 2, 1)], roll(x, -1, 0))
            else:
                n = fields[f, k, r + 1 : r + 1 + CHUNK]
            return x, n, s

        def second_get(f, r):
            return tuple(mid[f, PAD + r + d : PAD + r + d + CHUNK] for d in (0, 1, -1))

        for f in range(6):
            g = 4 * (4 * f + k)
            mid[f, PAD - 1 : PAD] = halo[0, pl.ds(g + 1, 1)]
            mid[f, PAD + 128 : PAD + 129] = halo[1, pl.ds(g + 2, 1)]
        for substep, get in enumerate((first_get, second_get)):
            for r in range(0, 128, CHUNK):
                rr = slice(r, r + CHUNK)
                u = get(4, r)[0]
                v, vn, vs = get(5, r)
                c = coefs(u + roll(u, -1, 1), u + roll(u, 1, 1), v + vn, v + vs,
                          *(mw5[n, rr] for n in range(5)))
                for f in range(6):
                    x, xn, xs = get(f, r)
                    xe, xw = roll(x, -1, 1), roll(x, 1, 1)
                    y = apply(c, x, xe, xw, xn, xs)
                    if substep == 0:
                        mid[f, PAD + r : PAD + r + CHUNK] = y
                    else:
                        res[f, k, rr] = y
                        beside[f, k, rr] = jnp.where(lane < 64, xe, xw)
        return 0

    lax.fori_loop(0, 4, level, 0)
    for r in range(0, 128, CHUNK):
        acc = jnp.zeros((CHUNK, 128), F32)
        for g in range(NP):
            x = roll(beside[g // 4, g % 4, r : r + CHUNK], 4 * g + 2, 1)
            acc = jnp.where(lane // 4 == g, x, acc)
        ends[r : r + CHUNK] = acc


def spread_matrix():
    out = np.zeros((7, 128, 128), np.float32)
    for l in range(128):
        k, j = l // 4 % 4, l % 4
        u, v = 64 + 4 * k + j, 80 + 4 * k + j
        for n, src in enumerate((
            (u, u + 1), (u, u - 1), (v,), (4 * GE + j,),
            (4 * GS if j == 0 else 4 * GE + j - 1,), (4 * GN + j,), (4 * GM + j,),
        )):
            for i in src:
                out[n, i, l] = 1.0
    return np.tile(np.concatenate(list(out), axis=1), (2, 1))


def spread(x, matrix):
    hi = x.astype(jnp.bfloat16)
    rest = x - hi.astype(F32)
    mid = rest.astype(jnp.bfloat16)
    lo = (rest - mid.astype(F32)).astype(jnp.bfloat16)
    dot = functools.partial(jnp.dot, preferred_element_type=F32)
    return dot(lo, matrix[0:128]) + dot(jnp.concatenate([hi, mid], axis=1), matrix)


def outer_kernel(pack, got_west, got_east, north, south, inner_a, inner_b, ends_a, ends_b, matrix, out_hbm,
                 side, wide, halo, z, res, sem):
    top = lax.axis_index("lat") == lax.axis_size("lat") - 1
    west, east = got_west[...], got_east[...]
    west = jnp.concatenate([west, roll(west, -2, 1)], axis=0)
    east = jnp.concatenate([east, roll(east, 2, 1)], axis=0)
    own = pack[...]
    early = runs_early()
    ends = jnp.where(early, ends_a[...], ends_b[...])
    lane = lanes((128, 128))
    j = lane % 4
    span = 128 + 2 * PAD

    def fill(s, strip, above, below):
        side[s, PAD : PAD + 128] = strip
        side[s, 0:PAD] = jnp.broadcast_to(below, (PAD, 128))
        side[s, PAD + 128 : span] = jnp.broadcast_to(above, (PAD, 128))

    def widen(n):
        for s in range(2):
            wide[s, :, 0 : 128 * n] = spread(side[s], matrix[:, 0 : 128 * n])

    def update(s, r):
        def rep(n, d=0):
            return wide[s, PAD + r + d : PAD + r + d + CHUNK, 128 * n : 128 * n + 128]

        def at(d):
            return side[s, PAD + r + d : PAD + r + d + CHUNK]

        m, v, x = rep(6), rep(2), at(0)
        me, mw, mn, ms = m * rep(3), m * rep(4), m * rep(5), m * rep(5, -1)
        base = 1.0 - ((me + mw) + (mn + ms))
        c = coefs(rep(0), rep(1), v + rep(2, 1), v + rep(2, -1), me, mw, mn, ms, base)
        return apply(c, x, roll(x, -1, 1), roll(x, 1, 1), at(1), at(-1))

    j1 = lanes((1, 128)) % 4

    def as_row(turned, columns, shift):
        parts = [roll(turned[c : c + 1], shift + d, 1) for c, d in zip(columns, (-2, -1, 0, 1))]
        low = jnp.where(j1 == 0, parts[0], parts[1])
        return jnp.where(j1 < 2, low, jnp.where(j1 == 2, parts[2], parts[3]))

    three = jnp.where(lane < 112, roll(own, -8, 1), jnp.where(lane < 120, west, roll(east, 8, 1)))
    turned = three.T
    above, below = as_row(turned, range(104, 108), 0), as_row(turned, range(108, 112), 1)
    fill(0, jnp.where(j < 2, west, own),
         jnp.where(j1 == 1, roll(turned[113:114], -1, 1), above),
         jnp.where(j1 == 1, turned[117:118], below))
    fill(1, jnp.where(j < 2, own, east),
         jnp.where(j1 == 2, turned[122:123], above),
         jnp.where(j1 == 2, roll(turned[126:127], 1, 1), below))
    widen(7)

    packs = (west, east)
    low = lat_strip(south, packs, 11, 9, None)
    high = lat_strip(north, packs, 15, 13, top)
    ring = rows_of((8, 128)) % 4 == 2
    for t in range(12):
        halo[8 * t : 8 * t + 8] = jnp.where(ring, high[t], low[t])
    halo[96:128] = jnp.zeros((32, 128), F32)
    turned = halo[...].T
    outer = (126, 127, 0, 1)
    above, below = as_row(turned, outer, 0), as_row(turned, outer, 1)

    new = [[update(s, r) for r in range(0, 128, CHUNK)] for s in range(2)]
    edge = (j == 0) | (j == 3)
    for s in range(2):
        strip = jnp.where(edge, roll(ends, 1 - 2 * s, 1), jnp.concatenate(new[s], axis=0))
        fill(s, strip, above, below)
    widen(3)
    jj = lanes((CHUNK, 128)) % 4
    for r in range(0, 128, CHUNK):
        z[r : r + CHUNK] = jnp.where(jj < 2, update(1, r), update(0, r))

    outs = []
    outer = (lanes((CHUNK, 128)) < 2) | (lanes((CHUNK, 128)) >= 126)
    for k in range(4):
        for r in range(0, 128, CHUNK):
            rr = slice(r, r + CHUNK)
            zr = z[rr]
            for f in range(6):
                x = jnp.where(early, inner_a[f, k, rr], inner_b[f, k, rr])
                res[f, k, rr] = jnp.where(outer, roll(zr, -(4 * (4 * f + k) + 2), 1), x)
        c = pltpu.make_async_copy(res.at[:, k], out_hbm.at[:, k], sem.at[k])
        c.start()
        outs.append(c)
    for c in outs:
        c.wait()


def cost(nbytes, flops):
    return pl.CostEstimate(flops=flops, bytes_accessed=nbytes, transcendentals=0)


def smem():
    return pl.BlockSpec(memory_space=pltpu.SMEM)


def vmem():
    return pl.BlockSpec(memory_space=pltpu.VMEM)


def local(nlon, nlat, fields, weights, area, mask, land):
    shape = jax.ShapeDtypeStruct
    planes = fields.reshape(NP, 128, 128)
    params = pltpu.CompilerParams(vmem_limit_bytes=24 << 20)

    rows = shape((ROWS2, 128), F32)
    to_odd, to_even = pl.pallas_call(
        rows_kernel,
        out_shape=(rows, rows),
        in_specs=[pl.BlockSpec(memory_space=pltpu.HBM)] * 4 + [smem()],
        out_specs=(vmem(),) * 2,
        scratch_shapes=[
            pltpu.VMEM((2, NP, 8, 128), F32),
            pltpu.VMEM((2, 2, 8, 128), F32),
            pltpu.VMEM((2, 8, 128), F32),
            pltpu.VMEM((2, 8, 128), jnp.int32),
            pltpu.SemaphoreType.DMA((8,)),
        ],
        compiler_params=params,
        cost_estimate=cost(1 << 18, 1 << 16),
        name="rows",
    )(*(pltpu.with_memory_space_constraint(x, pltpu.HBM) for x in (planes, weights, area, mask)), land)

    axes = ("lon", "lat")
    with jax.named_scope("lat_odd"):
        got_odd = lax.ppermute(to_odd, axes, lat_pairs(nlon, nlat, True))
    with jax.named_scope("lat_even"):
        got_even = lax.ppermute(to_even, axes, lat_pairs(nlon, nlat, False))

    tile, half = shape((128, 128), F32), shape((64, 128), F32)
    pack = pl.pallas_call(
        columns_kernel,
        out_shape=tile,
        in_specs=[vmem()] * 4 + [smem()],
        out_specs=vmem(),
        compiler_params=params,
        cost_estimate=cost(2 << 20, 1 << 20),
        name="columns",
    )(planes, weights, area, mask, land)

    pack, to_east, to_west, north, south = pl.pallas_call(
        strips_kernel,
        out_shape=(tile, half, half, shape((ROWS4, 128), F32), shape((ROWS4, 128), F32)),
        in_specs=[vmem()] * 5,
        out_specs=(vmem(),) * 5,
        scratch_shapes=[pltpu.VMEM((4, ROWS2, 128), F32)],
        compiler_params=params,
        cost_estimate=cost(1 << 18, 1 << 18),
        name="strips",
    )(to_odd, to_even, got_odd, got_even, pack)

    with jax.named_scope("lon_east"):
        got_west = lax.ppermute(to_east, axes, lon_pairs(nlon, nlat, 1))

    padded = 128 + 2 * PAD
    state = shape((6, 4, 128, 128), F32)
    inputs = (fields, weights, area, mask, land, north, south)

    def inner_call(early):
        return pl.pallas_call(
            functools.partial(inner_kernel, early),
            out_shape=(state, tile),
            in_specs=[vmem()] * 4 + [smem()] + [vmem()] * 2,
            out_specs=(vmem(), vmem()),
            scratch_shapes=[
                pltpu.VMEM((6, padded, 128), F32),
                pltpu.VMEM((2, 96, 128), F32),
                pltpu.VMEM((5, 128, 128), F32),
                pltpu.VMEM((6, 4, 128, 128), F32),
            ],
            compiler_params=params,
            cost_estimate=cost(4 << 20, 20 << 20),
            name="inner_early" if early else "inner_late",
        )(*inputs)

    inner_a, ends_a = inner_call(True)
    to_west, inner_a, ends_a = lax.optimization_barrier((to_west, inner_a, ends_a))
    with jax.named_scope("lon_west"):
        got_east = lax.ppermute(to_west, axes, lon_pairs(nlon, nlat, -1))
    inner_b, ends_b = inner_call(False)

    return pl.pallas_call(
        outer_kernel,
        out_shape=state,
        in_specs=[vmem()] * 10,
        out_specs=pl.BlockSpec(memory_space=pltpu.HBM),
        scratch_shapes=[
            pltpu.VMEM((2, padded, 128), F32),
            pltpu.VMEM((2, padded, 7 * 128), F32),
            pltpu.VMEM((128, 128), F32),
            pltpu.VMEM((128, 128), F32),
            pltpu.VMEM((6, 4, 128, 128), F32),
            pltpu.SemaphoreType.DMA((4,)),
        ],
        compiler_params=params,
        cost_estimate=cost(4 << 20, 1 << 20),
        name="outer",
    )(pack, got_west, got_east, north, south, inner_a, inner_b, ends_a, ends_b, jnp.asarray(spread_matrix(), jnp.bfloat16))


def solution(mesh):
    in_specs = (
        P(None, None, "lat", "lon"),
        P(None, "lat", "lon"),
        P("lat", "lon"),
        P("lat", "lon"),
        P("lat", "lon"),
    )
    body = functools.partial(local, mesh.shape["lon"], mesh.shape["lat"])
    return jax.shard_map(
        body, mesh=mesh, in_specs=in_specs, out_specs=P(None, None, "lat", "lon"), check_vma=False
    )
```

```python
import functools

import jax
import jax.numpy as jnp
import numpy as np
from jax import lax
from jax.experimental import pallas as pl
from jax.experimental.pallas import tpu as pltpu
from jax.sharding import PartitionSpec as P

F32 = jnp.float32
TIME_STEP = 0.1
NP = 24
GE, GN, GM, GS = 24, 25, 26, 27
ROWS2, ROWS4 = 56, 112
PAD = 8
CHUNK = 32
HIGH = lax.Precision.HIGHEST


def lon_pairs(nlon, nlat, step):
    return [(i * nlat + l, (i + step) % nlon * nlat + l) for i in range(nlon) for l in range(nlat)]


def lat_pairs(nlon, nlat, odd):
    pairs = []
    for i in range(nlon):
        for l in range(nlat):
            if not odd:
                pairs.append((i * nlat + l, i * nlat + (l ^ 1)))
            elif l == nlat - 1:
                pairs.append((i * nlat + l, (nlon - 1 - i) * nlat + l))
            elif l > 0:
                pairs.append((i * nlat + l, i * nlat + (l + 1 if l % 2 else l - 1)))
    return pairs


def lanes(shape):
    return lax.broadcasted_iota(jnp.int32, shape, 1)


def rows_of(shape):
    return lax.broadcasted_iota(jnp.int32, shape, 0)


def roll(x, shift, axis):
    n = x.shape[axis]
    shift %= n
    return x if shift == 0 else pltpu.roll(x, shift, axis)


def step_factor(area, mask, sea):
    return TIME_STEP * (mask.astype(F32) * sea) * area


def coefs(se, sw, sn, ss, me, mw, mn, ms, base):
    te, tw, tn, ts = me * (0.125 * se), mw * (0.125 * sw), mn * (0.125 * sn), ms * (0.125 * ss)
    return me - te, mw + tw, mn - tn, ms + ts, base + ((tw - te) + (ts - tn))


def apply(c, x, xe, xw, xn, xs):
    ce, cw, cn, cs, cc = c
    return cc * x + ((ce * xe + cw * xw) + (cn * xn + cs * xs))


def rows_kernel(f, w, area, mask, land, to_odd, to_even, fb, wb, ab, kb, sem):
    copies = []
    for n, (src, dst) in enumerate(((f, fb), (w, wb), (area, ab), (mask, kb))):
        for h in range(2):
            rows = pl.ds(120 * h, 8)
            part = src.at[:, rows] if len(src.shape) == 3 else src.at[rows]
            copies.append(pltpu.make_async_copy(part, dst.at[h], sem.at[2 * n + h]))
    for c in copies:
        c.start()
    odd = lax.axis_index("lat") % 2 == 1
    for c in copies:
        c.wait()
    is_sea = (1 - land[0, 0]).astype(F32)
    m_lo = step_factor(ab[0, 0:2], kb[0, 0:2], is_sea)
    m_hi = step_factor(ab[1, 6:8], kb[1, 6:8], is_sea)
    zero = jnp.zeros((2, 128), F32)
    for g in range(28):
        if g < NP:
            south, north = fb[0, g, 0:2], fb[1, g, 6:8]
        elif g < GM:
            south, north = wb[0, g - NP, 0:2], wb[1, g - NP, 6:8]
        elif g == GM:
            south, north = m_lo, m_hi
        else:
            south, north = zero, zero
        to_odd[2 * g : 2 * g + 2] = jnp.where(odd, north, south)
        to_even[2 * g : 2 * g + 2] = jnp.where(odd, south, north)


def columns_kernel(f, w, area, mask, land, out):
    sea = (1 - land[0, 0]).astype(F32)
    for r in range(0, 128, CHUNK):
        rr = slice(r, r + CHUNK)
        group = lanes((CHUNK, 128)) // 4
        acc = jnp.zeros((CHUNK, 128), F32)
        for g in range(28):
            if g < NP:
                x = f[g, rr]
            elif g < GM:
                x = w[g - NP, rr]
            elif g == GM:
                x = step_factor(area[rr], mask[rr], sea)
            else:
                x = w[0, rr]
            acc = jnp.where(group == g, roll(x, 4 * g + 2 + (g == GS), 1), acc)
        out[rr] = acc


def strips_kernel(to_odd, to_even, got_odd, got_even, pack, out, to_east, to_west, north, south, recv):
    odd = lax.axis_index("lat") % 2 == 1
    top = lax.axis_index("lat") == lax.axis_size("lat") - 1
    raw = jnp.where(odd, got_odd[...], got_even[...])
    row = rows_of((ROWS2, 128))
    flip = (rows_of((128, 128)) + lanes((128, 128)) == 127).astype(F32)
    mirrored = jnp.dot(raw, flip, precision=HIGH, preferred_element_type=F32)
    mirrored = jnp.where((row >= 32) & (row < 48), -mirrored, mirrored)
    mirrored = jnp.where(row % 2 == 0, roll(mirrored, -1, 0), roll(mirrored, 1, 0))
    recv[0] = jnp.where(top, mirrored, raw)
    recv[1] = jnp.where(odd, got_even[...], got_odd[...])
    recv[2] = jnp.where(odd, to_odd[...], to_even[...])
    recv[3] = jnp.where(odd, to_even[...], to_odd[...])
    for g in range(28):
        two = slice(2 * g, 2 * g + 2)
        north[4 * g : 4 * g + 2] = recv[2, two]
        north[4 * g + 2 : 4 * g + 4] = recv[0, two]
        south[4 * g : 4 * g + 2] = recv[1, two]
        south[4 * g + 2 : 4 * g + 4] = recv[3, two]
    a, b = recv[0, 2 * GN : 2 * GN + 1], recv[0, 2 * GN + 1 : 2 * GN + 2]
    north[4 * GN + 2 : 4 * GN + 3] = jnp.where(top, b, a)
    north[4 * GS + 2 : 4 * GS + 3] = jnp.where(top, a, recv[2, 2 * GN + 1 : 2 * GN + 2])
    south[4 * GS + 1 : 4 * GS + 2] = recv[1, 2 * GN : 2 * GN + 1]
    lane = lanes((ROWS4, 128))
    acc = jnp.where(lane // 4 == 28, roll(north[...], 114, 1), pack[0:ROWS4])
    out[0:ROWS4] = jnp.where(lane // 4 == 29, roll(south[...], 118, 1), acc)
    out[ROWS4:128] = pack[ROWS4:128]
    j = lanes((64, 128)) % 4
    a, b = out[0:64], out[64:128]
    to_east[...] = jnp.where(j < 2, a, roll(b, 2, 1))
    to_west[...] = jnp.where(j < 2, roll(b, -2, 1), a)


def repeat_half(v, half):
    low = rows_of(v.shape) < 4
    other = roll(v, 4, 0)
    return jnp.where(low, v, other) if half == 0 else jnp.where(low, other, v)


def lat_strip(strip, ends, shift_w, shift_e, top):
    lane = lanes((8, 128))
    if ends is not None:
        west = roll(ends[0][0:ROWS4], shift_w, 1)
        east = roll(ends[1][0:ROWS4], shift_e, 1)

    def tile(t):
        x = strip[8 * t : 8 * t + 8]
        xe, xw = roll(x, -1, 1), roll(x, 1, 1)
        if ends is not None:
            xe = jnp.where(lane == 127, east[8 * t : 8 * t + 8], xe)
            xw = jnp.where(lane == 0, west[8 * t : 8 * t + 8], xw)
        return x, xe, xw

    x12, e12, w12 = tile(12)
    x13 = strip[104:112]
    here, right, left = (repeat_half(a, 0) for a in (x12, e12, w12))
    we = here if top is None else jnp.where(top, right, here)
    ww = left if top is None else jnp.where(top, here, left)
    m = repeat_half(x13, 0)
    me, mw = m * we, m * ww
    mn, ms = m * repeat_half(x12, 1), m * repeat_half(x13, 1)
    base = 1.0 - ((me + mw) + (mn + ms))
    c = []
    for t in range(2):
        u, ue, uw = tile(8 + t)
        v = strip[8 * (10 + t) : 8 * (10 + t) + 8]
        c.append(coefs(u + ue, u + uw, v + roll(v, -1, 0), v + roll(v, 1, 0), me, mw, mn, ms, base))
    out = []
    for t in range(12):
        x, xe, xw = tile(t)
        out.append(apply(c[t % 2], x, xe, xw, roll(x, -1, 0), roll(x, 1, 0)))
    return out


def runs_early():
    first = lax.axis_index("lon") % (lax.axis_size("lon") // 2) == 0
    return first & (lax.axis_index("lat") < lax.axis_size("lat") - 2)


def inner_kernel(early, fields, w, area, mask, land, north, south, *refs):
    @pl.when(runs_early() if early else jnp.logical_not(runs_early()))
    def _():
        inner_steps(fields, w, area, mask, land, north, south, *refs)


def inner_steps(fields, w, area, mask, land, north, south, res, ends, mid, halo, mw5, beside):
    top = lax.axis_index("lat") == lax.axis_size("lat") - 1
    for s, tiles in enumerate(
        (lat_strip(south, None, 0, 0, None), lat_strip(north, None, 0, 0, top))
    ):
        for t in range(12):
            halo[s, 8 * t : 8 * t + 8] = tiles[t]

    m = step_factor(area[...], mask[...], (1 - land[0, 0]).astype(F32))
    we, wn = w[0], w[1]
    first = rows_of((128, 128)) == 0
    ws = jnp.where(first, south[4 * GN + 1 : 4 * GN + 2], roll(wn, 1, 0))
    me, mw, mn, ms = m * we, m * roll(we, 1, 1), m * wn, m * ws
    for n, x in enumerate((me, mw, mn, ms, 1.0 - ((me + mw) + (mn + ms)))):
        mw5[n] = x
    lane = lanes((CHUNK, 128))
    row = rows_of((CHUNK, 128))

    def level(k, _):
        def first_get(f, r):
            g = 4 * (4 * f + k)
            x = fields[f, k, r : r + CHUNK]
            if r == 0:
                s = jnp.where(row == 0, south[pl.ds(g + 1, 1)], roll(x, 1, 0))
            else:
                s = fields[f, k, r - 1 : r - 1 + CHUNK]
            if r == 128 - CHUNK:
                n = jnp.where(row == CHUNK - 1, north[pl.ds(g + 2, 1)], roll(x, -1, 0))
            else:
                n = fields[f, k, r + 1 : r + 1 + CHUNK]
            return x, n, s

        def second_get(f, r):
            return tuple(mid[f, PAD + r + d : PAD + r + d + CHUNK] for d in (0, 1, -1))

        for f in range(6):
            g = 4 * (4 * f + k)
            mid[f, PAD - 1 : PAD] = halo[0, pl.ds(g + 1, 1)]
            mid[f, PAD + 128 : PAD + 129] = halo[1, pl.ds(g + 2, 1)]
        for substep, get in enumerate((first_get, second_get)):
            for r in range(0, 128, CHUNK):
                rr = slice(r, r + CHUNK)
                u = get(4, r)[0]
                v, vn, vs = get(5, r)
                c = coefs(u + roll(u, -1, 1), u + roll(u, 1, 1), v + vn, v + vs,
                          *(mw5[n, rr] for n in range(5)))
                for f in range(6):
                    x, xn, xs = get(f, r)
                    xe, xw = roll(x, -1, 1), roll(x, 1, 1)
                    y = apply(c, x, xe, xw, xn, xs)
                    if substep == 0:
                        mid[f, PAD + r : PAD + r + CHUNK] = y
                    else:
                        res[f, k, rr] = y
                        beside[f, k, rr] = jnp.where(lane < 64, xe, xw)
        return 0

    lax.fori_loop(0, 4, level, 0)
    for r in range(0, 128, CHUNK):
        acc = jnp.zeros((CHUNK, 128), F32)
        for g in range(NP):
            x = roll(beside[g // 4, g % 4, r : r + CHUNK], 4 * g + 2, 1)
            acc = jnp.where(lane // 4 == g, x, acc)
        ends[r : r + CHUNK] = acc


def spread_matrix():
    out = np.zeros((7, 128, 128), np.float32)
    for l in range(128):
        k, j = l // 4 % 4, l % 4
        u, v = 64 + 4 * k + j, 80 + 4 * k + j
        for n, src in enumerate((
            (u, u + 1), (u, u - 1), (v,), (4 * GE + j,),
            (4 * GS if j == 0 else 4 * GE + j - 1,), (4 * GN + j,), (4 * GM + j,),
        )):
            for i in src:
                out[n, i, l] = 1.0
    return np.tile(np.concatenate(list(out), axis=1), (2, 1))


def spread(x, matrix):
    hi = x.astype(jnp.bfloat16)
    rest = x - hi.astype(F32)
    mid = rest.astype(jnp.bfloat16)
    lo = (rest - mid.astype(F32)).astype(jnp.bfloat16)
    dot = functools.partial(jnp.dot, preferred_element_type=F32)
    return dot(lo, matrix[0:128]) + dot(jnp.concatenate([hi, mid], axis=1), matrix)


def outer_kernel(pack, got_west, got_east, north, south, inner_a, inner_b, ends_a, ends_b, matrix, out_hbm,
                 side, wide, halo, z, res, sem):
    top = lax.axis_index("lat") == lax.axis_size("lat") - 1
    west, east = got_west[...], got_east[...]
    west = jnp.concatenate([west, roll(west, -2, 1)], axis=0)
    east = jnp.concatenate([east, roll(east, 2, 1)], axis=0)
    own = pack[...]
    early = runs_early()
    ends = jnp.where(early, ends_a[...], ends_b[...])
    lane = lanes((128, 128))
    j = lane % 4
    span = 128 + 2 * PAD

    def fill(s, strip, above, below):
        side[s, PAD : PAD + 128] = strip
        side[s, 0:PAD] = jnp.broadcast_to(below, (PAD, 128))
        side[s, PAD + 128 : span] = jnp.broadcast_to(above, (PAD, 128))

    def widen(n):
        for s in range(2):
            wide[s, :, 0 : 128 * n] = spread(side[s], matrix[:, 0 : 128 * n])

    def update(s, r):
        def rep(n, d=0):
            return wide[s, PAD + r + d : PAD + r + d + CHUNK, 128 * n : 128 * n + 128]

        def at(d):
            return side[s, PAD + r + d : PAD + r + d + CHUNK]

        m, v, x = rep(6), rep(2), at(0)
        me, mw, mn, ms = m * rep(3), m * rep(4), m * rep(5), m * rep(5, -1)
        base = 1.0 - ((me + mw) + (mn + ms))
        c = coefs(rep(0), rep(1), v + rep(2, 1), v + rep(2, -1), me, mw, mn, ms, base)
        return apply(c, x, roll(x, -1, 1), roll(x, 1, 1), at(1), at(-1))

    j1 = lanes((1, 128)) % 4

    def as_row(turned, columns, shift):
        parts = [roll(turned[c : c + 1], shift + d, 1) for c, d in zip(columns, (-2, -1, 0, 1))]
        low = jnp.where(j1 == 0, parts[0], parts[1])
        return jnp.where(j1 < 2, low, jnp.where(j1 == 2, parts[2], parts[3]))

    three = jnp.where(lane < 112, roll(own, -8, 1), jnp.where(lane < 120, west, roll(east, 8, 1)))
    turned = three.T
    above, below = as_row(turned, range(104, 108), 0), as_row(turned, range(108, 112), 1)
    fill(0, jnp.where(j < 2, west, own),
         jnp.where(j1 == 1, roll(turned[113:114], -1, 1), above),
         jnp.where(j1 == 1, turned[117:118], below))
    fill(1, jnp.where(j < 2, own, east),
         jnp.where(j1 == 2, turned[122:123], above),
         jnp.where(j1 == 2, roll(turned[126:127], 1, 1), below))
    widen(7)

    packs = (west, east)
    low = lat_strip(south, packs, 11, 9, None)
    high = lat_strip(north, packs, 15, 13, top)
    ring = rows_of((8, 128)) % 4 == 2
    for t in range(12):
        halo[8 * t : 8 * t + 8] = jnp.where(ring, high[t], low[t])
    halo[96:128] = jnp.zeros((32, 128), F32)
    turned = halo[...].T
    outer = (126, 127, 0, 1)
    above, below = as_row(turned, outer, 0), as_row(turned, outer, 1)

    new = [[update(s, r) for r in range(0, 128, CHUNK)] for s in range(2)]
    edge = (j == 0) | (j == 3)
    for s in range(2):
        strip = jnp.where(edge, roll(ends, 1 - 2 * s, 1), jnp.concatenate(new[s], axis=0))
        fill(s, strip, above, below)
    widen(3)
    jj = lanes((CHUNK, 128)) % 4
    for r in range(0, 128, CHUNK):
        z[r : r + CHUNK] = jnp.where(jj < 2, update(1, r), update(0, r))

    outs = []
    outer = (lanes((CHUNK, 128)) < 2) | (lanes((CHUNK, 128)) >= 126)
    for k in range(4):
        for r in range(0, 128, CHUNK):
            rr = slice(r, r + CHUNK)
            zr = z[rr]
            for f in range(6):
                x = jnp.where(early, inner_a[f, k, rr], inner_b[f, k, rr])
                res[f, k, rr] = jnp.where(outer, roll(zr, -(4 * (4 * f + k) + 2), 1), x)
        c = pltpu.make_async_copy(res.at[:, k], out_hbm.at[:, k], sem.at[k])
        c.start()
        outs.append(c)
    for c in outs:
        c.wait()


def cost(nbytes, flops):
    return pl.CostEstimate(flops=flops, bytes_accessed=nbytes, transcendentals=0)


def smem():
    return pl.BlockSpec(memory_space=pltpu.SMEM)


def vmem():
    return pl.BlockSpec(memory_space=pltpu.VMEM)


def local(nlon, nlat, fields, weights, area, mask, land):
    shape = jax.ShapeDtypeStruct
    planes = fields.reshape(NP, 128, 128)
    params = pltpu.CompilerParams(vmem_limit_bytes=24 << 20)

    rows = shape((ROWS2, 128), F32)
    to_odd, to_even = pl.pallas_call(
        rows_kernel,
        out_shape=(rows, rows),
        in_specs=[pl.BlockSpec(memory_space=pltpu.HBM)] * 4 + [smem()],
        out_specs=(vmem(),) * 2,
        scratch_shapes=[
            pltpu.VMEM((2, NP, 8, 128), F32),
            pltpu.VMEM((2, 2, 8, 128), F32),
            pltpu.VMEM((2, 8, 128), F32),
            pltpu.VMEM((2, 8, 128), jnp.int32),
            pltpu.SemaphoreType.DMA((8,)),
        ],
        compiler_params=params,
        cost_estimate=cost(1 << 18, 1 << 16),
        name="rows",
    )(*(pltpu.with_memory_space_constraint(x, pltpu.HBM) for x in (planes, weights, area, mask)), land)

    axes = ("lon", "lat")
    with jax.named_scope("lat_odd"):
        got_odd = lax.ppermute(to_odd, axes, lat_pairs(nlon, nlat, True))
    with jax.named_scope("lat_even"):
        got_even = lax.ppermute(to_even, axes, lat_pairs(nlon, nlat, False))

    tile, half = shape((128, 128), F32), shape((64, 128), F32)
    pack = pl.pallas_call(
        columns_kernel,
        out_shape=tile,
        in_specs=[vmem()] * 4 + [smem()],
        out_specs=vmem(),
        compiler_params=params,
        cost_estimate=cost(2 << 20, 1 << 20),
        name="columns",
    )(planes, weights, area, mask, land)

    pack, to_east, to_west, north, south = pl.pallas_call(
        strips_kernel,
        out_shape=(tile, half, half, shape((ROWS4, 128), F32), shape((ROWS4, 128), F32)),
        in_specs=[vmem()] * 5,
        out_specs=(vmem(),) * 5,
        scratch_shapes=[pltpu.VMEM((4, ROWS2, 128), F32)],
        compiler_params=params,
        cost_estimate=cost(1 << 18, 1 << 18),
        name="strips",
    )(to_odd, to_even, got_odd, got_even, pack)

    with jax.named_scope("lon_east"):
        got_west = lax.ppermute(to_east, axes, lon_pairs(nlon, nlat, 1))

    padded = 128 + 2 * PAD
    state = shape((6, 4, 128, 128), F32)
    inputs = (fields, weights, area, mask, land, north, south)

    def inner_call(early):
        return pl.pallas_call(
            functools.partial(inner_kernel, early),
            out_shape=(state, tile),
            in_specs=[vmem()] * 4 + [smem()] + [vmem()] * 2,
            out_specs=(vmem(), vmem()),
            scratch_shapes=[
                pltpu.VMEM((6, padded, 128), F32),
                pltpu.VMEM((2, 96, 128), F32),
                pltpu.VMEM((5, 128, 128), F32),
                pltpu.VMEM((6, 4, 128, 128), F32),
            ],
            compiler_params=params,
            cost_estimate=cost(4 << 20, 20 << 20),
            name="inner_early" if early else "inner_late",
        )(*inputs)

    inner_a, ends_a = inner_call(True)
    to_west, inner_a, ends_a = lax.optimization_barrier((to_west, inner_a, ends_a))
    with jax.named_scope("lon_west"):
        got_east = lax.ppermute(to_west, axes, lon_pairs(nlon, nlat, -1))
    inner_b, ends_b = inner_call(False)

    return pl.pallas_call(
        outer_kernel,
        out_shape=state,
        in_specs=[vmem()] * 10,
        out_specs=pl.BlockSpec(memory_space=pltpu.HBM),
        scratch_shapes=[
            pltpu.VMEM((2, padded, 128), F32),
            pltpu.VMEM((2, padded, 7 * 128), F32),
            pltpu.VMEM((128, 128), F32),
            pltpu.VMEM((128, 128), F32),
            pltpu.VMEM((6, 4, 128, 128), F32),
            pltpu.SemaphoreType.DMA((4,)),
        ],
        compiler_params=params,
        cost_estimate=cost(4 << 20, 1 << 20),
        name="outer",
    )(pack, got_west, got_east, north, south, inner_a, inner_b, ends_a, ends_b, jnp.asarray(spread_matrix(), jnp.bfloat16))


def solution(mesh):
    in_specs = (
        P(None, None, "lat", "lon"),
        P(None, "lat", "lon"),
        P("lat", "lon"),
        P("lat", "lon"),
        P("lat", "lon"),
    )
    body = functools.partial(local, mesh.shape["lon"], mesh.shape["lat"])
    return jax.shard_map(
        body, mesh=mesh, in_specs=in_specs, out_specs=P(None, None, "lat", "lon"), check_vma=False
    )
```

```python
import functools

import jax
import jax.numpy as jnp
import numpy as np
from jax import lax
from jax.experimental import pallas as pl
from jax.experimental.pallas import tpu as pltpu
from jax.sharding import PartitionSpec as P

F32 = jnp.float32
TIME_STEP = 0.1
NP = 24
GE, GN, GM, GS = 24, 25, 26, 27
ROWS2, ROWS4 = 56, 112
PAD = 8
CHUNK = 32
HIGH = lax.Precision.HIGHEST


def lon_pairs(nlon, nlat, step):
    return [(i * nlat + l, (i + step) % nlon * nlat + l) for i in range(nlon) for l in range(nlat)]


def lat_pairs(nlon, nlat, odd):
    pairs = []
    for i in range(nlon):
        for l in range(nlat):
            if not odd:
                pairs.append((i * nlat + l, i * nlat + (l ^ 1)))
            elif l == nlat - 1:
                pairs.append((i * nlat + l, (nlon - 1 - i) * nlat + l))
            elif l > 0:
                pairs.append((i * nlat + l, i * nlat + (l + 1 if l % 2 else l - 1)))
    return pairs


def lanes(shape):
    return lax.broadcasted_iota(jnp.int32, shape, 1)


def rows_of(shape):
    return lax.broadcasted_iota(jnp.int32, shape, 0)


def roll(x, shift, axis):
    n = x.shape[axis]
    shift %= n
    return x if shift == 0 else pltpu.roll(x, shift, axis)


def step_factor(area, mask, sea):
    return TIME_STEP * (mask.astype(F32) * sea) * area


def coefs(se, sw, sn, ss, me, mw, mn, ms, base):
    te, tw, tn, ts = me * (0.125 * se), mw * (0.125 * sw), mn * (0.125 * sn), ms * (0.125 * ss)
    return me - te, mw + tw, mn - tn, ms + ts, base + ((tw - te) + (ts - tn))


def apply(c, x, xe, xw, xn, xs):
    ce, cw, cn, cs, cc = c
    return cc * x + ((ce * xe + cw * xw) + (cn * xn + cs * xs))


def rows_kernel(f, w, area, mask, land, to_odd, to_even, fb, wb, ab, kb, sem):
    copies = []
    for n, (src, dst) in enumerate(((f, fb), (w, wb), (area, ab), (mask, kb))):
        for h in range(2):
            rows = pl.ds(120 * h, 8)
            part = src.at[:, rows] if len(src.shape) == 3 else src.at[rows]
            copies.append(pltpu.make_async_copy(part, dst.at[h], sem.at[2 * n + h]))
    for c in copies:
        c.start()
    odd = lax.axis_index("lat") % 2 == 1
    for c in copies:
        c.wait()
    is_sea = (1 - land[0, 0]).astype(F32)
    m_lo = step_factor(ab[0, 0:2], kb[0, 0:2], is_sea)
    m_hi = step_factor(ab[1, 6:8], kb[1, 6:8], is_sea)
    zero = jnp.zeros((2, 128), F32)
    for g in range(28):
        if g < NP:
            south, north = fb[0, g, 0:2], fb[1, g, 6:8]
        elif g < GM:
            south, north = wb[0, g - NP, 0:2], wb[1, g - NP, 6:8]
        elif g == GM:
            south, north = m_lo, m_hi
        else:
            south, north = zero, zero
        to_odd[2 * g : 2 * g + 2] = jnp.where(odd, north, south)
        to_even[2 * g : 2 * g + 2] = jnp.where(odd, south, north)


def columns_kernel(f, w, area, mask, land, out):
    sea = (1 - land[0, 0]).astype(F32)
    for r in range(0, 128, CHUNK):
        rr = slice(r, r + CHUNK)
        group = lanes((CHUNK, 128)) // 4
        acc = jnp.zeros((CHUNK, 128), F32)
        for g in range(28):
            if g < NP:
                x = f[g, rr]
            elif g < GM:
                x = w[g - NP, rr]
            elif g == GM:
                x = step_factor(area[rr], mask[rr], sea)
            else:
                x = w[0, rr]
            acc = jnp.where(group == g, roll(x, 4 * g + 2 + (g == GS), 1), acc)
        out[rr] = acc


def strips_kernel(to_odd, to_even, got_odd, got_even, pack, out, to_east, to_west, north, south, recv):
    odd = lax.axis_index("lat") % 2 == 1
    top = lax.axis_index("lat") == lax.axis_size("lat") - 1
    raw = jnp.where(odd, got_odd[...], got_even[...])
    row = rows_of((ROWS2, 128))
    flip = (rows_of((128, 128)) + lanes((128, 128)) == 127).astype(F32)
    mirrored = jnp.dot(raw, flip, precision=HIGH, preferred_element_type=F32)
    mirrored = jnp.where((row >= 32) & (row < 48), -mirrored, mirrored)
    mirrored = jnp.where(row % 2 == 0, roll(mirrored, -1, 0), roll(mirrored, 1, 0))
    recv[0] = jnp.where(top, mirrored, raw)
    recv[1] = jnp.where(odd, got_even[...], got_odd[...])
    recv[2] = jnp.where(odd, to_odd[...], to_even[...])
    recv[3] = jnp.where(odd, to_even[...], to_odd[...])
    for g in range(28):
        two = slice(2 * g, 2 * g + 2)
        north[4 * g : 4 * g + 2] = recv[2, two]
        north[4 * g + 2 : 4 * g + 4] = recv[0, two]
        south[4 * g : 4 * g + 2] = recv[1, two]
        south[4 * g + 2 : 4 * g + 4] = recv[3, two]
    a, b = recv[0, 2 * GN : 2 * GN + 1], recv[0, 2 * GN + 1 : 2 * GN + 2]
    north[4 * GN + 2 : 4 * GN + 3] = jnp.where(top, b, a)
    north[4 * GS + 2 : 4 * GS + 3] = jnp.where(top, a, recv[2, 2 * GN + 1 : 2 * GN + 2])
    south[4 * GS + 1 : 4 * GS + 2] = recv[1, 2 * GN : 2 * GN + 1]
    lane = lanes((ROWS4, 128))
    acc = jnp.where(lane // 4 == 28, roll(north[...], 114, 1), pack[0:ROWS4])
    out[0:ROWS4] = jnp.where(lane // 4 == 29, roll(south[...], 118, 1), acc)
    out[ROWS4:128] = pack[ROWS4:128]
    j = lanes((64, 128)) % 4
    a, b = out[0:64], out[64:128]
    to_east[...] = jnp.where(j < 2, a, roll(b, 2, 1))
    to_west[...] = jnp.where(j < 2, roll(b, -2, 1), a)


def repeat_half(v, half):
    low = rows_of(v.shape) < 4
    other = roll(v, 4, 0)
    return jnp.where(low, v, other) if half == 0 else jnp.where(low, other, v)


def lat_strip(strip, top, side=None, beside=None, shift=0):
    lane = lanes((8, 128))
    if beside is not None:
        beside = roll(beside[0:ROWS4], shift, 1)

    def tile(t):
        x = strip[8 * t : 8 * t + 8]
        xe, xw = roll(x, -1, 1), roll(x, 1, 1)
        if side == 0:
            xw = jnp.where(lane == 0, beside[8 * t : 8 * t + 8], xw)
        elif side == 1:
            xe = jnp.where(lane == 127, beside[8 * t : 8 * t + 8], xe)
        return x, xe, xw

    x12, e12, w12 = tile(12)
    x13 = strip[104:112]
    here, right, left = (repeat_half(a, 0) for a in (x12, e12, w12))
    we = here if top is None else jnp.where(top, right, here)
    ww = left if top is None else jnp.where(top, here, left)
    m = repeat_half(x13, 0)
    me, mw = m * we, m * ww
    mn, ms = m * repeat_half(x12, 1), m * repeat_half(x13, 1)
    base = 1.0 - ((me + mw) + (mn + ms))
    c = []
    for t in range(2):
        u, ue, uw = tile(8 + t)
        v = strip[8 * (10 + t) : 8 * (10 + t) + 8]
        c.append(coefs(u + ue, u + uw, v + roll(v, -1, 0), v + roll(v, 1, 0), me, mw, mn, ms, base))
    out = []
    for t in range(12):
        x, xe, xw = tile(t)
        out.append(apply(c[t % 2], x, xe, xw, roll(x, -1, 0), roll(x, 1, 0)))
    return out


def runs_early():
    first = lax.axis_index("lon") % (lax.axis_size("lon") // 2) == 0
    return first & (lax.axis_index("lat") < lax.axis_size("lat") - 2)


def inner_kernel(early, fields, w, area, mask, land, north, south, *refs):
    @pl.when(runs_early() if early else jnp.logical_not(runs_early()))
    def _():
        inner_steps(fields, w, area, mask, land, north, south, *refs)


def inner_steps(fields, w, area, mask, land, north, south, res, ends, mid, halo, mw5, beside):
    top = lax.axis_index("lat") == lax.axis_size("lat") - 1
    for s, tiles in enumerate(
        (lat_strip(south, None), lat_strip(north, top))
    ):
        for t in range(12):
            halo[s, 8 * t : 8 * t + 8] = tiles[t]

    m = step_factor(area[...], mask[...], (1 - land[0, 0]).astype(F32))
    we, wn = w[0], w[1]
    first = rows_of((128, 128)) == 0
    ws = jnp.where(first, south[4 * GN + 1 : 4 * GN + 2], roll(wn, 1, 0))
    me, mw, mn, ms = m * we, m * roll(we, 1, 1), m * wn, m * ws
    for n, x in enumerate((me, mw, mn, ms, 1.0 - ((me + mw) + (mn + ms)))):
        mw5[n] = x
    lane = lanes((CHUNK, 128))
    row = rows_of((CHUNK, 128))

    def level(k, _):
        def first_get(f, r):
            g = 4 * (4 * f + k)
            x = fields[f, k, r : r + CHUNK]
            if r == 0:
                s = jnp.where(row == 0, south[pl.ds(g + 1, 1)], roll(x, 1, 0))
            else:
                s = fields[f, k, r - 1 : r - 1 + CHUNK]
            if r == 128 - CHUNK:
                n = jnp.where(row == CHUNK - 1, north[pl.ds(g + 2, 1)], roll(x, -1, 0))
            else:
                n = fields[f, k, r + 1 : r + 1 + CHUNK]
            return x, n, s

        def second_get(f, r):
            return tuple(mid[f, PAD + r + d : PAD + r + d + CHUNK] for d in (0, 1, -1))

        for f in range(6):
            g = 4 * (4 * f + k)
            mid[f, PAD - 1 : PAD] = halo[0, pl.ds(g + 1, 1)]
            mid[f, PAD + 128 : PAD + 129] = halo[1, pl.ds(g + 2, 1)]
        for substep, get in enumerate((first_get, second_get)):
            for r in range(0, 128, CHUNK):
                rr = slice(r, r + CHUNK)
                u = get(4, r)[0]
                v, vn, vs = get(5, r)
                c = coefs(u + roll(u, -1, 1), u + roll(u, 1, 1), v + vn, v + vs,
                          *(mw5[n, rr] for n in range(5)))
                for f in range(6):
                    x, xn, xs = get(f, r)
                    xe, xw = roll(x, -1, 1), roll(x, 1, 1)
                    y = apply(c, x, xe, xw, xn, xs)
                    if substep == 0:
                        mid[f, PAD + r : PAD + r + CHUNK] = y
                    else:
                        res[f, k, rr] = y
                        beside[f, k, rr] = jnp.where(lane < 64, xe, xw)
        return 0

    lax.fori_loop(0, 4, level, 0)
    for r in range(0, 128, CHUNK):
        acc = jnp.zeros((CHUNK, 128), F32)
        for g in range(NP):
            x = roll(beside[g // 4, g % 4, r : r + CHUNK], 4 * g + 2, 1)
            acc = jnp.where(lane // 4 == g, x, acc)
        ends[r : r + CHUNK] = acc


def spread_matrix():
    out = np.zeros((7, 128, 128), np.float32)
    for l in range(128):
        k, j = l // 4 % 4, l % 4
        u, v = 64 + 4 * k + j, 80 + 4 * k + j
        for n, src in enumerate((
            (u, u + 1), (u, u - 1), (v,), (4 * GE + j,),
            (4 * GS if j == 0 else 4 * GE + j - 1,), (4 * GN + j,), (4 * GM + j,),
        )):
            for i in src:
                out[n, i, l] = 1.0
    return np.tile(np.concatenate(list(out), axis=1), (2, 1))


def spread(x, matrix):
    hi = x.astype(jnp.bfloat16)
    rest = x - hi.astype(F32)
    mid = rest.astype(jnp.bfloat16)
    lo = (rest - mid.astype(F32)).astype(jnp.bfloat16)
    dot = functools.partial(jnp.dot, preferred_element_type=F32)
    return dot(lo, matrix[0:128]) + dot(jnp.concatenate([hi, mid], axis=1), matrix)


def side_columns(s, pack, got, north, south, ends, matrix, side, wide, halo):
    top = lax.axis_index("lat") == lax.axis_size("lat") - 1
    beside, own = got[...], pack[...]
    beside = jnp.concatenate([beside, roll(beside, 2 if s else -2, 1)], axis=0)
    lane = lanes((128, 128))
    j, j1 = lane % 4, lanes((1, 128)) % 4

    def fill(strip, above, below):
        side[PAD : PAD + 128] = strip
        side[0:PAD] = jnp.broadcast_to(below, (PAD, 128))
        side[PAD + 128 : 128 + 2 * PAD] = jnp.broadcast_to(above, (PAD, 128))

    def widen(n):
        wide[:, 0 : 128 * n] = spread(side[...], matrix[:, 0 : 128 * n])

    def update(r):
        def rep(n, d=0):
            return wide[PAD + r + d : PAD + r + d + CHUNK, 128 * n : 128 * n + 128]

        def at(d):
            return side[PAD + r + d : PAD + r + d + CHUNK]

        m, v, x = rep(6), rep(2), at(0)
        me, mw, mn, ms = m * rep(3), m * rep(4), m * rep(5), m * rep(5, -1)
        base = 1.0 - ((me + mw) + (mn + ms))
        c = coefs(rep(0), rep(1), v + rep(2, 1), v + rep(2, -1), me, mw, mn, ms, base)
        return apply(c, x, roll(x, -1, 1), roll(x, 1, 1), at(1), at(-1))

    def as_row(turned, columns, shift):
        parts = [roll(turned[c : c + 1], shift + d, 1) for c, d in zip(columns, (-2, -1, 0, 1))]
        low = jnp.where(j1 == 0, parts[0], parts[1])
        return jnp.where(j1 < 2, low, jnp.where(j1 == 2, parts[2], parts[3]))

    turned = jnp.where(lane < 112, roll(own, -8, 1), beside).T
    above, below = as_row(turned, range(104, 108), 0), as_row(turned, range(108, 112), 1)
    if s == 0:
        above = jnp.where(j1 == 1, roll(turned[113:114], -1, 1), above)
        below = jnp.where(j1 == 1, turned[117:118], below)
        fill(jnp.where(j < 2, beside, own), above, below)
    else:
        above = jnp.where(j1 == 2, turned[114:115], above)
        below = jnp.where(j1 == 2, roll(turned[118:119], 1, 1), below)
        fill(jnp.where(j < 2, own, beside), above, below)
    widen(7)

    low = lat_strip(south, None, s, beside, (11, 9)[s])
    high = lat_strip(north, top, s, beside, (15, 13)[s])
    ring = rows_of((8, 128)) % 4 == 2
    for t in range(12):
        halo[8 * t : 8 * t + 8] = jnp.where(ring, high[t], low[t])
    halo[96:128] = jnp.zeros((32, 128), F32)
    turned = halo[...].T
    outer = (126, 127, 0, 1)
    above, below = as_row(turned, outer, 0), as_row(turned, outer, 1)

    new = jnp.concatenate([update(r) for r in range(0, 128, CHUNK)], axis=0)
    fill(jnp.where((j == 0) | (j == 3), roll(ends, 1 - 2 * s, 1), new), above, below)
    widen(3)
    return update


def west_kernel(pack, got_west, north, south, ends_a, ends_b, matrix, z, *scratch):
    ends = jnp.where(runs_early(), ends_a[...], ends_b[...])
    update = side_columns(0, pack, got_west, north, south, ends, matrix, *scratch)
    for r in range(0, 128, CHUNK):
        z[r : r + CHUNK] = update(r)


def last_kernel(pack, got_east, north, south, ends_a, ends_b, matrix, z_west, inner_a, inner_b, out_hbm,
                side, wide, halo, z, res, sem):
    early = runs_early()
    ends = jnp.where(early, ends_a[...], ends_b[...])
    update = side_columns(1, pack, got_east, north, south, ends, matrix, side, wide, halo)
    jj = lanes((CHUNK, 128)) % 4
    for r in range(0, 128, CHUNK):
        z[r : r + CHUNK] = jnp.where(jj < 2, update(r), z_west[r : r + CHUNK])

    outs = []
    outer = (lanes((CHUNK, 128)) < 2) | (lanes((CHUNK, 128)) >= 126)
    for k in range(4):
        for r in range(0, 128, CHUNK):
            rr = slice(r, r + CHUNK)
            zr = z[rr]
            for f in range(6):
                x = jnp.where(early, inner_a[f, k, rr], inner_b[f, k, rr])
                res[f, k, rr] = jnp.where(outer, roll(zr, -(4 * (4 * f + k) + 2), 1), x)
        c = pltpu.make_async_copy(res.at[:, k], out_hbm.at[:, k], sem.at[k])
        c.start()
        outs.append(c)
    for c in outs:
        c.wait()


def cost(nbytes, flops):
    return pl.CostEstimate(flops=flops, bytes_accessed=nbytes, transcendentals=0)


def smem():
    return pl.BlockSpec(memory_space=pltpu.SMEM)


def vmem():
    return pl.BlockSpec(memory_space=pltpu.VMEM)


def local(nlon, nlat, fields, weights, area, mask, land):
    shape = jax.ShapeDtypeStruct
    planes = fields.reshape(NP, 128, 128)
    params = pltpu.CompilerParams(vmem_limit_bytes=24 << 20)

    rows = shape((ROWS2, 128), F32)
    to_odd, to_even = pl.pallas_call(
        rows_kernel,
        out_shape=(rows, rows),
        in_specs=[pl.BlockSpec(memory_space=pltpu.HBM)] * 4 + [smem()],
        out_specs=(vmem(),) * 2,
        scratch_shapes=[
            pltpu.VMEM((2, NP, 8, 128), F32),
            pltpu.VMEM((2, 2, 8, 128), F32),
            pltpu.VMEM((2, 8, 128), F32),
            pltpu.VMEM((2, 8, 128), jnp.int32),
            pltpu.SemaphoreType.DMA((8,)),
        ],
        compiler_params=params,
        cost_estimate=cost(1 << 18, 1 << 16),
        name="rows",
    )(*(pltpu.with_memory_space_constraint(x, pltpu.HBM) for x in (planes, weights, area, mask)), land)

    axes = ("lon", "lat")
    with jax.named_scope("lat_odd"):
        got_odd = lax.ppermute(to_odd, axes, lat_pairs(nlon, nlat, True))
    with jax.named_scope("lat_even"):
        got_even = lax.ppermute(to_even, axes, lat_pairs(nlon, nlat, False))

    tile, half = shape((128, 128), F32), shape((64, 128), F32)
    pack = pl.pallas_call(
        columns_kernel,
        out_shape=tile,
        in_specs=[vmem()] * 4 + [smem()],
        out_specs=vmem(),
        compiler_params=params,
        cost_estimate=cost(2 << 20, 1 << 20),
        name="columns",
    )(planes, weights, area, mask, land)

    pack, to_east, to_west, north, south = pl.pallas_call(
        strips_kernel,
        out_shape=(tile, half, half, shape((ROWS4, 128), F32), shape((ROWS4, 128), F32)),
        in_specs=[vmem()] * 5,
        out_specs=(vmem(),) * 5,
        scratch_shapes=[pltpu.VMEM((4, ROWS2, 128), F32)],
        compiler_params=params,
        cost_estimate=cost(1 << 18, 1 << 18),
        name="strips",
    )(to_odd, to_even, got_odd, got_even, pack)

    with jax.named_scope("lon_east"):
        got_west = lax.ppermute(to_east, axes, lon_pairs(nlon, nlat, 1))

    padded = 128 + 2 * PAD
    state = shape((6, 4, 128, 128), F32)
    inputs = (fields, weights, area, mask, land, north, south)

    def inner_call(early):
        return pl.pallas_call(
            functools.partial(inner_kernel, early),
            out_shape=(state, tile),
            in_specs=[vmem()] * 4 + [smem()] + [vmem()] * 2,
            out_specs=(vmem(), vmem()),
            scratch_shapes=[
                pltpu.VMEM((6, padded, 128), F32),
                pltpu.VMEM((2, 96, 128), F32),
                pltpu.VMEM((5, 128, 128), F32),
                pltpu.VMEM((6, 4, 128, 128), F32),
            ],
            compiler_params=params,
            cost_estimate=cost(4 << 20, 20 << 20),
            name="inner_early" if early else "inner_late",
        )(*inputs)

    inner_a, ends_a = inner_call(True)
    to_west, inner_a, ends_a = lax.optimization_barrier((to_west, inner_a, ends_a))
    with jax.named_scope("lon_west"):
        got_east = lax.ppermute(to_west, axes, lon_pairs(nlon, nlat, -1))
    inner_b, ends_b = inner_call(False)

    matrix = jnp.asarray(spread_matrix(), jnp.bfloat16)
    strip_scratch = [
        pltpu.VMEM((padded, 128), F32),
        pltpu.VMEM((padded, 7 * 128), F32),
        pltpu.VMEM((128, 128), F32),
    ]
    z_west = pl.pallas_call(
        west_kernel,
        out_shape=tile,
        in_specs=[vmem()] * 7,
        out_specs=vmem(),
        scratch_shapes=strip_scratch,
        compiler_params=params,
        cost_estimate=cost(2 << 20, 10 << 20),
        name="west",
    )(pack, got_west, north, south, ends_a, ends_b, matrix)

    return pl.pallas_call(
        last_kernel,
        out_shape=state,
        in_specs=[vmem()] * 10,
        out_specs=pl.BlockSpec(memory_space=pltpu.HBM),
        scratch_shapes=strip_scratch
        + [
            pltpu.VMEM((128, 128), F32),
            pltpu.VMEM((6, 4, 128, 128), F32),
            pltpu.SemaphoreType.DMA((4,)),
        ],
        compiler_params=params,
        cost_estimate=cost(4 << 20, 1 << 20),
        name="last",
    )(pack, got_east, north, south, ends_a, ends_b, matrix, z_west, inner_a, inner_b)


def solution(mesh):
    in_specs = (
        P(None, None, "lat", "lon"),
        P(None, "lat", "lon"),
        P("lat", "lon"),
        P("lat", "lon"),
        P("lat", "lon"),
    )
    body = functools.partial(local, mesh.shape["lon"], mesh.shape["lat"])
    return jax.shard_map(
        body, mesh=mesh, in_specs=in_specs, out_specs=P(None, None, "lat", "lon"), check_vma=False
    )
```

```python
import functools

import jax
import jax.numpy as jnp
import numpy as np
from jax import lax
from jax.experimental import pallas as pl
from jax.experimental.pallas import tpu as pltpu
from jax.sharding import PartitionSpec as P

F32 = jnp.float32
TIME_STEP = 0.1
NP = 24
GE, GN, GM, GS = 24, 25, 26, 27
ROWS2, ROWS4 = 56, 112
PAD = 8
CHUNK = 32
HIGH = lax.Precision.HIGHEST


def lon_pairs(nlon, nlat, step):
    return [(i * nlat + l, (i + step) % nlon * nlat + l) for i in range(nlon) for l in range(nlat)]


def lat_pairs(nlon, nlat, odd):
    pairs = []
    for i in range(nlon):
        for l in range(nlat):
            if not odd:
                pairs.append((i * nlat + l, i * nlat + (l ^ 1)))
            elif l == nlat - 1:
                pairs.append((i * nlat + l, (nlon - 1 - i) * nlat + l))
            elif l > 0:
                pairs.append((i * nlat + l, i * nlat + (l + 1 if l % 2 else l - 1)))
    return pairs


def lanes(shape):
    return lax.broadcasted_iota(jnp.int32, shape, 1)


def rows_of(shape):
    return lax.broadcasted_iota(jnp.int32, shape, 0)


def roll(x, shift, axis):
    n = x.shape[axis]
    shift %= n
    return x if shift == 0 else pltpu.roll(x, shift, axis)


def step_factor(area, mask, sea):
    return TIME_STEP * (mask.astype(F32) * sea) * area


def coefs(se, sw, sn, ss, me, mw, mn, ms, base):
    te, tw, tn, ts = me * (0.125 * se), mw * (0.125 * sw), mn * (0.125 * sn), ms * (0.125 * ss)
    return me - te, mw + tw, mn - tn, ms + ts, base + ((tw - te) + (ts - tn))


def apply(c, x, xe, xw, xn, xs):
    ce, cw, cn, cs, cc = c
    return cc * x + ((ce * xe + cw * xw) + (cn * xn + cs * xs))


def rows_kernel(f, w, area, mask, land, to_odd, to_even, fb, wb, ab, kb, sem):
    copies = []
    for n, (src, dst) in enumerate(((f, fb), (w, wb), (area, ab), (mask, kb))):
        for h in range(2):
            rows = pl.ds(120 * h, 8)
            part = src.at[:, rows] if len(src.shape) == 3 else src.at[rows]
            copies.append(pltpu.make_async_copy(part, dst.at[h], sem.at[2 * n + h]))
    for c in copies:
        c.start()
    odd = lax.axis_index("lat") % 2 == 1
    for c in copies:
        c.wait()
    is_sea = (1 - land[0, 0]).astype(F32)
    m_lo = step_factor(ab[0, 0:2], kb[0, 0:2], is_sea)
    m_hi = step_factor(ab[1, 6:8], kb[1, 6:8], is_sea)
    zero = jnp.zeros((2, 128), F32)
    for g in range(28):
        if g < NP:
            south, north = fb[0, g, 0:2], fb[1, g, 6:8]
        elif g < GM:
            south, north = wb[0, g - NP, 0:2], wb[1, g - NP, 6:8]
        elif g == GM:
            south, north = m_lo, m_hi
        else:
            south, north = zero, zero
        to_odd[2 * g : 2 * g + 2] = jnp.where(odd, north, south)
        to_even[2 * g : 2 * g + 2] = jnp.where(odd, south, north)


def columns_kernel(f, w, area, mask, land, out):
    sea = (1 - land[0, 0]).astype(F32)
    for r in range(0, 128, CHUNK):
        rr = slice(r, r + CHUNK)
        group = lanes((CHUNK, 128)) // 4
        acc = jnp.zeros((CHUNK, 128), F32)
        for g in range(28):
            if g < NP:
                x = f[g, rr]
            elif g < GM:
                x = w[g - NP, rr]
            elif g == GM:
                x = step_factor(area[rr], mask[rr], sea)
            else:
                x = w[0, rr]
            acc = jnp.where(group == g, roll(x, 4 * g + 2 + (g == GS), 1), acc)
        out[rr] = acc


def strips_kernel(to_odd, to_even, got_odd, got_even, pack, out, to_east, to_west, north, south, recv):
    odd = lax.axis_index("lat") % 2 == 1
    top = lax.axis_index("lat") == lax.axis_size("lat") - 1
    raw = jnp.where(odd, got_odd[...], got_even[...])
    row = rows_of((ROWS2, 128))
    flip = (rows_of((128, 128)) + lanes((128, 128)) == 127).astype(F32)
    mirrored = jnp.dot(raw, flip, precision=HIGH, preferred_element_type=F32)
    mirrored = jnp.where((row >= 32) & (row < 48), -mirrored, mirrored)
    mirrored = jnp.where(row % 2 == 0, roll(mirrored, -1, 0), roll(mirrored, 1, 0))
    recv[0] = jnp.where(top, mirrored, raw)
    recv[1] = jnp.where(odd, got_even[...], got_odd[...])
    recv[2] = jnp.where(odd, to_odd[...], to_even[...])
    recv[3] = jnp.where(odd, to_even[...], to_odd[...])
    for g in range(28):
        two = slice(2 * g, 2 * g + 2)
        north[4 * g : 4 * g + 2] = recv[2, two]
        north[4 * g + 2 : 4 * g + 4] = recv[0, two]
        south[4 * g : 4 * g + 2] = recv[1, two]
        south[4 * g + 2 : 4 * g + 4] = recv[3, two]
    a, b = recv[0, 2 * GN : 2 * GN + 1], recv[0, 2 * GN + 1 : 2 * GN + 2]
    north[4 * GN + 2 : 4 * GN + 3] = jnp.where(top, b, a)
    north[4 * GS + 2 : 4 * GS + 3] = jnp.where(top, a, recv[2, 2 * GN + 1 : 2 * GN + 2])
    south[4 * GS + 1 : 4 * GS + 2] = recv[1, 2 * GN : 2 * GN + 1]
    lane = lanes((ROWS4, 128))
    acc = jnp.where(lane // 4 == 28, roll(north[...], 114, 1), pack[0:ROWS4])
    out[0:ROWS4] = jnp.where(lane // 4 == 29, roll(south[...], 118, 1), acc)
    out[ROWS4:128] = pack[ROWS4:128]
    j = lanes((64, 128)) % 4
    a, b = out[0:64], out[64:128]
    to_east[...] = jnp.where(j < 2, a, roll(b, 2, 1))
    to_west[...] = jnp.where(j < 2, roll(b, -2, 1), a)


def repeat_half(v, half):
    low = rows_of(v.shape) < 4
    other = roll(v, 4, 0)
    return jnp.where(low, v, other) if half == 0 else jnp.where(low, other, v)


def lat_strip(strip, top, side=None, beside=None, shift=0):
    lane = lanes((8, 128))
    if beside is not None:
        beside = roll(beside[0:ROWS4], shift, 1)

    def tile(t):
        x = strip[8 * t : 8 * t + 8]
        xe, xw = roll(x, -1, 1), roll(x, 1, 1)
        if side == 0:
            xw = jnp.where(lane == 0, beside[8 * t : 8 * t + 8], xw)
        elif side == 1:
            xe = jnp.where(lane == 127, beside[8 * t : 8 * t + 8], xe)
        return x, xe, xw

    x12, e12, w12 = tile(12)
    x13 = strip[104:112]
    here, right, left = (repeat_half(a, 0) for a in (x12, e12, w12))
    we = here if top is None else jnp.where(top, right, here)
    ww = left if top is None else jnp.where(top, here, left)
    m = repeat_half(x13, 0)
    me, mw = m * we, m * ww
    mn, ms = m * repeat_half(x12, 1), m * repeat_half(x13, 1)
    base = 1.0 - ((me + mw) + (mn + ms))
    c = []
    for t in range(2):
        u, ue, uw = tile(8 + t)
        v = strip[8 * (10 + t) : 8 * (10 + t) + 8]
        c.append(coefs(u + ue, u + uw, v + roll(v, -1, 0), v + roll(v, 1, 0), me, mw, mn, ms, base))
    out = []
    for t in range(12):
        x, xe, xw = tile(t)
        out.append(apply(c[t % 2], x, xe, xw, roll(x, -1, 0), roll(x, 1, 0)))
    return out


def runs_early():
    first = lax.axis_index("lon") % (lax.axis_size("lon") // 2) == 0
    return first & (lax.axis_index("lat") < lax.axis_size("lat") - 2)


def inner_kernel(early, fields, w, area, mask, land, north, south, *refs):
    @pl.when(runs_early() if early else jnp.logical_not(runs_early()))
    def _():
        inner_steps(fields, w, area, mask, land, north, south, *refs)


def inner_steps(fields, w, area, mask, land, north, south, res, ends, mid, halo, mw5, beside):
    top = lax.axis_index("lat") == lax.axis_size("lat") - 1
    for s, tiles in enumerate(
        (lat_strip(south, None), lat_strip(north, top))
    ):
        for t in range(12):
            halo[s, 8 * t : 8 * t + 8] = tiles[t]

    m = step_factor(area[...], mask[...], (1 - land[0, 0]).astype(F32))
    we, wn = w[0], w[1]
    first = rows_of((128, 128)) == 0
    ws = jnp.where(first, south[4 * GN + 1 : 4 * GN + 2], roll(wn, 1, 0))
    me, mw, mn, ms = m * we, m * roll(we, 1, 1), m * wn, m * ws
    for n, x in enumerate((me, mw, mn, ms, 1.0 - ((me + mw) + (mn + ms)))):
        mw5[n] = x
    lane = lanes((CHUNK, 128))
    row = rows_of((CHUNK, 128))

    def level(k, _):
        def first_get(f, r):
            g = 4 * (4 * f + k)
            x = fields[f, k, r : r + CHUNK]
            if r == 0:
                s = jnp.where(row == 0, south[pl.ds(g + 1, 1)], roll(x, 1, 0))
            else:
                s = fields[f, k, r - 1 : r - 1 + CHUNK]
            if r == 128 - CHUNK:
                n = jnp.where(row == CHUNK - 1, north[pl.ds(g + 2, 1)], roll(x, -1, 0))
            else:
                n = fields[f, k, r + 1 : r + 1 + CHUNK]
            return x, n, s

        def second_get(f, r):
            return tuple(mid[f, PAD + r + d : PAD + r + d + CHUNK] for d in (0, 1, -1))

        for f in range(6):
            g = 4 * (4 * f + k)
            mid[f, PAD - 1 : PAD] = halo[0, pl.ds(g + 1, 1)]
            mid[f, PAD + 128 : PAD + 129] = halo[1, pl.ds(g + 2, 1)]
        for substep, get in enumerate((first_get, second_get)):
            for r in range(0, 128, CHUNK):
                rr = slice(r, r + CHUNK)
                u = get(4, r)[0]
                v, vn, vs = get(5, r)
                c = coefs(u + roll(u, -1, 1), u + roll(u, 1, 1), v + vn, v + vs,
                          *(mw5[n, rr] for n in range(5)))
                for f in range(6):
                    x, xn, xs = get(f, r)
                    xe, xw = roll(x, -1, 1), roll(x, 1, 1)
                    y = apply(c, x, xe, xw, xn, xs)
                    if substep == 0:
                        mid[f, PAD + r : PAD + r + CHUNK] = y
                    else:
                        res[f, k, rr] = y
                        beside[f, k, rr] = jnp.where(lane < 64, xe, xw)
        return 0

    lax.fori_loop(0, 4, level, 0)
    for r in range(0, 128, CHUNK):
        acc = jnp.zeros((CHUNK, 128), F32)
        for g in range(NP):
            x = roll(beside[g // 4, g % 4, r : r + CHUNK], 4 * g + 2, 1)
            acc = jnp.where(lane // 4 == g, x, acc)
        ends[r : r + CHUNK] = acc


def spread_matrix():
    out = np.zeros((7, 128, 128), np.float32)
    for l in range(128):
        k, j = l // 4 % 4, l % 4
        u, v = 64 + 4 * k + j, 80 + 4 * k + j
        for n, src in enumerate((
            (u, u + 1), (u, u - 1), (v,), (4 * GE + j,),
            (4 * GS if j == 0 else 4 * GE + j - 1,), (4 * GN + j,), (4 * GM + j,),
        )):
            for i in src:
                out[n, i, l] = 1.0
    return np.tile(np.concatenate(list(out), axis=1), (2, 1))


def spread(x, matrix):
    hi = x.astype(jnp.bfloat16)
    rest = x - hi.astype(F32)
    mid = rest.astype(jnp.bfloat16)
    lo = (rest - mid.astype(F32)).astype(jnp.bfloat16)
    dot = functools.partial(jnp.dot, preferred_element_type=F32)
    return dot(lo, matrix[0:128]) + dot(jnp.concatenate([hi, mid], axis=1), matrix)


def side_columns(s, pack, got, north, south, ends, matrix, side, wide, halo):
    top = lax.axis_index("lat") == lax.axis_size("lat") - 1
    beside, own = got[...], pack[...]
    beside = jnp.concatenate([beside, roll(beside, 2 if s else -2, 1)], axis=0)
    lane = lanes((128, 128))
    j, j1 = lane % 4, lanes((1, 128)) % 4

    def fill(strip, above, below):
        side[PAD : PAD + 128] = strip
        side[0:PAD] = jnp.broadcast_to(below, (PAD, 128))
        side[PAD + 128 : 128 + 2 * PAD] = jnp.broadcast_to(above, (PAD, 128))

    def widen(n):
        wide[:, 0 : 128 * n] = spread(side[...], matrix[:, 0 : 128 * n])

    def update(r):
        def rep(n, d=0):
            return wide[PAD + r + d : PAD + r + d + CHUNK, 128 * n : 128 * n + 128]

        def at(d):
            return side[PAD + r + d : PAD + r + d + CHUNK]

        m, v, x = rep(6), rep(2), at(0)
        me, mw, mn, ms = m * rep(3), m * rep(4), m * rep(5), m * rep(5, -1)
        base = 1.0 - ((me + mw) + (mn + ms))
        c = coefs(rep(0), rep(1), v + rep(2, 1), v + rep(2, -1), me, mw, mn, ms, base)
        return apply(c, x, roll(x, -1, 1), roll(x, 1, 1), at(1), at(-1))

    def as_row(turned, columns, shift):
        parts = [roll(turned[c : c + 1], shift + d, 1) for c, d in zip(columns, (-2, -1, 0, 1))]
        low = jnp.where(j1 == 0, parts[0], parts[1])
        return jnp.where(j1 < 2, low, jnp.where(j1 == 2, parts[2], parts[3]))

    turned = jnp.where(lane < 112, roll(own, -8, 1), beside).T
    above, below = as_row(turned, range(104, 108), 0), as_row(turned, range(108, 112), 1)
    if s == 0:
        above = jnp.where(j1 == 1, roll(turned[113:114], -1, 1), above)
        below = jnp.where(j1 == 1, turned[117:118], below)
        fill(jnp.where(j < 2, beside, own), above, below)
    else:
        above = jnp.where(j1 == 2, turned[114:115], above)
        below = jnp.where(j1 == 2, roll(turned[118:119], 1, 1), below)
        fill(jnp.where(j < 2, own, beside), above, below)
    widen(7)

    low = lat_strip(south, None, s, beside, (11, 9)[s])
    high = lat_strip(north, top, s, beside, (15, 13)[s])
    ring = rows_of((8, 128)) % 4 == 2
    for t in range(12):
        halo[8 * t : 8 * t + 8] = jnp.where(ring, high[t], low[t])
    halo[96:128] = jnp.zeros((32, 128), F32)
    turned = halo[...].T
    outer = (126, 127, 0, 1)
    above, below = as_row(turned, outer, 0), as_row(turned, outer, 1)

    new = jnp.concatenate([update(r) for r in range(0, 128, CHUNK)], axis=0)
    fill(jnp.where((j == 0) | (j == 3), roll(ends, 1 - 2 * s, 1), new), above, below)
    widen(3)
    return update


def east_kernel(pack, got_east, north, south, ends_a, ends_b, matrix, z, *scratch):
    ends = jnp.where(runs_early(), ends_a[...], ends_b[...])
    update = side_columns(1, pack, got_east, north, south, ends, matrix, *scratch)
    for r in range(0, 128, CHUNK):
        z[r : r + CHUNK] = update(r)


def last_kernel(pack, got_west, north, south, ends_a, ends_b, matrix, z_east, inner_a, inner_b, out_hbm,
                side, wide, halo, z, res, sem):
    early = runs_early()
    ends = jnp.where(early, ends_a[...], ends_b[...])
    update = side_columns(0, pack, got_west, north, south, ends, matrix, side, wide, halo)
    jj = lanes((CHUNK, 128)) % 4
    for r in range(0, 128, CHUNK):
        z[r : r + CHUNK] = jnp.where(jj < 2, z_east[r : r + CHUNK], update(r))

    outs = []
    outer = (lanes((CHUNK, 128)) < 2) | (lanes((CHUNK, 128)) >= 126)
    for k in range(4):
        for r in range(0, 128, CHUNK):
            rr = slice(r, r + CHUNK)
            zr = z[rr]
            for f in range(6):
                x = jnp.where(early, inner_a[f, k, rr], inner_b[f, k, rr])
                res[f, k, rr] = jnp.where(outer, roll(zr, -(4 * (4 * f + k) + 2), 1), x)
        c = pltpu.make_async_copy(res.at[:, k], out_hbm.at[:, k], sem.at[k])
        c.start()
        outs.append(c)
    for c in outs:
        c.wait()


def cost(nbytes, flops):
    return pl.CostEstimate(flops=flops, bytes_accessed=nbytes, transcendentals=0)


def smem():
    return pl.BlockSpec(memory_space=pltpu.SMEM)


def vmem():
    return pl.BlockSpec(memory_space=pltpu.VMEM)


def local(nlon, nlat, fields, weights, area, mask, land):
    shape = jax.ShapeDtypeStruct
    planes = fields.reshape(NP, 128, 128)
    params = pltpu.CompilerParams(vmem_limit_bytes=24 << 20)

    rows = shape((ROWS2, 128), F32)
    to_odd, to_even = pl.pallas_call(
        rows_kernel,
        out_shape=(rows, rows),
        in_specs=[pl.BlockSpec(memory_space=pltpu.HBM)] * 4 + [smem()],
        out_specs=(vmem(),) * 2,
        scratch_shapes=[
            pltpu.VMEM((2, NP, 8, 128), F32),
            pltpu.VMEM((2, 2, 8, 128), F32),
            pltpu.VMEM((2, 8, 128), F32),
            pltpu.VMEM((2, 8, 128), jnp.int32),
            pltpu.SemaphoreType.DMA((8,)),
        ],
        compiler_params=params,
        cost_estimate=cost(1 << 18, 1 << 16),
        name="rows",
    )(*(pltpu.with_memory_space_constraint(x, pltpu.HBM) for x in (planes, weights, area, mask)), land)

    axes = ("lon", "lat")
    with jax.named_scope("lat_odd"):
        got_odd = lax.ppermute(to_odd, axes, lat_pairs(nlon, nlat, True))
    with jax.named_scope("lat_even"):
        got_even = lax.ppermute(to_even, axes, lat_pairs(nlon, nlat, False))

    tile, half = shape((128, 128), F32), shape((64, 128), F32)
    pack = pl.pallas_call(
        columns_kernel,
        out_shape=tile,
        in_specs=[vmem()] * 4 + [smem()],
        out_specs=vmem(),
        compiler_params=params,
        cost_estimate=cost(2 << 20, 1 << 20),
        name="columns",
    )(planes, weights, area, mask, land)

    pack, to_east, to_west, north, south = pl.pallas_call(
        strips_kernel,
        out_shape=(tile, half, half, shape((ROWS4, 128), F32), shape((ROWS4, 128), F32)),
        in_specs=[vmem()] * 5,
        out_specs=(vmem(),) * 5,
        scratch_shapes=[pltpu.VMEM((4, ROWS2, 128), F32)],
        compiler_params=params,
        cost_estimate=cost(1 << 18, 1 << 18),
        name="strips",
    )(to_odd, to_even, got_odd, got_even, pack)

    padded = 128 + 2 * PAD
    state = shape((6, 4, 128, 128), F32)
    inputs = (fields, weights, area, mask, land, north, south)

    def inner_call(early):
        return pl.pallas_call(
            functools.partial(inner_kernel, early),
            out_shape=(state, tile),
            in_specs=[vmem()] * 4 + [smem()] + [vmem()] * 2,
            out_specs=(vmem(), vmem()),
            scratch_shapes=[
                pltpu.VMEM((6, padded, 128), F32),
                pltpu.VMEM((2, 96, 128), F32),
                pltpu.VMEM((5, 128, 128), F32),
                pltpu.VMEM((6, 4, 128, 128), F32),
            ],
            compiler_params=params,
            cost_estimate=cost(4 << 20, 20 << 20),
            name="inner_early" if early else "inner_late",
        )(*inputs)

    inner_a, ends_a = inner_call(True)
    to_west, to_east, inner_a, ends_a = lax.optimization_barrier((to_west, to_east, inner_a, ends_a))
    with jax.named_scope("lon_west"):
        got_east = lax.ppermute(to_west, axes, lon_pairs(nlon, nlat, -1))
    with jax.named_scope("lon_east"):
        got_west = lax.ppermute(to_east, axes, lon_pairs(nlon, nlat, 1))
    inner_b, ends_b = inner_call(False)

    matrix = jnp.asarray(spread_matrix(), jnp.bfloat16)
    strip_scratch = [
        pltpu.VMEM((padded, 128), F32),
        pltpu.VMEM((padded, 7 * 128), F32),
        pltpu.VMEM((128, 128), F32),
    ]
    z_east = pl.pallas_call(
        east_kernel,
        out_shape=tile,
        in_specs=[vmem()] * 7,
        out_specs=vmem(),
        scratch_shapes=strip_scratch,
        compiler_params=params,
        cost_estimate=cost(2 << 20, 10 << 20),
        name="east",
    )(pack, got_east, north, south, ends_a, ends_b, matrix)

    return pl.pallas_call(
        last_kernel,
        out_shape=state,
        in_specs=[vmem()] * 10,
        out_specs=pl.BlockSpec(memory_space=pltpu.HBM),
        scratch_shapes=strip_scratch
        + [
            pltpu.VMEM((128, 128), F32),
            pltpu.VMEM((6, 4, 128, 128), F32),
            pltpu.SemaphoreType.DMA((4,)),
        ],
        compiler_params=params,
        cost_estimate=cost(4 << 20, 1 << 20),
        name="last",
    )(pack, got_west, north, south, ends_a, ends_b, matrix, z_east, inner_a, inner_b)


def solution(mesh):
    in_specs = (
        P(None, None, "lat", "lon"),
        P(None, "lat", "lon"),
        P("lat", "lon"),
        P("lat", "lon"),
        P("lat", "lon"),
    )
    body = functools.partial(local, mesh.shape["lon"], mesh.shape["lat"])
    return jax.shard_map(
        body, mesh=mesh, in_specs=in_specs, out_specs=P(None, None, "lat", "lon"), check_vma=False
    )
```

```python
import functools

import jax
import jax.numpy as jnp
import numpy as np
from jax import lax
from jax.experimental import pallas as pl
from jax.experimental.pallas import tpu as pltpu
from jax.sharding import PartitionSpec as P

F32 = jnp.float32
TIME_STEP = 0.1
NP = 24
GE, GN, GM, GS = 24, 25, 26, 27
ROWS2, ROWS4 = 56, 112
PAD = 8
CHUNK = 32
HIGH = lax.Precision.HIGHEST


def lon_pairs(nlon, nlat, step):
    return [(i * nlat + l, (i + step) % nlon * nlat + l) for i in range(nlon) for l in range(nlat)]


def lat_pairs(nlon, nlat, odd):
    pairs = []
    for i in range(nlon):
        for l in range(nlat):
            if not odd:
                pairs.append((i * nlat + l, i * nlat + (l ^ 1)))
            elif l == nlat - 1:
                pairs.append((i * nlat + l, (nlon - 1 - i) * nlat + l))
            elif l > 0:
                pairs.append((i * nlat + l, i * nlat + (l + 1 if l % 2 else l - 1)))
    return pairs


def lanes(shape):
    return lax.broadcasted_iota(jnp.int32, shape, 1)


def rows_of(shape):
    return lax.broadcasted_iota(jnp.int32, shape, 0)


def roll(x, shift, axis):
    n = x.shape[axis]
    shift %= n
    return x if shift == 0 else pltpu.roll(x, shift, axis)


def step_factor(area, mask, sea):
    return TIME_STEP * (mask.astype(F32) * sea) * area


def coefs(se, sw, sn, ss, me, mw, mn, ms, base):
    te, tw, tn, ts = me * (0.125 * se), mw * (0.125 * sw), mn * (0.125 * sn), ms * (0.125 * ss)
    return me - te, mw + tw, mn - tn, ms + ts, base + ((tw - te) + (ts - tn))


def apply(c, x, xe, xw, xn, xs):
    ce, cw, cn, cs, cc = c
    return cc * x + ((ce * xe + cw * xw) + (cn * xn + cs * xs))


def rows_kernel(f, w, area, mask, land, to_odd, to_even, fb, wb, ab, kb, sem):
    copies = []
    for n, (src, dst) in enumerate(((f, fb), (w, wb), (area, ab), (mask, kb))):
        for h in range(2):
            rows = pl.ds(120 * h, 8)
            part = src.at[:, rows] if len(src.shape) == 3 else src.at[rows]
            copies.append(pltpu.make_async_copy(part, dst.at[h], sem.at[2 * n + h]))
    for c in copies:
        c.start()
    odd = lax.axis_index("lat") % 2 == 1
    for c in copies:
        c.wait()
    is_sea = (1 - land[0, 0]).astype(F32)
    m_lo = step_factor(ab[0, 0:2], kb[0, 0:2], is_sea)
    m_hi = step_factor(ab[1, 6:8], kb[1, 6:8], is_sea)
    zero = jnp.zeros((2, 128), F32)
    for g in range(28):
        if g < NP:
            south, north = fb[0, g, 0:2], fb[1, g, 6:8]
        elif g < GM:
            south, north = wb[0, g - NP, 0:2], wb[1, g - NP, 6:8]
        elif g == GM:
            south, north = m_lo, m_hi
        else:
            south, north = zero, zero
        to_odd[2 * g : 2 * g + 2] = jnp.where(odd, north, south)
        to_even[2 * g : 2 * g + 2] = jnp.where(odd, south, north)


def columns_kernel(f, w, area, mask, land, out):
    sea = (1 - land[0, 0]).astype(F32)
    for r in range(0, 128, CHUNK):
        rr = slice(r, r + CHUNK)
        group = lanes((CHUNK, 128)) // 4
        acc = jnp.zeros((CHUNK, 128), F32)
        for g in range(28):
            if g < NP:
                x = f[g, rr]
            elif g < GM:
                x = w[g - NP, rr]
            elif g == GM:
                x = step_factor(area[rr], mask[rr], sea)
            else:
                x = w[0, rr]
            acc = jnp.where(group == g, roll(x, 4 * g + 2 + (g == GS), 1), acc)
        out[rr] = acc


def strips_kernel(to_odd, to_even, got_odd, got_even, pack, out, to_east, to_west, north, south, recv):
    odd = lax.axis_index("lat") % 2 == 1
    top = lax.axis_index("lat") == lax.axis_size("lat") - 1
    raw = jnp.where(odd, got_odd[...], got_even[...])
    row = rows_of((ROWS2, 128))
    flip = (rows_of((128, 128)) + lanes((128, 128)) == 127).astype(F32)
    mirrored = jnp.dot(raw, flip, precision=HIGH, preferred_element_type=F32)
    mirrored = jnp.where((row >= 32) & (row < 48), -mirrored, mirrored)
    mirrored = jnp.where(row % 2 == 0, roll(mirrored, -1, 0), roll(mirrored, 1, 0))
    recv[0] = jnp.where(top, mirrored, raw)
    recv[1] = jnp.where(odd, got_even[...], got_odd[...])
    recv[2] = jnp.where(odd, to_odd[...], to_even[...])
    recv[3] = jnp.where(odd, to_even[...], to_odd[...])
    for g in range(28):
        two = slice(2 * g, 2 * g + 2)
        north[4 * g : 4 * g + 2] = recv[2, two]
        north[4 * g + 2 : 4 * g + 4] = recv[0, two]
        south[4 * g : 4 * g + 2] = recv[1, two]
        south[4 * g + 2 : 4 * g + 4] = recv[3, two]
    a, b = recv[0, 2 * GN : 2 * GN + 1], recv[0, 2 * GN + 1 : 2 * GN + 2]
    north[4 * GN + 2 : 4 * GN + 3] = jnp.where(top, b, a)
    north[4 * GS + 2 : 4 * GS + 3] = jnp.where(top, a, recv[2, 2 * GN + 1 : 2 * GN + 2])
    south[4 * GS + 1 : 4 * GS + 2] = recv[1, 2 * GN : 2 * GN + 1]
    lane = lanes((ROWS4, 128))
    acc = jnp.where(lane // 4 == 28, roll(north[...], 114, 1), pack[0:ROWS4])
    out[0:ROWS4] = jnp.where(lane // 4 == 29, roll(south[...], 118, 1), acc)
    out[ROWS4:128] = pack[ROWS4:128]
    j = lanes((64, 128)) % 4
    a, b = out[0:64], out[64:128]
    to_east[...] = jnp.where(j < 2, a, roll(b, 2, 1))
    to_west[...] = jnp.where(j < 2, roll(b, -2, 1), a)


def repeat_half(v, half):
    low = rows_of(v.shape) < 4
    other = roll(v, 4, 0)
    return jnp.where(low, v, other) if half == 0 else jnp.where(low, other, v)


def lat_strip(strip, top, side=None, beside=None, shift=0):
    lane = lanes((8, 128))
    if beside is not None:
        beside = roll(beside[0:ROWS4], shift, 1)

    def tile(t):
        x = strip[8 * t : 8 * t + 8]
        xe, xw = roll(x, -1, 1), roll(x, 1, 1)
        if side == 0:
            xw = jnp.where(lane == 0, beside[8 * t : 8 * t + 8], xw)
        elif side == 1:
            xe = jnp.where(lane == 127, beside[8 * t : 8 * t + 8], xe)
        return x, xe, xw

    x12, e12, w12 = tile(12)
    x13 = strip[104:112]
    here, right, left = (repeat_half(a, 0) for a in (x12, e12, w12))
    we = here if top is None else jnp.where(top, right, here)
    ww = left if top is None else jnp.where(top, here, left)
    m = repeat_half(x13, 0)
    me, mw = m * we, m * ww
    mn, ms = m * repeat_half(x12, 1), m * repeat_half(x13, 1)
    base = 1.0 - ((me + mw) + (mn + ms))
    c = []
    for t in range(2):
        u, ue, uw = tile(8 + t)
        v = strip[8 * (10 + t) : 8 * (10 + t) + 8]
        c.append(coefs(u + ue, u + uw, v + roll(v, -1, 0), v + roll(v, 1, 0), me, mw, mn, ms, base))
    out = []
    for t in range(12):
        x, xe, xw = tile(t)
        out.append(apply(c[t % 2], x, xe, xw, roll(x, -1, 0), roll(x, 1, 0)))
    return out


def runs_early():
    return lax.axis_index("lon") % (lax.axis_size("lon") // 2) == 0


def inner_kernel(early, fields, w, area, mask, land, north, south, *refs):
    @pl.when(runs_early() if early else jnp.logical_not(runs_early()))
    def _():
        inner_steps(fields, w, area, mask, land, north, south, *refs)


def inner_steps(fields, w, area, mask, land, north, south, res, ends, mid, halo, mw5, beside):
    top = lax.axis_index("lat") == lax.axis_size("lat") - 1
    for s, tiles in enumerate(
        (lat_strip(south, None), lat_strip(north, top))
    ):
        for t in range(12):
            halo[s, 8 * t : 8 * t + 8] = tiles[t]

    m = step_factor(area[...], mask[...], (1 - land[0, 0]).astype(F32))
    we, wn = w[0], w[1]
    first = rows_of((128, 128)) == 0
    ws = jnp.where(first, south[4 * GN + 1 : 4 * GN + 2], roll(wn, 1, 0))
    me, mw, mn, ms = m * we, m * roll(we, 1, 1), m * wn, m * ws
    for n, x in enumerate((me, mw, mn, ms, 1.0 - ((me + mw) + (mn + ms)))):
        mw5[n] = x
    lane = lanes((CHUNK, 128))
    row = rows_of((CHUNK, 128))

    def level(k, _):
        def first_get(f, r):
            g = 4 * (4 * f + k)
            x = fields[f, k, r : r + CHUNK]
            if r == 0:
                s = jnp.where(row == 0, south[pl.ds(g + 1, 1)], roll(x, 1, 0))
            else:
                s = fields[f, k, r - 1 : r - 1 + CHUNK]
            if r == 128 - CHUNK:
                n = jnp.where(row == CHUNK - 1, north[pl.ds(g + 2, 1)], roll(x, -1, 0))
            else:
                n = fields[f, k, r + 1 : r + 1 + CHUNK]
            return x, n, s

        def second_get(f, r):
            return tuple(mid[f, PAD + r + d : PAD + r + d + CHUNK] for d in (0, 1, -1))

        for f in range(6):
            g = 4 * (4 * f + k)
            mid[f, PAD - 1 : PAD] = halo[0, pl.ds(g + 1, 1)]
            mid[f, PAD + 128 : PAD + 129] = halo[1, pl.ds(g + 2, 1)]
        for substep, get in enumerate((first_get, second_get)):
            for r in range(0, 128, CHUNK):
                rr = slice(r, r + CHUNK)
                u = get(4, r)[0]
                v, vn, vs = get(5, r)
                c = coefs(u + roll(u, -1, 1), u + roll(u, 1, 1), v + vn, v + vs,
                          *(mw5[n, rr] for n in range(5)))
                for f in range(6):
                    x, xn, xs = get(f, r)
                    xe, xw = roll(x, -1, 1), roll(x, 1, 1)
                    y = apply(c, x, xe, xw, xn, xs)
                    if substep == 0:
                        mid[f, PAD + r : PAD + r + CHUNK] = y
                    else:
                        res[f, k, rr] = y
                        beside[f, k, rr] = jnp.where(lane < 64, xe, xw)
        return 0

    lax.fori_loop(0, 4, level, 0)
    for r in range(0, 128, CHUNK):
        acc = jnp.zeros((CHUNK, 128), F32)
        for g in range(NP):
            x = roll(beside[g // 4, g % 4, r : r + CHUNK], 4 * g + 2, 1)
            acc = jnp.where(lane // 4 == g, x, acc)
        ends[r : r + CHUNK] = acc


def spread_matrix():
    out = np.zeros((7, 128, 128), np.float32)
    for l in range(128):
        k, j = l // 4 % 4, l % 4
        u, v = 64 + 4 * k + j, 80 + 4 * k + j
        for n, src in enumerate((
            (u, u + 1), (u, u - 1), (v,), (4 * GE + j,),
            (4 * GS if j == 0 else 4 * GE + j - 1,), (4 * GN + j,), (4 * GM + j,),
        )):
            for i in src:
                out[n, i, l] = 1.0
    return np.tile(np.concatenate(list(out), axis=1), (2, 1))


def spread(x, matrix):
    hi = x.astype(jnp.bfloat16)
    rest = x - hi.astype(F32)
    mid = rest.astype(jnp.bfloat16)
    lo = (rest - mid.astype(F32)).astype(jnp.bfloat16)
    dot = functools.partial(jnp.dot, preferred_element_type=F32)
    return dot(lo, matrix[0:128]) + dot(jnp.concatenate([hi, mid], axis=1), matrix)


def side_columns(s, pack, got, north, south, ends, matrix, side, wide, halo):
    top = lax.axis_index("lat") == lax.axis_size("lat") - 1
    beside, own = got[...], pack[...]
    beside = jnp.concatenate([beside, roll(beside, 2 if s else -2, 1)], axis=0)
    lane = lanes((128, 128))
    j, j1 = lane % 4, lanes((1, 128)) % 4

    def fill(strip, above, below):
        side[PAD : PAD + 128] = strip
        side[0:PAD] = jnp.broadcast_to(below, (PAD, 128))
        side[PAD + 128 : 128 + 2 * PAD] = jnp.broadcast_to(above, (PAD, 128))

    def widen(n):
        wide[:, 0 : 128 * n] = spread(side[...], matrix[:, 0 : 128 * n])

    def update(r):
        def rep(n, d=0):
            return wide[PAD + r + d : PAD + r + d + CHUNK, 128 * n : 128 * n + 128]

        def at(d):
            return side[PAD + r + d : PAD + r + d + CHUNK]

        m, v, x = rep(6), rep(2), at(0)
        me, mw, mn, ms = m * rep(3), m * rep(4), m * rep(5), m * rep(5, -1)
        base = 1.0 - ((me + mw) + (mn + ms))
        c = coefs(rep(0), rep(1), v + rep(2, 1), v + rep(2, -1), me, mw, mn, ms, base)
        return apply(c, x, roll(x, -1, 1), roll(x, 1, 1), at(1), at(-1))

    def as_row(turned, columns, shift):
        parts = [roll(turned[c : c + 1], shift + d, 1) for c, d in zip(columns, (-2, -1, 0, 1))]
        low = jnp.where(j1 == 0, parts[0], parts[1])
        return jnp.where(j1 < 2, low, jnp.where(j1 == 2, parts[2], parts[3]))

    turned = jnp.where(lane < 112, roll(own, -8, 1), beside).T
    above, below = as_row(turned, range(104, 108), 0), as_row(turned, range(108, 112), 1)
    if s == 0:
        above = jnp.where(j1 == 1, roll(turned[113:114], -1, 1), above)
        below = jnp.where(j1 == 1, turned[117:118], below)
        fill(jnp.where(j < 2, beside, own), above, below)
    else:
        above = jnp.where(j1 == 2, turned[114:115], above)
        below = jnp.where(j1 == 2, roll(turned[118:119], 1, 1), below)
        fill(jnp.where(j < 2, own, beside), above, below)
    widen(7)

    low = lat_strip(south, None, s, beside, (11, 9)[s])
    high = lat_strip(north, top, s, beside, (15, 13)[s])
    ring = rows_of((8, 128)) % 4 == 2
    for t in range(12):
        halo[8 * t : 8 * t + 8] = jnp.where(ring, high[t], low[t])
    halo[96:128] = jnp.zeros((32, 128), F32)
    turned = halo[...].T
    outer = (126, 127, 0, 1)
    above, below = as_row(turned, outer, 0), as_row(turned, outer, 1)

    new = jnp.concatenate([update(r) for r in range(0, 128, CHUNK)], axis=0)
    fill(jnp.where((j == 0) | (j == 3), roll(ends, 1 - 2 * s, 1), new), above, below)
    widen(3)
    return update


def west_kernel(pack, got_west, north, south, ends_a, ends_b, matrix, z, *scratch):
    ends = jnp.where(runs_early(), ends_a[...], ends_b[...])
    update = side_columns(0, pack, got_west, north, south, ends, matrix, *scratch)
    for r in range(0, 128, CHUNK):
        z[r : r + CHUNK] = update(r)


def last_kernel(pack, got_east, north, south, ends_a, ends_b, matrix, z_west, inner_a, inner_b, out_hbm,
                side, wide, halo, z, res, sem):
    early = runs_early()
    ends = jnp.where(early, ends_a[...], ends_b[...])
    update = side_columns(1, pack, got_east, north, south, ends, matrix, side, wide, halo)
    jj = lanes((CHUNK, 128)) % 4
    for r in range(0, 128, CHUNK):
        z[r : r + CHUNK] = jnp.where(jj < 2, update(r), z_west[r : r + CHUNK])

    outs = []
    outer = (lanes((CHUNK, 128)) < 2) | (lanes((CHUNK, 128)) >= 126)
    for k in range(4):
        for r in range(0, 128, CHUNK):
            rr = slice(r, r + CHUNK)
            zr = z[rr]
            for f in range(6):
                x = jnp.where(early, inner_a[f, k, rr], inner_b[f, k, rr])
                res[f, k, rr] = jnp.where(outer, roll(zr, -(4 * (4 * f + k) + 2), 1), x)
        c = pltpu.make_async_copy(res.at[:, k], out_hbm.at[:, k], sem.at[k])
        c.start()
        outs.append(c)
    for c in outs:
        c.wait()


def cost(nbytes, flops):
    return pl.CostEstimate(flops=flops, bytes_accessed=nbytes, transcendentals=0)


def smem():
    return pl.BlockSpec(memory_space=pltpu.SMEM)


def vmem():
    return pl.BlockSpec(memory_space=pltpu.VMEM)


def local(nlon, nlat, fields, weights, area, mask, land):
    shape = jax.ShapeDtypeStruct
    planes = fields.reshape(NP, 128, 128)
    params = pltpu.CompilerParams(vmem_limit_bytes=24 << 20)

    rows = shape((ROWS2, 128), F32)
    to_odd, to_even = pl.pallas_call(
        rows_kernel,
        out_shape=(rows, rows),
        in_specs=[pl.BlockSpec(memory_space=pltpu.HBM)] * 4 + [smem()],
        out_specs=(vmem(),) * 2,
        scratch_shapes=[
            pltpu.VMEM((2, NP, 8, 128), F32),
            pltpu.VMEM((2, 2, 8, 128), F32),
            pltpu.VMEM((2, 8, 128), F32),
            pltpu.VMEM((2, 8, 128), jnp.int32),
            pltpu.SemaphoreType.DMA((8,)),
        ],
        compiler_params=params,
        cost_estimate=cost(1 << 18, 1 << 16),
        name="rows",
    )(*(pltpu.with_memory_space_constraint(x, pltpu.HBM) for x in (planes, weights, area, mask)), land)

    axes = ("lon", "lat")
    with jax.named_scope("lat_odd"):
        got_odd = lax.ppermute(to_odd, axes, lat_pairs(nlon, nlat, True))
    with jax.named_scope("lat_even"):
        got_even = lax.ppermute(to_even, axes, lat_pairs(nlon, nlat, False))

    tile, half = shape((128, 128), F32), shape((64, 128), F32)
    pack = pl.pallas_call(
        columns_kernel,
        out_shape=tile,
        in_specs=[vmem()] * 4 + [smem()],
        out_specs=vmem(),
        compiler_params=params,
        cost_estimate=cost(2 << 20, 1 << 20),
        name="columns",
    )(planes, weights, area, mask, land)

    pack, to_east, to_west, north, south = pl.pallas_call(
        strips_kernel,
        out_shape=(tile, half, half, shape((ROWS4, 128), F32), shape((ROWS4, 128), F32)),
        in_specs=[vmem()] * 5,
        out_specs=(vmem(),) * 5,
        scratch_shapes=[pltpu.VMEM((4, ROWS2, 128), F32)],
        compiler_params=params,
        cost_estimate=cost(1 << 18, 1 << 18),
        name="strips",
    )(to_odd, to_even, got_odd, got_even, pack)

    padded = 128 + 2 * PAD
    state = shape((6, 4, 128, 128), F32)
    inputs = (fields, weights, area, mask, land, north, south)

    def inner_call(early):
        return pl.pallas_call(
            functools.partial(inner_kernel, early),
            out_shape=(state, tile),
            in_specs=[vmem()] * 4 + [smem()] + [vmem()] * 2,
            out_specs=(vmem(), vmem()),
            scratch_shapes=[
                pltpu.VMEM((6, padded, 128), F32),
                pltpu.VMEM((2, 96, 128), F32),
                pltpu.VMEM((5, 128, 128), F32),
                pltpu.VMEM((6, 4, 128, 128), F32),
            ],
            compiler_params=params,
            cost_estimate=cost(4 << 20, 20 << 20),
            name="inner_early" if early else "inner_late",
        )(*inputs)

    inner_a, ends_a = inner_call(True)
    to_west, to_east, inner_a, ends_a = lax.optimization_barrier((to_west, to_east, inner_a, ends_a))
    with jax.named_scope("lon_east"):
        got_west = lax.ppermute(to_east, axes, lon_pairs(nlon, nlat, 1))
    with jax.named_scope("lon_west"):
        got_east = lax.ppermute(to_west, axes, lon_pairs(nlon, nlat, -1))
    inner_b, ends_b = inner_call(False)

    matrix = jnp.asarray(spread_matrix(), jnp.bfloat16)
    strip_scratch = [
        pltpu.VMEM((padded, 128), F32),
        pltpu.VMEM((padded, 7 * 128), F32),
        pltpu.VMEM((128, 128), F32),
    ]
    z_west = pl.pallas_call(
        west_kernel,
        out_shape=tile,
        in_specs=[vmem()] * 7,
        out_specs=vmem(),
        scratch_shapes=strip_scratch,
        compiler_params=params,
        cost_estimate=cost(2 << 20, 10 << 20),
        name="west",
    )(pack, got_west, north, south, ends_a, ends_b, matrix)

    return pl.pallas_call(
        last_kernel,
        out_shape=state,
        in_specs=[vmem()] * 10,
        out_specs=pl.BlockSpec(memory_space=pltpu.HBM),
        scratch_shapes=strip_scratch
        + [
            pltpu.VMEM((128, 128), F32),
            pltpu.VMEM((6, 4, 128, 128), F32),
            pltpu.SemaphoreType.DMA((4,)),
        ],
        compiler_params=params,
        cost_estimate=cost(4 << 20, 1 << 20),
        name="last",
    )(pack, got_east, north, south, ends_a, ends_b, matrix, z_west, inner_a, inner_b)


def solution(mesh):
    in_specs = (
        P(None, None, "lat", "lon"),
        P(None, "lat", "lon"),
        P("lat", "lon"),
        P("lat", "lon"),
        P("lat", "lon"),
    )
    body = functools.partial(local, mesh.shape["lon"], mesh.shape["lat"])
    return jax.shard_map(
        body, mesh=mesh, in_specs=in_specs, out_specs=P(None, None, "lat", "lon"), check_vma=False
    )
```
